128 devices in a mesh: group: 8 (over y, x_hi), strip: 16 (over x_lo, z, core).
Axes of the slice: x: 4 (x_hi: 2, x_lo: 2; x = x_hi * 2 + x_lo), y: 4, z: 4, core: 2. Of those that a mesh axis runs over, the one named last changes fastest.
Arguments:
- initial: float32 [8, 512, 1024], P('group', 'strip'), may hold values from -6 to 6
- conductivity: float32 [8, 512, 1024], P('group', 'strip'), may hold values from 0.5 to 1.5
- step_count: int32 [8], P('group'), may hold values from 16 to 32, as said below
- emit_steps: int32 [8, 16], P('group'), may hold values from 1 to 32
- assign: int32 [512], replicated, may hold values from 0 to 127
- sample_inputs: bfloat16 [512, 128], P(('group', 'strip')), may hold values from -6 to 6
- w_first: bfloat16 [128, 512], replicated, may hold values from -0.5 to 0.5
- w_second: bfloat16 [512, 512], replicated, may hold values from -0.25 to 0.25
- w_third: bfloat16 [512, 512], replicated, may hold values from -0.25 to 0.25
- w_out: bfloat16 [512, 512, 1024], P(None, 'strip', 'group'), may hold values from -0.25 to 0.25
Outputs:
- grad_first: float32 [128, 512], replicated
- grad_second: float32 [512, 512], replicated
- grad_third: float32 [512, 512], replicated
- grad_out: bfloat16 [512, 512, 1024], P(None, 'strip', 'group')
The draws below stay inside these ranges and needn't reach their ends.
Inputs may be any that keep to these rules, and one draw needn't show every extreme that they name: `step_count`: at least 16; some field runs all 32 steps.
All inputs are finite; a program needn't handle non-finite values.
Results may differ from the reference program's by a relative error of at most 0.0039.
The reference program's roundings to bfloat16 on the way count: a program that leaves them out, or rounds other values in their place, can miss the bound.
Values may be sent and summed in bfloat16 or wider, within the bound.
A program may use at most 64 MiB of HBM per device.

```python
import math
import jax
import jax.numpy as jnp
from jax import lax

ROWS_DEV = 32
NY = 1024
STEPS = 32
SNAPS = 16
HIDDEN_SIZE = 512
FEATURES = 128
FIELDS = 8
NX = 512
BATCH = 512


def draw_step_count(key, part):
    key_counts = jax.random.fold_in(key, 11)
    key_full = jax.random.fold_in(key, 12)
    counts = jax.random.randint(key_counts, (FIELDS,), STEPS // 2, STEPS + 1)
    full_field = jax.random.randint(key_full, (), 0, FIELDS)
    return jnp.where(jnp.arange(FIELDS) == full_field, STEPS, counts).astype(jnp.int32)


def draw_emit_steps(key, part):
    key_steps = jax.random.fold_in(key, 21)
    key_place = jax.random.fold_in(key, 22)
    emitted = jax.random.randint(key_steps, (FIELDS, SNAPS), 1, STEPS + 1)
    last_place = jax.random.randint(key_place, (FIELDS, 1), 0, SNAPS)
    first_place = (last_place + 1) % SNAPS
    columns = jnp.arange(SNAPS)[None, :]
    emitted = jnp.where(columns == last_place, STEPS, emitted)
    emitted = jnp.where(columns == first_place, 1, emitted)
    return emitted.astype(jnp.int32)


def place_ends(array, rng, smallest, high):
    longest = array.shape.index(max(array.shape))
    spots = []
    for shift in (0, 1):
        where = [jax.random.randint(jax.random.fold_in(rng, axis), (), 0, length) for axis, length in enumerate(array.shape)]
        where[longest] = (where[longest] + shift) % array.shape[longest]
        spots.append(tuple(where))
    return array.at[spots[0]].set(smallest).at[spots[1]].set(high)


def block_levels(stream_key, extent, shards, low, high):
    factor_of = 1.0
    for position, blocks in shards:
        steps = jax.random.uniform(jax.random.fold_in(jax.random.fold_in(stream_key, 6), position), (blocks,), jnp.float32, low / len(shards), high / len(shards))
        factor_of = factor_of * jnp.repeat(jnp.exp(steps), extent[position] // blocks).reshape((-1,) + (1,) * (len(extent) - 1 - position))
    return factor_of


def normal_values(own_key, extent, deviation, bound, shards=(), kind=jnp.bfloat16):
    gain = block_levels(own_key, extent, shards, -0.22, 0.18) if shards else 1.0
    values = jax.random.normal(own_key, extent, jnp.float32) * deviation * gain
    return jnp.minimum(jnp.maximum(values, -bound), bound).astype(kind)


def setup_inputs(seed: int = 0) -> dict:
    key_of = jax.random.split(jax.random.key(seed), 11)
    return {
        "initial": normal_values(key_of[0], (FIELDS, NX, NY), 1.0, 6.0, ((0, 8), (1, 16)), jnp.float32),
        "conductivity": jnp.clip(jnp.exp(math.log(1.5) - 1.0986123 * jax.random.uniform(key_of[1], (FIELDS, NX, NY), jnp.float32) ** block_levels(key_of[1], (FIELDS, NX, NY), ((0, 8), (1, 16)), -0.2, 0.2)), 0.5, 1.5),
        "step_count": draw_step_count(jax.random.fold_in(key_of[10], 71), 0),
        "emit_steps": draw_emit_steps(jax.random.fold_in(key_of[10], 71), 0),
        "assign": place_ends(jax.random.randint(key_of[4], (BATCH,), 0, FIELDS * SNAPS), jax.random.fold_in(key_of[4], 1), 0, (FIELDS * SNAPS) - 1).astype(jnp.int32),
        "sample_inputs": normal_values(key_of[5], (BATCH, FEATURES), 1.0, 6.0, ((0, 128),)),
        "w_first": normal_values(key_of[6], (FEATURES, HIDDEN_SIZE), FEATURES ** -0.5, 0.5),
        "w_second": normal_values(key_of[7], (HIDDEN_SIZE, HIDDEN_SIZE), HIDDEN_SIZE ** -0.5, 0.25),
        "w_third": normal_values(key_of[8], (HIDDEN_SIZE, HIDDEN_SIZE), HIDDEN_SIZE ** -0.5, 0.25),
        "w_out": normal_values(key_of[9], (HIDDEN_SIZE, NX, NY), HIDDEN_SIZE ** -0.5, 0.25, ((1, 16), (2, 8))),
    }


step_rate = 0.125

def evolve(initial, conductivity, step_count, emit_steps):

    def one_step(step_index, carried):
        field_now, snapshots = carried
        padded = jnp.pad(field_now, ((0, 0), (1, 1), (1, 1)))
        beside_all = padded[:, 2:, 1:-1] + padded[:, :-2, 1:-1] + padded[:, 1:-1, 2:] + padded[:, 1:-1, :-2]
        candidate = field_now + step_rate * conductivity * (1.0 + 0.25 * jnp.tanh(field_now)) * (beside_all - 4.0 * field_now)
        field_now = jnp.where((step_index < step_count)[:, None, None], candidate, field_now)
        matched = emit_steps == step_index + 1
        snapshots = jnp.where(matched[:, :, None, None], field_now[:, None], snapshots)
        return (field_now, snapshots)
    start_snaps = jnp.zeros((FIELDS, SNAPS, NX, NY), jnp.float32)
    field_now, snapshots = lax.fori_loop(0, STEPS, one_step, (initial, start_snaps))
    return snapshots.astype(jnp.bfloat16)

def contract_rows(left, right):
    return lax.dot_general(left, right, (((0,), (0,)), ((), ())), preferred_element_type=jnp.float32)

def contract_cols(left, right):
    return lax.dot_general(left, right, (((1,), (1,)), ((), ())), preferred_element_type=jnp.float32)

def reference(initial, conductivity, step_count, emit_steps, assign, sample_inputs, w_first, w_second, w_third, w_out):
    snapshots = evolve(initial, conductivity, step_count, emit_steps)
    flat_snaps = snapshots.reshape(FIELDS * SNAPS, NX, NY)
    act_a = jnp.tanh(jnp.dot(sample_inputs, w_first, preferred_element_type=jnp.float32))
    hidden_a = act_a.astype(jnp.bfloat16)
    act_b = jnp.tanh(jnp.dot(hidden_a, w_second, preferred_element_type=jnp.float32))
    hidden_b = act_b.astype(jnp.bfloat16)
    act_c = jnp.tanh(jnp.dot(hidden_b, w_third, preferred_element_type=jnp.float32))
    hidden_c = act_c.astype(jnp.bfloat16)
    inverse_root = 1.0 / jnp.sqrt(jnp.float32(BATCH))

    def block_fn(block_index):
        first_row = (block_index * ROWS_DEV).astype(jnp.int32)
        weight_block = lax.dynamic_slice_in_dim(w_out, first_row, ROWS_DEV, 1).reshape(HIDDEN_SIZE, ROWS_DEV * NY)
        snap_block = lax.dynamic_slice_in_dim(flat_snaps, first_row, ROWS_DEV, 1)
        target_block = jnp.take(snap_block, assign, axis=0).reshape(BATCH, ROWS_DEV * NY)
        predicted = jnp.dot(hidden_c, weight_block, preferred_element_type=jnp.float32)
        residual = ((predicted - target_block.astype(jnp.float32)) * inverse_root).astype(jnp.bfloat16)
        grad_block = contract_rows(hidden_c, residual).astype(jnp.bfloat16)
        back_block = contract_cols(residual, weight_block)
        return (grad_block.reshape(HIDDEN_SIZE, ROWS_DEV, NY), back_block)
    grad_blocks, back_blocks = lax.map(block_fn, jnp.arange(NX // ROWS_DEV, dtype=jnp.int32))
    grad_out = jnp.transpose(grad_blocks, (1, 0, 2, 3)).reshape(HIDDEN_SIZE, NX, NY)
    back_c = lax.optimization_barrier(jnp.sum(back_blocks, axis=0))
    delta_c = (back_c * (1.0 - act_c * act_c)).astype(jnp.bfloat16)
    grad_third = contract_rows(hidden_b, delta_c)
    back_b = contract_cols(delta_c, w_third)
    delta_b = (back_b * (1.0 - act_b * act_b)).astype(jnp.bfloat16)
    grad_second = contract_rows(hidden_a, delta_b)
    back_a = contract_cols(delta_b, w_second)
    delta_a = (back_a * (1.0 - act_a * act_a)).astype(jnp.bfloat16)
    grad_first = contract_rows(sample_inputs, delta_a)
    return (grad_first, grad_second, grad_third, grad_out)
```

```python
import jax
import jax.numpy as jnp
from jax import lax
from jax.experimental import pallas as pl
from jax.experimental.pallas import tpu as pltpu
from jax.sharding import PartitionSpec as P

MESH = pl.DeviceIdType.MESH
F32, BF16 = jnp.float32, jnp.bfloat16
STEPS, SNAPS, ROWS, HID, FEAT = 32, 16, 32, 512, 128
GROUPS, STRIPS = 8, 16
DEVS, CHIPS = GROUPS * STRIPS, GROUPS * STRIPS // 2
REGION = 3 * ROWS
PAIRS = ROWS // 2
CHUNK = 4


def dot(a, b):
    return jnp.dot(a, b, preferred_element_type=F32)


def dot_nt(a, b):
    return lax.dot_general(a, b, (((1,), (1,)), ((), ())), preferred_element_type=F32)


def swap_matrix():
    row = lax.broadcasted_iota(jnp.int32, (256, 256), 0)
    col = lax.broadcasted_iota(jnp.int32, (256, 256), 1)
    return jnp.where((row % 16) * 16 + row // 16 == col, 1.0, 0.0).astype(BF16)


def main_kernel(
    initial, conductivity, step_count, emit_steps, assign, sample_inputs,
    w_first, w_second, w_third, w_out,
    gout_hbm, acta_hbm, actb_hbm, hat_hbm, hbt_hbm, xt_hbm, delta_hbm,
    land_u, land_k, state_a, state_b, kap, hist, tmp, send, snaps, part, gath,
    raw, w2, pred, resid, acc, pair_in, pieces, delta, act_a, act_b, act_c, hat, hbt, hct, xt, hidc, onehot,
    wf, ws, wt,
    halo_send, halo_recv, part_send, part_recv, gath_send, gath_recv, snap_send, snap_recv,
    pair_send, pair_recv, piece_send, piece_recv, delta_send, delta_recv, twin_send, twin_recv,
    w_sem, raw_sem, own_sem, out_sem,
):
    g, s = lax.axis_index("group"), lax.axis_index("strip")
    me = g * STRIPS + s
    core = s % 2
    chip = g * (STRIPS // 2) + s // 2
    twin = (g, s + 1 - 2 * core)

    def remote(src, dst, send_sem, recv_sem, device):
        return pltpu.make_async_remote_copy(
            src_ref=src, dst_ref=dst, send_sem=send_sem, recv_sem=recv_sem, device_id=device, device_id_type=MESH
        )

    barrier = pltpu.get_barrier_semaphore()

    @pl.loop(1, DEVS)
    def _(i):
        peer = (me + i) % DEVS
        pl.semaphore_signal(barrier, inc=1, device_id=(peer // STRIPS, peer % STRIPS), device_id_type=MESH)

    raw_copies = [
        pltpu.make_async_copy(w_out.at[pl.ds(64 * i, 64)], raw.at[pl.ds(64 * i, 64)], raw_sem.at[i]) for i in range(8)
    ]
    for copy in raw_copies:
        copy.start()
    weight_copies = [
        pltpu.make_async_copy(a, b, w_sem.at[i]) for i, (a, b) in enumerate(((w_first, wf), (w_second, ws), (w_third, wt)))
    ]
    for copy in weight_copies:
        copy.start()

    def spread(ref, first_row, x):
        for j in range(8):
            ref[pl.ds(first_row * 8 + j, ROWS, stride=8), :] = x[:, j * 128 : (j + 1) * 128]

    spread(state_a, ROWS, initial[0])
    spread(kap, ROWS, 0.125 * conductivity[0])
    quad = s % 4
    part[quad, 0:4, :] = sample_inputs[...].astype(F32)
    ids = lax.broadcasted_iota(jnp.int32, (DEVS, HID), 0)
    onehot[...] = jnp.transpose(jnp.where(ids == assign[...], 1.0, 0.0)).astype(BF16)
    swap = swap_matrix()

    pl.semaphore_wait(barrier, DEVS - 1)

    above, below = (g, jnp.maximum(s - 1, 0)), (g, jnp.minimum(s + 1, STRIPS - 1))
    up_copies = [
        remote(initial.at[0], land_u.at[1], halo_send.at[0], halo_recv.at[0], above),
        remote(conductivity.at[0], land_k.at[1], halo_send.at[1], halo_recv.at[1], above),
    ]
    down_copies = [
        remote(initial.at[0], land_u.at[0], halo_send.at[2], halo_recv.at[2], below),
        remote(conductivity.at[0], land_k.at[0], halo_send.at[3], halo_recv.at[3], below),
    ]

    @pl.when(s > 0)
    def _():
        for copy in up_copies:
            copy.start()

    @pl.when(s < STRIPS - 1)
    def _():
        for copy in down_copies:
            copy.start()

    for i in range(1, 4):
        remote(part.at[quad], part.at[quad], part_send, part_recv, (g, s - quad + (quad + i) % 4)).start()

    def relayout_weights(i, carry):
        for half in range(2):
            k0 = pl.multiple_of((i * 2 + half) * 16, 16)
            x = jnp.concatenate([raw[pl.ds(k0, 16), b * 16 : b * 16 + 16, :].reshape(256, 128) for b in range(2)], axis=1)
            y = dot(swap, x).astype(BF16)
            for b in range(2):
                for r in range(16):
                    row = b * 16 + r
                    w2[row // 2, pl.ds(k0, 16), (row % 2) * 128 : (row % 2) * 128 + 128] = y[
                        r * 16 : r * 16 + 16, b * 128 : b * 128 + 128
                    ]
        return carry

    for i, copy in enumerate(raw_copies):
        copy.wait()
    lax.fori_loop(0, 16, relayout_weights, 0)

    remote(part.at[pl.ds(0, 3)], part.at[pl.ds(0, 3)], part_send, part_recv, twin).wait()
    low = lax.broadcasted_iota(jnp.int32, (8, 128), 0) < 4
    tile = jnp.concatenate(
        [jnp.where(low, part[2 * i], pltpu.roll(part[2 * i + 1], 4, axis=0)) for i in range(2)], axis=0
    )
    mine = g * 4 + s // 4
    gath[mine] = tile.astype(BF16)

    @pl.loop(1, 32)
    def _(i):
        other = (mine + i) % 32
        remote(gath.at[mine], gath.at[mine], gath_send, gath_recv, (other // 4, (other % 4) * 4 + quad)).start()

    def land(has, copies_in, first_row, side):
        @pl.when(has)
        def _():
            for copy in copies_in:
                copy.wait_recv()
            spread(state_a, first_row, land_u[side])
            spread(kap, first_row, 0.125 * land_k[side])

        @pl.when(jnp.logical_not(has))
        def _():
            zero = jnp.zeros((ROWS * 8, 128), F32)
            state_a[pl.ds(first_row * 8, ROWS * 8), :] = zero
            kap[pl.ds(first_row * 8, ROWS * 8), :] = zero

    land(s > 0, down_copies, 0, 0)
    land(s < STRIPS - 1, up_copies, 2 * ROWS, 1)

    lane = lax.broadcasted_iota(jnp.int32, (8, 128), 1)
    sub = lax.broadcasted_iota(jnp.int32, (8, 128), 0)
    first_lane, last_lane = lane == 0, lane == 127
    west_end, east_end = first_lane & (sub == 0), last_lane & (sub == 7)

    def step(src, dst, first, last, t):
        prev = src[(first - 1) * 8 : first * 8, :]
        here = src[first * 8 : first * 8 + 8, :]
        for r in range(first, last + 1):
            after = src[(r + 1) * 8 : (r + 2) * 8, :]
            w = pltpu.roll(here, 1, axis=1)
            w = jnp.where(west_end, 0.0, jnp.where(first_lane, pltpu.roll(w, 1, axis=0), w))
            e = pltpu.roll(here, 127, axis=1)
            e = jnp.where(east_end, 0.0, jnp.where(last_lane, pltpu.roll(e, 7, axis=0), e))
            beside = (after + prev) + (e + w)
            new = here + kap[r * 8 : r * 8 + 8, :] * (1.0 + 0.25 * jnp.tanh(here)) * (beside - 4.0 * here)
            dst[r * 8 : r * 8 + 8, :] = new
            if ROWS <= r < 2 * ROWS:
                hist[t * ROWS + (r - ROWS)] = new
            prev, here = here, after

    for phase in range(8):
        first, last = 4 * phase + 1, REGION - 2 - 4 * phase

        @pl.loop(2 * phase, 2 * phase + 2)
        def _(i):
            step(state_a, state_b, first, last, 2 * i)
            step(state_b, state_a, first, last, 2 * i + 1)

    count = step_count[0]
    bases = [jnp.maximum(jnp.minimum(emit_steps[0, k], count) - 1, 0) * ROWS for k in range(SNAPS)]

    def pack(rp, carry):
        for h in range(2):
            for k in range(SNAPS):
                tmp[h, pl.ds(k, 8, stride=16), :] = hist[bases[k] + (2 * rp + h)]
            for to in range(GROUPS):
                send[to, rp, :, h * 128 : h * 128 + 128] = tmp[h, to * 16 : to * 16 + 16, :].astype(BF16)
        return carry

    def snap_copy(c, to):
        rows = pl.ds(c * CHUNK, CHUNK)
        return remote(
            send.at[to, rows],
            snaps.at[rows, pl.ds(pl.multiple_of(g * SNAPS, SNAPS), SNAPS), :],
            snap_send,
            snap_recv.at[c],
            (to, s),
        )

    for c in range(PAIRS // CHUNK):
        lax.fori_loop(c * CHUNK, (c + 1) * CHUNK, pack, 0)

        @pl.loop(1, GROUPS)
        def _(i):
            snap_copy(c, (g + i) % GROUPS).start()

    own = pltpu.make_async_copy(
        send.at[g], snaps.at[:, pl.ds(pl.multiple_of(g * SNAPS, SNAPS), SNAPS), :], own_sem
    )
    own.start()

    for copy in weight_copies:
        copy.wait()
    remote(gath.at[pl.ds(0, 31)], gath.at[pl.ds(0, 31)], gath_send, gath_recv, twin).wait()

    @pl.loop(0, 4)
    def _(m):
        rows = pl.ds(pl.multiple_of(m * 128, 128), 128)
        x = gath[pl.ds(m * 8, 8)].reshape(128, FEAT)
        xt[:, rows] = jnp.transpose(x.astype(F32)).astype(BF16)
        a = jnp.tanh(dot(x, wf[...]))
        act_a[rows, :] = a
        hat[:, rows] = jnp.transpose(a).astype(BF16)
        b = jnp.tanh(dot(a.astype(BF16), ws[...]))
        act_b[rows, :] = b
        hbt[:, rows] = jnp.transpose(b).astype(BF16)
        c = jnp.tanh(dot(b.astype(BF16), wt[...]))
        hct[:, rows] = jnp.transpose(c).astype(BF16)
        hidc[rows, :] = c.astype(BF16)
        for kb in range(4):
            act_c[pl.ds(kb * 32 + m * 8, 8)] = c[:, kb * 128 : kb * 128 + 128].reshape(8, 16, 128)

    outs = [
        pltpu.make_async_copy(a, b, out_sem.at[i])
        for i, (a, b) in enumerate(((act_a, acta_hbm), (act_b, actb_hbm), (hat, hat_hbm), (hbt, hbt_hbm), (xt, xt_hbm)))
    ]
    for copy in outs:
        copy.start()

    @pl.loop(0, PAIRS)
    def _(rp):
        pred[rp] = dot(hidc[...], w2[rp])

    own.wait()
    inverse_root = F32(1.0) / jnp.sqrt(F32(HID))

    def residual_chunk(c):
        remote(snaps.at[pl.ds(0, CHUNK), pl.ds(0, 112), :], snaps.at[pl.ds(0, CHUNK), pl.ds(0, 112), :],
               snap_send, snap_recv.at[c], twin).wait_recv()

        @pl.loop(c * CHUNK, (c + 1) * CHUNK)
        def _(rp):
            resid[rp] = ((pred[rp] - dot(onehot[...], snaps[rp])) * inverse_root).astype(BF16)

    def back_half(c, half, fresh):
        left = jnp.concatenate([resid[c * CHUNK + i] for i in range(CHUNK)], axis=1)
        k0 = pl.multiple_of(half * 256, 256)
        right = jnp.concatenate([w2[c * CHUNK + i, pl.ds(k0, 256), :] for i in range(CHUNK)], axis=1)
        value = dot_nt(left, right)
        for kb in range(2):
            at = pl.ds(half * 64 + kb * 32, 32)
            v = value[:, kb * 128 : kb * 128 + 128].reshape(32, 16, 128)
            acc[at] = v if fresh else acc[at] + v

    residual_chunk(0)
    back_half(0, 1 - core, True)
    back_half(0, core, True)

    @pl.loop(1, 3)
    def _(c):
        residual_chunk(c)
        back_half(c, 1 - core, False)
        back_half(c, core, False)

    residual_chunk(3)
    back_half(3, 1 - core, False)
    theirs = pl.ds((1 - core) * 64, 64)
    to_twin = remote(acc.at[theirs], pair_in, pair_send, pair_recv, twin)
    to_twin.start()
    back_half(3, core, False)
    to_twin.wait_recv()

    @pl.loop(0, 8)
    def _(i):
        at = pl.ds(core * 64 + i * 8, 8)
        acc[at] = acc[at] + pair_in[pl.ds(i * 8, 8)]

    @pl.loop(1, CHIPS)
    def _(i):
        p = (chip + i) % CHIPS
        remote(acc.at[core * 64 + p], pieces.at[chip], piece_send, piece_recv, (p // 8, (p % 8) * 2 + core)).start()

    pieces[chip] = acc[core * 64 + chip]

    @pl.loop(0, PAIRS)
    def _(rp):
        w2[rp] = dot(hct[...], resid[rp]).astype(BF16)

    remote(pieces.at[pl.ds(0, 63)], pieces.at[pl.ds(0, 63)], piece_send, piece_recv, twin).wait_recv()
    total = pieces[0]
    for i in range(1, CHIPS):
        total = total + pieces[i]
    a = act_c[core * 64 + chip]
    delta[core * 64 + chip] = (total * (1.0 - a * a)).astype(BF16)

    @pl.loop(1, CHIPS)
    def _(i):
        p = (chip + i) % CHIPS
        at = core * 64 + chip
        remote(delta.at[at], delta.at[at], delta_send, delta_recv, (p // 8, (p % 8) * 2 + core)).start()

    def relayout_grad(i, carry):
        for half in range(2):
            k0 = pl.multiple_of((i * 2 + half) * 16, 16)
            x = jnp.concatenate(
                [
                    jnp.concatenate(
                        [w2[b * 8 + r // 2, pl.ds(k0, 16), (r % 2) * 128 : (r % 2) * 128 + 128] for r in range(16)], axis=0
                    )
                    for b in range(2)
                ],
                axis=1,
            )
            y = dot(swap, x).astype(BF16)
            for b in range(2):
                raw[pl.ds(k0, 16), b * 16 : b * 16 + 16, :] = y[:, b * 128 : b * 128 + 128].reshape(16, 16, 128)
        return carry

    lax.fori_loop(0, 16, relayout_grad, 0)
    grad_copy = pltpu.make_async_copy(raw, gout_hbm, out_sem.at[5])
    grad_copy.start()

    remote(delta.at[pl.ds(0, 63)], delta.at[pl.ds(0, 63)], delta_send, delta_recv, twin).wait_recv()
    ours = pl.ds(core * 64, 64)
    to_twin2 = remote(delta.at[ours], delta.at[ours], twin_send, twin_recv, twin)
    to_twin2.start()
    to_twin2.wait_recv()
    delta_copy = pltpu.make_async_copy(delta, delta_hbm, out_sem.at[6])
    delta_copy.start()

    @pl.when(s > 0)
    def _():
        for copy in up_copies:
            copy.wait_send()

    @pl.when(s < STRIPS - 1)
    def _():
        for copy in down_copies:
            copy.wait_send()

    remote(send.at[pl.ds(0, 7)], send.at[pl.ds(0, 7)], snap_send, snap_recv.at[0], twin).wait_send()
    to_twin.wait_send()
    remote(pieces.at[pl.ds(0, 63)], pieces.at[pl.ds(0, 63)], piece_send, piece_recv, twin).wait_send()
    remote(delta.at[pl.ds(0, 63)], delta.at[pl.ds(0, 63)], delta_send, delta_recv, twin).wait_send()
    to_twin2.wait_send()
    for copy in outs:
        copy.wait()
    grad_copy.wait()
    delta_copy.wait()


def final_kernel(
    gout_in, acta_in, actb_in, hat_in, hbt_in, xt_in, delta_in, ws_in, wt_in,
    g1_out, g2_out, g3_out, gout_out,
    stage, act_a, act_b, hat, hbt, xt, delta, ws, wt, g1, g2, g3, in_sem, stage_in, stage_out, out_sem,
):
    loads = [
        pltpu.make_async_copy(a, b, in_sem.at[i])
        for i, (a, b) in enumerate((
            (delta_in, delta), (hbt_in, hbt), (wt_in, wt), (actb_in, act_b), (hat_in, hat), (ws_in, ws),
            (acta_in, act_a), (xt_in, xt),
        ))
    ]
    for copy in loads:
        copy.start()
    parts = [pl.ds(i * 64, 64) for i in range(8)]
    ins = [pltpu.make_async_copy(gout_in.at[p], stage.at[p], stage_in.at[i]) for i, p in enumerate(parts)]
    outs = [pltpu.make_async_copy(stage.at[p], gout_out.at[p], stage_out.at[i]) for i, p in enumerate(parts)]
    for copy in ins:
        copy.start()
    for copy in loads[:3]:
        copy.wait()
    dc = jnp.concatenate([delta[i * 32 : i * 32 + 32].reshape(HID, 128) for i in range(4)], axis=1)
    g3[...] = dot(hbt[...], dc)
    to_g3 = pltpu.make_async_copy(g3, g3_out, out_sem.at[0])
    to_g3.start()
    for a, b in zip(ins, outs):
        a.wait()
        b.start()
    loads[3].wait()
    db = (dot_nt(dc, wt[...]) * (1.0 - act_b[...] * act_b[...])).astype(BF16)
    loads[4].wait()
    g2[...] = dot(hat[...], db)
    to_g2 = pltpu.make_async_copy(g2, g2_out, out_sem.at[1])
    to_g2.start()
    loads[5].wait()
    loads[6].wait()
    da = (dot_nt(db, ws[...]) * (1.0 - act_a[...] * act_a[...])).astype(BF16)
    loads[7].wait()
    g1[...] = dot(xt[...], da)
    to_g1 = pltpu.make_async_copy(g1, g1_out, out_sem.at[2])
    to_g1.start()
    for copy in outs + [to_g3, to_g2, to_g1]:
        copy.wait()


def per_device(initial, conductivity, step_count, emit_steps, assign, sample_inputs, w_first, w_second, w_third, w_out):
    vmem, smem = pl.BlockSpec(memory_space=pltpu.VMEM), pl.BlockSpec(memory_space=pltpu.SMEM)
    hbm = pl.BlockSpec(memory_space=pl.ANY)
    shape = jax.ShapeDtypeStruct
    dma = pltpu.SemaphoreType.DMA
    mats = (
        shape((HID, HID), F32), shape((HID, HID), F32), shape((HID, HID), BF16), shape((HID, HID), BF16),
        shape((FEAT, HID), BF16), shape((DEVS, 16, 128), BF16),
    )
    gout, *kept = pl.pallas_call(
        main_kernel,
        out_shape=(shape((HID, ROWS, 128), BF16),) + mats,
        in_specs=[vmem, vmem, smem, smem, vmem, vmem, hbm, hbm, hbm, hbm],
        out_specs=[hbm] * 7,
        scratch_shapes=[
            pltpu.VMEM((2, ROWS, 1024), F32), pltpu.VMEM((2, ROWS, 1024), F32),
            pltpu.VMEM((REGION * 8, 128), F32), pltpu.VMEM((REGION * 8, 128), F32), pltpu.VMEM((REGION * 8, 128), F32),
            pltpu.VMEM((STEPS * ROWS, 8, 128), F32),
            pltpu.VMEM((2, 128, 128), F32),
            pltpu.VMEM((GROUPS, PAIRS, SNAPS, 256), BF16),
            pltpu.VMEM((PAIRS, DEVS, 256), BF16),
            pltpu.VMEM((4, 8, 128), F32),
            pltpu.VMEM((32, 16, 128), BF16),
            pltpu.VMEM((HID, ROWS, 128), BF16),
            pltpu.VMEM((PAIRS, HID, 256), BF16),
            pltpu.VMEM((PAIRS, HID, 256), F32),
            pltpu.VMEM((PAIRS, HID, 256), BF16),
            pltpu.VMEM((DEVS, 16, 128), F32),
            pltpu.VMEM((64, 16, 128), F32),
            pltpu.VMEM((CHIPS, 16, 128), F32),
            pltpu.VMEM((DEVS, 16, 128), BF16),
            pltpu.VMEM((HID, HID), F32), pltpu.VMEM((HID, HID), F32), pltpu.VMEM((DEVS, 16, 128), F32),
            pltpu.VMEM((HID, HID), BF16), pltpu.VMEM((HID, HID), BF16), pltpu.VMEM((HID, HID), BF16),
            pltpu.VMEM((FEAT, HID), BF16), pltpu.VMEM((HID, HID), BF16), pltpu.VMEM((HID, DEVS), BF16),
            pltpu.VMEM((FEAT, HID), BF16), pltpu.VMEM((HID, HID), BF16), pltpu.VMEM((HID, HID), BF16),
            dma((4,)), dma((4,)), dma, dma, dma, dma, dma, dma((4,)),
            dma, dma, dma, dma, dma, dma, dma, dma,
            dma((3,)), dma((8,)), dma, dma((7,)),
        ],
        compiler_params=pltpu.CompilerParams(
            collective_id=0, has_side_effects=True, vmem_limit_bytes=60 * 1024 * 1024
        ),
        name="solve_and_reduce",
    )(
        initial, conductivity, step_count, emit_steps, assign.reshape(1, HID), sample_inputs,
        w_first, w_second, w_third, w_out,
    )
    outs = pl.pallas_call(
        final_kernel,
        out_shape=(shape((FEAT, HID), F32), shape((HID, HID), F32), shape((HID, HID), F32), shape((HID, ROWS, 128), BF16)),
        in_specs=[hbm] * 9,
        out_specs=[hbm] * 4,
        scratch_shapes=[
            pltpu.VMEM((HID, ROWS, 128), BF16), pltpu.VMEM((HID, HID), F32), pltpu.VMEM((HID, HID), F32),
            pltpu.VMEM((HID, HID), BF16), pltpu.VMEM((HID, HID), BF16), pltpu.VMEM((FEAT, HID), BF16),
            pltpu.VMEM((DEVS, 16, 128), BF16), pltpu.VMEM((HID, HID), BF16), pltpu.VMEM((HID, HID), BF16),
            pltpu.VMEM((FEAT, HID), F32), pltpu.VMEM((HID, HID), F32), pltpu.VMEM((HID, HID), F32),
            dma((8,)), dma((8,)), dma((8,)), dma((3,)),
        ],
        name="outputs",
        compiler_params=pltpu.CompilerParams(vmem_limit_bytes=63 * 1024 * 1024),
    )(gout, *kept, w_second, w_third)
    return tuple(outs)


def solution(mesh):
    placed = (
        P("group", "strip", None), P("group", "strip", None), P("group"), P("group", None), P(),
        P(("group", "strip"), None), P(), P(), P(), P(None, "strip", "group"),
    )
    return jax.shard_map(
        per_device, mesh=mesh, in_specs=placed, out_specs=(P(), P(), P(), P(None, "strip", "group")), check_vma=False
    )
```

```python
import jax
import jax.numpy as jnp
from jax import lax
from jax.experimental import pallas as pl
from jax.experimental.pallas import tpu as pltpu
from jax.sharding import PartitionSpec as P

FLAT = pl.DeviceIdType.LOGICAL
F32, BF16 = jnp.float32, jnp.bfloat16
STEPS, SNAPS, ROWS, HID, FEAT = 32, 16, 32, 512, 128
GROUPS, STRIPS = 8, 16
DEVS, CHIPS = GROUPS * STRIPS, GROUPS * STRIPS // 2
REGION = 3 * ROWS
PAIRS = ROWS // 2
CHUNK = 4
PAD = 8
MAIN_VMEM = 42 * 1024 * 1024


def dot(a, b):
    return jnp.dot(a, b, preferred_element_type=F32)


def dot_nt(a, b):
    return lax.dot_general(a, b, (((1,), (1,)), ((), ())), preferred_element_type=F32)


def swap_matrix():
    row = lax.broadcasted_iota(jnp.int32, (256, 256), 0)
    col = lax.broadcasted_iota(jnp.int32, (256, 256), 1)
    return jnp.where((row % 16) * 16 + row // 16 == col, 1.0, 0.0).astype(BF16)


def main_kernel(
    initial_hbm, conductivity_hbm, step_count, emit_steps, assign_hbm, sample_hbm,
    w_first, w_second, w_third, w_out,
    gout_hbm, acta_hbm, actb_hbm, hat_hbm, hbt_hbm, xt_hbm, delta_hbm,
    state_a, state_b, kap, quarter, hist, tmp, send, snaps, part, gath,
    raw, w2, pred, resid, acc, pair_in, pieces, delta, act_a, act_b, act_c, hat, hbt, hct, xt, hidc, onehot,
    wf, ws, wt, initial, conductivity, assign, sample_inputs,
    halo_send, halo_recv, part_send, part_recv, gath_send, gath_recv, snap_send, snap_recv,
    pair_send, pair_recv, piece_send, piece_recv, delta_send, delta_recv, twin_send, twin_recv,
    w_sem, raw_sem, own_sem, out_sem, in_sem,
):
    g, s = lax.axis_index("group"), lax.axis_index("strip")
    me = g * STRIPS + s
    core = s % 2
    chip = g * (STRIPS // 2) + s // 2
    twin = me + 1 - 2 * core
    quad = s % 4

    def wrap(i, n):
        return jnp.where(i >= n, i - n, i)

    def each_chip(fn):
        @pl.loop(0, 7)
        def _(i):
            for j in range(9):
                p = wrap(chip + 1 + i * 9 + j, CHIPS)
                fn(p, p * 2 + core)

    def remote(src, dst, send_sem, recv_sem, device):
        return pltpu.make_async_remote_copy(
            src_ref=src, dst_ref=dst, send_sem=send_sem, recv_sem=recv_sem, device_id=device, device_id_type=FLAT
        )

    inputs = [
        pltpu.make_async_copy(a, b, in_sem.at[i])
        for i, (a, b) in enumerate((
            (initial_hbm, initial), (conductivity_hbm, conductivity), (sample_hbm, sample_inputs), (assign_hbm, assign)
        ))
    ]
    for copy in inputs:
        copy.start()
    barrier = pltpu.get_barrier_semaphore()

    def greet(device):
        pl.semaphore_signal(barrier, inc=1, device_id=device, device_id_type=FLAT)

    greet(twin)
    greet(me + 3 - 2 * quad)
    next_quad = ((quad == 0) & (s > 0)) | ((quad == 3) & (s < STRIPS - 1))

    @pl.when(next_quad)
    def _():
        greet(jnp.where(quad == 0, me - 1, me + 1))

    each_chip(lambda p, device: greet(device))

    raw_copies = [
        pltpu.make_async_copy(w_out.at[pl.ds(64 * i, 64)], raw.at[pl.ds(64 * i, 64)], raw_sem.at[i]) for i in range(8)
    ]
    for copy in raw_copies:
        copy.start()
    weight_copies = [
        pltpu.make_async_copy(a, b, w_sem.at[i]) for i, (a, b) in enumerate(((w_first, wf), (w_second, ws), (w_third, wt)))
    ]
    for copy in weight_copies:
        copy.start()

    for copy in inputs:
        copy.wait()
    own_rows, rows_above, rows_below = pl.ds(PAD + ROWS, ROWS), pl.ds(PAD, ROWS), pl.ds(PAD + 2 * ROWS, ROWS)
    for j in range(8):
        state_a[j, own_rows, :] = initial[0, :, j * 128 : (j + 1) * 128]
        kap[j, own_rows, :] = 0.125 * conductivity[0, :, j * 128 : (j + 1) * 128]
        for ref in (state_a, state_b):
            ref[j, 0:PAD, :] = jnp.zeros((PAD, 128), F32)
            ref[j, PAD + REGION :, :] = jnp.zeros((PAD, 128), F32)
    part[quad, 0:4, :] = sample_inputs[...].astype(F32)
    ids = lax.broadcasted_iota(jnp.int32, (DEVS, HID), 0)
    onehot[...] = jnp.transpose(jnp.where(ids == assign[...], 1.0, 0.0)).astype(BF16)
    swap = swap_matrix()

    pl.semaphore_wait(barrier, CHIPS + 1 + jnp.where(next_quad, 1, 0))

    above, below = jnp.where(s > 0, me - 1, me), jnp.where(s < STRIPS - 1, me + 1, me)
    up_copies = [
        remote(ref.at[:, own_rows], ref.at[:, rows_below], halo_send.at[i], halo_recv.at[i], above)
        for i, ref in enumerate((state_a, kap))
    ]
    down_copies = [
        remote(ref.at[:, own_rows], ref.at[:, rows_above], halo_send.at[2 + i], halo_recv.at[2 + i], below)
        for i, ref in enumerate((state_a, kap))
    ]

    @pl.when(s > 0)
    def _():
        for copy in up_copies:
            copy.start()

    @pl.when(s < STRIPS - 1)
    def _():
        for copy in down_copies:
            copy.start()

    for i in range(1, 4):
        remote(part.at[quad], part.at[quad], part_send, part_recv, me - quad + wrap(quad + i, 4)).start()

    def relayout_weights(i, carry):
        for half in range(2):
            k0 = pl.multiple_of((i * 2 + half) * 16, 16)
            x = jnp.concatenate([raw[pl.ds(k0, 16), b * 16 : b * 16 + 16, :].reshape(256, 128) for b in range(2)], axis=1)
            y = dot(swap, x).astype(BF16)
            for b in range(2):
                for r in range(16):
                    row = b * 16 + r
                    w2[row // 2, pl.ds(k0, 16), (row % 2) * 128 : (row % 2) * 128 + 128] = y[
                        r * 16 : r * 16 + 16, b * 128 : b * 128 + 128
                    ]
        return carry

    for i, copy in enumerate(raw_copies):
        copy.wait()
    lax.fori_loop(0, 16, relayout_weights, 0)

    remote(part.at[pl.ds(0, 3)], part.at[pl.ds(0, 3)], part_send, part_recv, twin).wait()
    low = lax.broadcasted_iota(jnp.int32, (8, 128), 0) < 4
    tile = jnp.concatenate(
        [jnp.where(low, part[2 * i], pltpu.roll(part[2 * i + 1], 4, axis=0)) for i in range(2)], axis=0
    )
    mine = g * 4 + s // 4
    gath[mine] = tile.astype(BF16)

    for i in range(1, 32):
        remote(gath.at[mine], gath.at[mine], gath_send, gath_recv, wrap(mine + i, 32) * 4 + quad).start()

    def land(has, copies_in, copies_out, rows):
        @pl.when(has)
        def _():
            for copy in copies_in:
                copy.wait_recv()
            for copy in copies_out:
                copy.wait_send()

        @pl.when(jnp.logical_not(has))
        def _():
            zero = jnp.zeros((8, ROWS, 128), F32)
            state_a[:, rows] = zero
            kap[:, rows] = zero

    land(s > 0, down_copies, up_copies, rows_above)
    land(s < STRIPS - 1, up_copies, down_copies, rows_below)

    @pl.loop(0, 8)
    def _(j):
        quarter[j] = 0.25 * kap[j]

    lane = lax.broadcasted_iota(jnp.int32, (8, 128), 1)
    first_lane, last_lane = lane == 0, lane == 127
    zero_tile = jnp.zeros((8, 128), F32)

    def step(src, dst, first, last, t):
        for tile in range(first, last):
            r = PAD + tile * 8
            here = [src[j, r : r + 8, :] for j in range(8)]
            to_east = [zero_tile] + [pltpu.roll(x, 1, axis=1) for x in here]
            to_west = [pltpu.roll(x, 127, axis=1) for x in here] + [zero_tile]
            for j in range(8):
                w = jnp.where(first_lane, to_east[j], to_east[j + 1])
                e = jnp.where(last_lane, to_west[j + 1], to_west[j])
                beside = (src[j, r - 1 : r + 7, :] + src[j, r + 1 : r + 9, :]) + (e + w)
                rate = kap[j, r : r + 8, :] + quarter[j, r : r + 8, :] * jnp.tanh(here[j])
                new = here[j] + rate * (beside - 4.0 * here[j])
                dst[j, r : r + 8, :] = new
                if ROWS // 8 <= tile < 2 * ROWS // 8:
                    hist[t * 32 + (j * 4 + tile - ROWS // 8)] = new

    for phase in range(4):

        @pl.loop(4 * phase, 4 * phase + 4)
        def _(i):
            step(state_a, state_b, phase, REGION // 8 - phase, 2 * i)
            step(state_b, state_a, phase, REGION // 8 - phase, 2 * i + 1)

    count = step_count[0]
    bases = [jnp.maximum(jnp.minimum(emit_steps[0, k], count) - 1, 0) * 32 for k in range(SNAPS)]

    def pack(c):
        @pl.loop(0, 4)
        def _(i):
            for half in range(2):
                to = i * 2 + half
                for k in range(SNAPS):
                    tmp[to, pl.ds(k, 8, stride=16), :] = hist[bases[k] + (to * 4 + c)]
                for j in range(8):
                    send[to, c * CHUNK + j // 2, :, (j % 2) * 128 : (j % 2) * 128 + 128] = tmp[
                        to, j * 16 : j * 16 + 16, :
                    ].astype(BF16)

    def snap_copy(c, to):
        rows = pl.ds(c * CHUNK, CHUNK)
        return remote(
            send.at[to, rows],
            snaps.at[rows, pl.ds(pl.multiple_of(g * SNAPS, SNAPS), SNAPS), :],
            snap_send,
            snap_recv.at[c],
            to * STRIPS + s,
        )

    for c in range(PAIRS // CHUNK):
        pack(c)
        for i in range(1, GROUPS):
            snap_copy(c, wrap(g + i, GROUPS)).start()

    own = pltpu.make_async_copy(
        send.at[g], snaps.at[:, pl.ds(pl.multiple_of(g * SNAPS, SNAPS), SNAPS), :], own_sem
    )
    own.start()

    for copy in weight_copies:
        copy.wait()
    remote(gath.at[pl.ds(0, 31)], gath.at[pl.ds(0, 31)], gath_send, gath_recv, twin).wait()

    @pl.loop(0, 4)
    def _(m):
        rows = pl.ds(pl.multiple_of(m * 128, 128), 128)
        x = gath[pl.ds(m * 8, 8)].reshape(128, FEAT)
        xt[:, rows] = jnp.transpose(x.astype(F32)).astype(BF16)
        a = jnp.tanh(dot(x, wf[...]))
        act_a[rows, :] = a
        hat[:, rows] = jnp.transpose(a).astype(BF16)
        b = jnp.tanh(dot(a.astype(BF16), ws[...]))
        act_b[rows, :] = b
        hbt[:, rows] = jnp.transpose(b).astype(BF16)
        c = jnp.tanh(dot(b.astype(BF16), wt[...]))
        hct[:, rows] = jnp.transpose(c).astype(BF16)
        hidc[rows, :] = c.astype(BF16)
        for kb in range(4):
            act_c[pl.ds(kb * 32 + m * 8, 8)] = c[:, kb * 128 : kb * 128 + 128].reshape(8, 16, 128)

    outs = [
        pltpu.make_async_copy(a, b, out_sem.at[i])
        for i, (a, b) in enumerate(((act_a, acta_hbm), (act_b, actb_hbm), (hat, hat_hbm), (hbt, hbt_hbm), (xt, xt_hbm)))
    ]
    for copy in outs:
        copy.start()

    @pl.loop(0, PAIRS)
    def _(rp):
        pred[rp] = dot(hidc[...], w2[rp])

    own.wait()
    inverse_root = F32(1.0) / jnp.sqrt(F32(HID))

    def residual_chunk(c):
        remote(snaps.at[pl.ds(0, CHUNK), pl.ds(0, 112), :], snaps.at[pl.ds(0, CHUNK), pl.ds(0, 112), :],
               snap_send, snap_recv.at[c], twin).wait_recv()

        @pl.loop(c * CHUNK, (c + 1) * CHUNK)
        def _(rp):
            resid[rp] = ((pred[rp] - dot(onehot[...], snaps[rp])) * inverse_root).astype(BF16)

    def back_half(c, half, fresh):
        left = jnp.concatenate([resid[c * CHUNK + i] for i in range(CHUNK)], axis=1)
        k0 = pl.multiple_of(half * 256, 256)
        right = jnp.concatenate([w2[c * CHUNK + i, pl.ds(k0, 256), :] for i in range(CHUNK)], axis=1)
        value = dot_nt(left, right)
        for kb in range(2):
            at = pl.ds(half * 64 + kb * 32, 32)
            v = value[:, kb * 128 : kb * 128 + 128].reshape(32, 16, 128)
            acc[at] = v if fresh else acc[at] + v

    residual_chunk(0)
    back_half(0, 1 - core, True)
    back_half(0, core, True)

    @pl.loop(1, 3)
    def _(c):
        residual_chunk(c)
        back_half(c, 1 - core, False)
        back_half(c, core, False)

    residual_chunk(3)
    back_half(3, 1 - core, False)
    theirs = pl.ds((1 - core) * 64, 64)
    to_twin = remote(acc.at[theirs], pair_in, pair_send, pair_recv, twin)
    to_twin.start()
    back_half(3, core, False)
    to_twin.wait_recv()

    @pl.loop(0, 8)
    def _(i):
        at = pl.ds(core * 64 + i * 8, 8)
        acc[at] = acc[at] + pair_in[pl.ds(i * 8, 8)]

    each_chip(
        lambda p, device: remote(acc.at[core * 64 + p], pieces.at[chip], piece_send, piece_recv, device).start()
    )

    pieces[chip] = acc[core * 64 + chip]

    @pl.loop(0, PAIRS)
    def _(rp):
        w2[rp] = dot(hct[...], resid[rp]).astype(BF16)

    remote(pieces.at[pl.ds(0, 63)], pieces.at[pl.ds(0, 63)], piece_send, piece_recv, twin).wait_recv()
    total = pieces[0]
    for i in range(1, CHIPS):
        total = total + pieces[i]
    a = act_c[core * 64 + chip]
    delta[core * 64 + chip] = (total * (1.0 - a * a)).astype(BF16)

    at = core * 64 + chip
    each_chip(lambda p, device: remote(delta.at[at], delta.at[at], delta_send, delta_recv, device).start())

    def relayout_grad(i, carry):
        for half in range(2):
            k0 = pl.multiple_of((i * 2 + half) * 16, 16)
            x = jnp.concatenate(
                [
                    jnp.concatenate(
                        [w2[b * 8 + r // 2, pl.ds(k0, 16), (r % 2) * 128 : (r % 2) * 128 + 128] for r in range(16)], axis=0
                    )
                    for b in range(2)
                ],
                axis=1,
            )
            y = dot(swap, x).astype(BF16)
            for b in range(2):
                raw[pl.ds(k0, 16), b * 16 : b * 16 + 16, :] = y[:, b * 128 : b * 128 + 128].reshape(16, 16, 128)
        return carry

    lax.fori_loop(0, 16, relayout_grad, 0)
    grad_copy = pltpu.make_async_copy(raw, gout_hbm, out_sem.at[5])
    grad_copy.start()

    remote(delta.at[pl.ds(0, 63)], delta.at[pl.ds(0, 63)], delta_send, delta_recv, twin).wait_recv()
    ours = pl.ds(core * 64, 64)
    to_twin2 = remote(delta.at[ours], delta.at[ours], twin_send, twin_recv, twin)
    to_twin2.start()
    to_twin2.wait_recv()
    delta_copy = pltpu.make_async_copy(delta, delta_hbm, out_sem.at[6])
    delta_copy.start()

    remote(send.at[pl.ds(0, 7)], send.at[pl.ds(0, 7)], snap_send, snap_recv.at[0], twin).wait_send()
    to_twin.wait_send()
    remote(pieces.at[pl.ds(0, 63)], pieces.at[pl.ds(0, 63)], piece_send, piece_recv, twin).wait_send()
    remote(delta.at[pl.ds(0, 63)], delta.at[pl.ds(0, 63)], delta_send, delta_recv, twin).wait_send()
    to_twin2.wait_send()
    for copy in outs:
        copy.wait()
    grad_copy.wait()
    delta_copy.wait()


def final_kernel(
    gout_in, act_a, act_b, hat, hbt, xt, delta, ws_in, wt_in, g1_out, g2_out, g3_out, gout_out, ws, wt, g1, g2, g3, in_sem, out_sem
):
    loads = [pltpu.make_async_copy(a, b, in_sem.at[i]) for i, (a, b) in enumerate(((wt_in, wt), (ws_in, ws)))]
    for copy in loads:
        copy.start()
    to_gout = pltpu.make_async_copy(gout_in, gout_out, out_sem.at[3])
    to_gout.start()
    dc = jnp.concatenate([delta[i * 32 : i * 32 + 32].reshape(HID, 128) for i in range(4)], axis=1)
    g3[...] = dot(hbt[...], dc)
    to_g3 = pltpu.make_async_copy(g3, g3_out, out_sem.at[0])
    to_g3.start()
    loads[0].wait()
    db = (dot_nt(dc, wt[...]) * (1.0 - act_b[...] * act_b[...])).astype(BF16)
    g2[...] = dot(hat[...], db)
    to_g2 = pltpu.make_async_copy(g2, g2_out, out_sem.at[1])
    to_g2.start()
    loads[1].wait()
    da = (dot_nt(db, ws[...]) * (1.0 - act_a[...] * act_a[...])).astype(BF16)
    g1[...] = dot(xt[...], da)
    to_g1 = pltpu.make_async_copy(g1, g1_out, out_sem.at[2])
    to_g1.start()
    for copy in (to_gout, to_g3, to_g2, to_g1):
        copy.wait()


def per_device(initial, conductivity, step_count, emit_steps, assign, sample_inputs, w_first, w_second, w_third, w_out):
    vmem, smem = pl.BlockSpec(memory_space=pltpu.VMEM), pl.BlockSpec(memory_space=pltpu.SMEM)
    hbm = pl.BlockSpec(memory_space=pl.ANY)
    far = pl.BlockSpec(memory_space=pltpu.HBM)
    shape = jax.ShapeDtypeStruct
    dma = pltpu.SemaphoreType.DMA
    pin = lambda x: pltpu.with_memory_space_constraint(x, pltpu.HBM)
    mats = (
        shape((HID, HID), F32), shape((HID, HID), F32), shape((HID, HID), BF16), shape((HID, HID), BF16),
        shape((FEAT, HID), BF16), shape((DEVS, 16, 128), BF16),
    )
    gout, *kept = pl.pallas_call(
        main_kernel,
        out_shape=(shape((HID, ROWS, 128), BF16),) + mats,
        in_specs=[far, far, smem, smem, far, far, far, far, far, far],
        out_specs=[hbm] * 7,
        scratch_shapes=[
            *[pltpu.VMEM((8, REGION + 2 * PAD, 128), F32)] * 4,
            pltpu.VMEM((STEPS * ROWS, 8, 128), F32),
            pltpu.VMEM((GROUPS, 128, 128), F32),
            pltpu.VMEM((GROUPS, PAIRS, SNAPS, 256), BF16),
            pltpu.VMEM((PAIRS, DEVS, 256), BF16),
            pltpu.VMEM((4, 8, 128), F32),
            pltpu.VMEM((32, 16, 128), BF16),
            pltpu.VMEM((HID, ROWS, 128), BF16),
            pltpu.VMEM((PAIRS, HID, 256), BF16),
            pltpu.VMEM((PAIRS, HID, 256), F32),
            pltpu.VMEM((PAIRS, HID, 256), BF16),
            pltpu.VMEM((DEVS, 16, 128), F32),
            pltpu.VMEM((64, 16, 128), F32),
            pltpu.VMEM((CHIPS, 16, 128), F32),
            pltpu.VMEM((DEVS, 16, 128), BF16),
            pltpu.VMEM((HID, HID), F32), pltpu.VMEM((HID, HID), F32), pltpu.VMEM((DEVS, 16, 128), F32),
            pltpu.VMEM((HID, HID), BF16), pltpu.VMEM((HID, HID), BF16), pltpu.VMEM((HID, HID), BF16),
            pltpu.VMEM((FEAT, HID), BF16), pltpu.VMEM((HID, HID), BF16), pltpu.VMEM((HID, DEVS), BF16),
            pltpu.VMEM((FEAT, HID), BF16), pltpu.VMEM((HID, HID), BF16), pltpu.VMEM((HID, HID), BF16),
            pltpu.VMEM((1, ROWS, 1024), F32), pltpu.VMEM((1, ROWS, 1024), F32), pltpu.VMEM((1, HID), jnp.int32), pltpu.VMEM((4, FEAT), BF16),
            dma((4,)), dma((4,)), dma, dma, dma, dma, dma, dma((4,)),
            dma, dma, dma, dma, dma, dma, dma, dma,
            dma((3,)), dma((8,)), dma, dma((7,)), dma((4,)),
        ],
        compiler_params=pltpu.CompilerParams(
            collective_id=0, has_side_effects=True, vmem_limit_bytes=MAIN_VMEM
        ),
        name="solve_and_reduce",
    )(
        pin(initial), pin(conductivity), step_count, pin(emit_steps), pin(assign.reshape(1, HID)), pin(sample_inputs),
        pin(w_first), pin(w_second), pin(w_third), pin(w_out),
    )
    outs = pl.pallas_call(
        final_kernel,
        out_shape=(shape((FEAT, HID), F32), shape((HID, HID), F32), shape((HID, HID), F32), shape((HID, ROWS, 128), BF16)),
        in_specs=[hbm] + [vmem] * 6 + [far] * 2,
        out_specs=[hbm] * 4,
        scratch_shapes=[
            pltpu.VMEM((HID, HID), BF16), pltpu.VMEM((HID, HID), BF16),
            pltpu.VMEM((FEAT, HID), F32), pltpu.VMEM((HID, HID), F32), pltpu.VMEM((HID, HID), F32),
            dma((2,)), dma((4,)),
        ],
        name="outputs",
        compiler_params=pltpu.CompilerParams(vmem_limit_bytes=12 * 1024 * 1024),
    )(gout, *kept, pin(w_second), pin(w_third))
    return tuple(outs)


def solution(mesh):
    placed = (
        P("group", "strip", None), P("group", "strip", None), P("group"), P("group", None), P(),
        P(("group", "strip"), None), P(), P(), P(), P(None, "strip", "group"),
    )
    return jax.shard_map(
        per_device, mesh=mesh, in_specs=placed, out_specs=(P(), P(), P(), P(None, "strip", "group")), check_vma=False
    )
```

```python
import jax
import jax.numpy as jnp
from jax import lax
from jax.experimental import pallas as pl
from jax.experimental.pallas import tpu as pltpu
from jax.sharding import PartitionSpec as P

FLAT = pl.DeviceIdType.LOGICAL
F32, BF16 = jnp.float32, jnp.bfloat16
STEPS, SNAPS, ROWS, HID, FEAT = 32, 16, 32, 512, 128
GROUPS, STRIPS = 8, 16
DEVS, CHIPS = GROUPS * STRIPS, GROUPS * STRIPS // 2
REGION = 3 * ROWS
PAIRS = ROWS // 2
CHUNK = 4
PAD = 8
MAIN_VMEM = 42 * 1024 * 1024


def dot(a, b):
    return jnp.dot(a, b, preferred_element_type=F32)


def dot_nt(a, b):
    return lax.dot_general(a, b, (((1,), (1,)), ((), ())), preferred_element_type=F32)


def swap_matrix():
    row = lax.broadcasted_iota(jnp.int32, (256, 256), 0)
    col = lax.broadcasted_iota(jnp.int32, (256, 256), 1)
    return jnp.where((row % 16) * 16 + row // 16 == col, 1.0, 0.0).astype(BF16)


def main_kernel(
    initial_hbm, conductivity_hbm, step_count, emit_steps, assign_hbm, sample_hbm,
    w_first, w_second, w_third, w_out,
    gout, act_a, act_b, hat, hbt, xt, delta_out,
    state_a, state_b, kap, quarter, hist, tmp, send, snaps, part, gath,
    raw, w2, pred, resid, acc, pair_in, pieces, mine_bf, delta, act_c, hct, hidc, onehot,
    wf, ws, wt, initial, conductivity, assign, sample_inputs,
    halo_send, halo_recv, part_send, part_recv, gath_send, gath_recv, snap_send, snap_recv,
    pair_send, pair_recv, piece_send, piece_recv, delta_send, delta_recv, twin_send, twin_recv,
    w_sem, raw_sem, own_sem, in_sem,
):
    g, s = lax.axis_index("group"), lax.axis_index("strip")
    me = g * STRIPS + s
    core = s % 2
    chip = g * (STRIPS // 2) + s // 2
    twin = me + 1 - 2 * core
    quad = s % 4

    def wrap(i, n):
        return jnp.where(i >= n, i - n, i)

    def each_chip(fn):
        @pl.loop(0, 7)
        def _(i):
            for j in range(9):
                p = wrap(chip + 1 + i * 9 + j, CHIPS)
                fn(p, p * 2 + core)

    def remote(src, dst, send_sem, recv_sem, device):
        return pltpu.make_async_remote_copy(
            src_ref=src, dst_ref=dst, send_sem=send_sem, recv_sem=recv_sem, device_id=device, device_id_type=FLAT
        )

    inputs = [
        pltpu.make_async_copy(a, b, in_sem.at[i])
        for i, (a, b) in enumerate((
            (initial_hbm, initial), (conductivity_hbm, conductivity), (sample_hbm, sample_inputs), (assign_hbm, assign)
        ))
    ]
    for copy in inputs:
        copy.start()
    barrier = pltpu.get_barrier_semaphore()

    def greet(device):
        pl.semaphore_signal(barrier, inc=1, device_id=device, device_id_type=FLAT)

    greet(twin)
    greet(me + 3 - 2 * quad)
    next_quad = ((quad == 0) & (s > 0)) | ((quad == 3) & (s < STRIPS - 1))

    @pl.when(next_quad)
    def _():
        greet(jnp.where(quad == 0, me - 1, me + 1))

    each_chip(lambda p, device: greet(device))

    raw_copies = [
        pltpu.make_async_copy(w_out.at[pl.ds(64 * i, 64)], raw.at[pl.ds(64 * i, 64)], raw_sem.at[i]) for i in range(8)
    ]
    for copy in raw_copies:
        copy.start()
    weight_copies = [
        pltpu.make_async_copy(a, b, w_sem.at[i]) for i, (a, b) in enumerate(((w_first, wf), (w_second, ws), (w_third, wt)))
    ]
    for copy in weight_copies:
        copy.start()

    for copy in inputs:
        copy.wait()
    own_rows, rows_above, rows_below = pl.ds(PAD + ROWS, ROWS), pl.ds(PAD, ROWS), pl.ds(PAD + 2 * ROWS, ROWS)
    for j in range(8):
        state_a[j, own_rows, :] = initial[0, :, j * 128 : (j + 1) * 128]
        kap[j, own_rows, :] = 0.125 * conductivity[0, :, j * 128 : (j + 1) * 128]
        for ref in (state_a, state_b):
            ref[j, 0:PAD, :] = jnp.zeros((PAD, 128), F32)
            ref[j, PAD + REGION :, :] = jnp.zeros((PAD, 128), F32)
    part[quad, 0:4, :] = sample_inputs[...].astype(F32)
    ids = lax.broadcasted_iota(jnp.int32, (DEVS, HID), 0)
    onehot[...] = jnp.transpose(jnp.where(ids == assign[...], 1.0, 0.0)).astype(BF16)
    swap = swap_matrix()

    pl.semaphore_wait(barrier, CHIPS + 1 + jnp.where(next_quad, 1, 0))

    above, below = jnp.where(s > 0, me - 1, me), jnp.where(s < STRIPS - 1, me + 1, me)
    up_copies = [
        remote(ref.at[:, own_rows], ref.at[:, rows_below], halo_send.at[i], halo_recv.at[i], above)
        for i, ref in enumerate((state_a, kap))
    ]
    down_copies = [
        remote(ref.at[:, own_rows], ref.at[:, rows_above], halo_send.at[2 + i], halo_recv.at[2 + i], below)
        for i, ref in enumerate((state_a, kap))
    ]

    @pl.when(s > 0)
    def _():
        for copy in up_copies:
            copy.start()

    @pl.when(s < STRIPS - 1)
    def _():
        for copy in down_copies:
            copy.start()

    for i in range(1, 4):
        remote(part.at[quad], part.at[quad], part_send, part_recv, me - quad + wrap(quad + i, 4)).start()

    def relayout_weights(i, carry):
        for half in range(2):
            k0 = pl.multiple_of((i * 2 + half) * 16, 16)
            x = jnp.concatenate([raw[pl.ds(k0, 16), b * 16 : b * 16 + 16, :].reshape(256, 128) for b in range(2)], axis=1)
            y = dot(swap, x).astype(BF16)
            for b in range(2):
                for r in range(16):
                    row = b * 16 + r
                    w2[row // 2, pl.ds(k0, 16), (row % 2) * 128 : (row % 2) * 128 + 128] = y[
                        r * 16 : r * 16 + 16, b * 128 : b * 128 + 128
                    ]
        return carry

    for i, copy in enumerate(raw_copies):
        copy.wait()
    lax.fori_loop(0, 16, relayout_weights, 0)

    remote(part.at[pl.ds(0, 3)], part.at[pl.ds(0, 3)], part_send, part_recv, twin).wait()
    low = lax.broadcasted_iota(jnp.int32, (8, 128), 0) < 4
    tile = jnp.concatenate(
        [jnp.where(low, part[2 * i], pltpu.roll(part[2 * i + 1], 4, axis=0)) for i in range(2)], axis=0
    )
    mine = g * 4 + s // 4
    gath[mine] = tile.astype(BF16)

    for i in range(1, 32):
        remote(gath.at[mine], gath.at[mine], gath_send, gath_recv, wrap(mine + i, 32) * 4 + quad).start()

    def land(has, copies_in, copies_out, rows):
        @pl.when(has)
        def _():
            for copy in copies_in:
                copy.wait_recv()
            for copy in copies_out:
                copy.wait_send()

        @pl.when(jnp.logical_not(has))
        def _():
            zero = jnp.zeros((8, ROWS, 128), F32)
            state_a[:, rows] = zero
            kap[:, rows] = zero

    land(s > 0, down_copies, up_copies, rows_above)
    land(s < STRIPS - 1, up_copies, down_copies, rows_below)

    @pl.loop(0, 8)
    def _(j):
        quarter[j] = 0.25 * kap[j]

    lane = lax.broadcasted_iota(jnp.int32, (8, 128), 1)
    first_lane, last_lane = lane == 0, lane == 127
    zero_tile = jnp.zeros((8, 128), F32)

    def step(src, dst, first, last, t):
        for tile in range(first, last):
            r = PAD + tile * 8
            here = [src[j, r : r + 8, :] for j in range(8)]
            to_east = [zero_tile] + [pltpu.roll(x, 1, axis=1) for x in here]
            to_west = [pltpu.roll(x, 127, axis=1) for x in here] + [zero_tile]
            for j in range(8):
                w = jnp.where(first_lane, to_east[j], to_east[j + 1])
                e = jnp.where(last_lane, to_west[j + 1], to_west[j])
                beside = (src[j, r - 1 : r + 7, :] + src[j, r + 1 : r + 9, :]) + (e + w)
                rate = kap[j, r : r + 8, :] + quarter[j, r : r + 8, :] * jnp.tanh(here[j])
                new = here[j] + rate * (beside - 4.0 * here[j])
                dst[j, r : r + 8, :] = new
                if ROWS // 8 <= tile < 2 * ROWS // 8:
                    hist[t * 32 + (j * 4 + tile - ROWS // 8)] = new

    for phase in range(4):

        @pl.loop(4 * phase, 4 * phase + 4)
        def _(i):
            step(state_a, state_b, phase, REGION // 8 - phase, 2 * i)
            step(state_b, state_a, phase, REGION // 8 - phase, 2 * i + 1)

    count = step_count[0]
    bases = [jnp.maximum(jnp.minimum(emit_steps[0, k], count) - 1, 0) * 32 for k in range(SNAPS)]

    def pack(c):
        @pl.loop(0, 4)
        def _(i):
            for half in range(2):
                to = i * 2 + half
                for k in range(SNAPS):
                    tmp[to, pl.ds(k, 8, stride=16), :] = hist[bases[k] + (to * 4 + c)]
                for j in range(8):
                    send[to, c * CHUNK + j // 2, :, (j % 2) * 128 : (j % 2) * 128 + 128] = tmp[
                        to, j * 16 : j * 16 + 16, :
                    ].astype(BF16)

    def snap_copy(c, to):
        rows = pl.ds(c * CHUNK, CHUNK)
        return remote(
            send.at[to, rows],
            snaps.at[rows, pl.ds(pl.multiple_of(g * SNAPS, SNAPS), SNAPS), :],
            snap_send,
            snap_recv.at[c],
            to * STRIPS + s,
        )

    for c in range(PAIRS // CHUNK):
        pack(c)
        for i in range(1, GROUPS):
            snap_copy(c, wrap(g + i, GROUPS)).start()

    own = pltpu.make_async_copy(
        send.at[g], snaps.at[:, pl.ds(pl.multiple_of(g * SNAPS, SNAPS), SNAPS), :], own_sem
    )
    own.start()

    for copy in weight_copies:
        copy.wait()
    remote(gath.at[pl.ds(0, 31)], gath.at[pl.ds(0, 31)], gath_send, gath_recv, twin).wait()

    @pl.loop(0, 4)
    def _(m):
        rows = pl.ds(pl.multiple_of(m * 128, 128), 128)
        x = gath[pl.ds(m * 8, 8)].reshape(128, FEAT)
        xt[:, rows] = jnp.transpose(x.astype(F32)).astype(BF16)
        a = jnp.tanh(dot(x, wf[...]))
        act_a[rows, :] = a
        hat[:, rows] = jnp.transpose(a).astype(BF16)
        b = jnp.tanh(dot(a.astype(BF16), ws[...]))
        act_b[rows, :] = b
        hbt[:, rows] = jnp.transpose(b).astype(BF16)
        c = jnp.tanh(dot(b.astype(BF16), wt[...]))
        hct[:, rows] = jnp.transpose(c).astype(BF16)
        hidc[rows, :] = c.astype(BF16)
        for kb in range(4):
            act_c[pl.ds(kb * 32 + m * 8, 8)] = c[:, kb * 128 : kb * 128 + 128].reshape(8, 16, 128)

    @pl.loop(0, PAIRS)
    def _(rp):
        pred[rp] = dot(hidc[...], w2[rp])

    own.wait()
    inverse_root = F32(1.0) / jnp.sqrt(F32(HID))

    def residual_chunk(c):
        remote(snaps.at[pl.ds(0, CHUNK), pl.ds(0, 112), :], snaps.at[pl.ds(0, CHUNK), pl.ds(0, 112), :],
               snap_send, snap_recv.at[c], twin).wait_recv()

        @pl.loop(0, CHUNK // 2)
        def _(i):
            for half in range(2):
                rp = c * CHUNK + 2 * i + half
                resid[rp] = ((pred[rp] - dot(onehot[...], snaps[rp])) * inverse_root).astype(BF16)

    def back_half(c, half, fresh):
        left = jnp.concatenate([resid[c * CHUNK + i] for i in range(CHUNK)], axis=1)
        k0 = pl.multiple_of(half * 256, 256)
        right = jnp.concatenate([w2[c * CHUNK + i, pl.ds(k0, 256), :] for i in range(CHUNK)], axis=1)
        value = dot_nt(left, right)
        for kb in range(2):
            at = pl.ds(half * 64 + kb * 32, 32)
            v = value[:, kb * 128 : kb * 128 + 128].reshape(32, 16, 128)
            acc[at] = v if fresh else acc[at] + v

    residual_chunk(0)
    back_half(0, 1 - core, True)

    @pl.loop(1, PAIRS // CHUNK)
    def _(c):
        residual_chunk(c)
        back_half(c, 1 - core, False)

    theirs = pl.ds((1 - core) * 64, 64)
    to_twin = remote(acc.at[theirs], pair_in, pair_send, pair_recv, twin)
    to_twin.start()
    back_half(0, core, True)

    @pl.loop(1, PAIRS // CHUNK)
    def _(c):
        back_half(c, core, False)

    to_twin.wait_recv()

    @pl.loop(0, 8)
    def _(i):
        at = pl.ds(i * 8, 8)
        mine_bf[at] = (acc[pl.ds(core * 64 + i * 8, 8)] + pair_in[at]).astype(BF16)

    each_chip(
        lambda p, device: remote(mine_bf.at[p], pieces.at[chip], piece_send, piece_recv, device).start()
    )

    pieces[chip] = mine_bf[chip]

    @pl.loop(0, PAIRS)
    def _(rp):
        w2[rp] = dot(hct[...], resid[rp]).astype(BF16)

    remote(pieces.at[pl.ds(0, 63)], pieces.at[pl.ds(0, 63)], piece_send, piece_recv, twin).wait_recv()
    total = pieces[0].astype(F32)
    for i in range(1, CHIPS):
        total = total + pieces[i].astype(F32)
    a = act_c[core * 64 + chip]
    delta[core * 64 + chip] = (total * (1.0 - a * a)).astype(BF16)

    at = core * 64 + chip
    each_chip(lambda p, device: remote(delta.at[at], delta.at[at], delta_send, delta_recv, device).start())

    def relayout_grad(i, carry):
        for half in range(2):
            k0 = pl.multiple_of((i * 2 + half) * 16, 16)
            x = jnp.concatenate(
                [
                    jnp.concatenate(
                        [w2[b * 8 + r // 2, pl.ds(k0, 16), (r % 2) * 128 : (r % 2) * 128 + 128] for r in range(16)], axis=0
                    )
                    for b in range(2)
                ],
                axis=1,
            )
            y = dot(swap, x).astype(BF16)
            for b in range(2):
                gout[pl.ds(k0, 16), b * 16 : b * 16 + 16, :] = y[:, b * 128 : b * 128 + 128].reshape(16, 16, 128)
        return carry

    lax.fori_loop(0, 16, relayout_grad, 0)

    remote(delta.at[pl.ds(0, 63)], delta.at[pl.ds(0, 63)], delta_send, delta_recv, twin).wait_recv()
    ours = pl.ds(core * 64, 64)
    to_twin2 = remote(delta.at[ours], delta.at[ours], twin_send, twin_recv, twin)
    to_twin2.start()
    to_twin2.wait_recv()
    delta_out[...] = delta[...]

    remote(send.at[pl.ds(0, 7)], send.at[pl.ds(0, 7)], snap_send, snap_recv.at[0], twin).wait_send()
    to_twin.wait_send()
    remote(pieces.at[pl.ds(0, 63)], pieces.at[pl.ds(0, 63)], piece_send, piece_recv, twin).wait_send()
    remote(delta.at[pl.ds(0, 63)], delta.at[pl.ds(0, 63)], delta_send, delta_recv, twin).wait_send()
    to_twin2.wait_send()


def final_kernel(
    gout_in, act_a, act_b, hat, hbt, xt, delta, ws_in, wt_in, g1_out, g2_out, g3_out, gout_out, ws, wt, g1, g2, g3, in_sem, out_sem
):
    loads = [pltpu.make_async_copy(a, b, in_sem.at[i]) for i, (a, b) in enumerate(((wt_in, wt), (ws_in, ws)))]
    for copy in loads:
        copy.start()
    to_gout = pltpu.make_async_copy(gout_in, gout_out, out_sem.at[3])
    to_gout.start()
    dc = jnp.concatenate([delta[i * 32 : i * 32 + 32].reshape(HID, 128) for i in range(4)], axis=1)
    g3[...] = dot(hbt[...], dc)
    to_g3 = pltpu.make_async_copy(g3, g3_out, out_sem.at[0])
    to_g3.start()
    loads[0].wait()
    db = (dot_nt(dc, wt[...]) * (1.0 - act_b[...] * act_b[...])).astype(BF16)
    g2[...] = dot(hat[...], db)
    to_g2 = pltpu.make_async_copy(g2, g2_out, out_sem.at[1])
    to_g2.start()
    loads[1].wait()
    da = (dot_nt(db, ws[...]) * (1.0 - act_a[...] * act_a[...])).astype(BF16)
    g1[...] = dot(xt[...], da)
    to_g1 = pltpu.make_async_copy(g1, g1_out, out_sem.at[2])
    to_g1.start()
    for copy in (to_gout, to_g3, to_g2, to_g1):
        copy.wait()


def per_device(initial, conductivity, step_count, emit_steps, assign, sample_inputs, w_first, w_second, w_third, w_out):
    vmem, smem = pl.BlockSpec(memory_space=pltpu.VMEM), pl.BlockSpec(memory_space=pltpu.SMEM)
    hbm = pl.BlockSpec(memory_space=pl.ANY)
    far = pl.BlockSpec(memory_space=pltpu.HBM)
    shape = jax.ShapeDtypeStruct
    dma = pltpu.SemaphoreType.DMA
    pin = lambda x: pltpu.with_memory_space_constraint(x, pltpu.HBM)
    mats = (
        shape((HID, HID), F32), shape((HID, HID), F32), shape((HID, HID), BF16), shape((HID, HID), BF16),
        shape((FEAT, HID), BF16), shape((DEVS, 16, 128), BF16),
    )
    gout, *kept = pl.pallas_call(
        main_kernel,
        out_shape=(shape((HID, ROWS, 128), BF16),) + mats,
        in_specs=[far, far, smem, smem, far, far, far, far, far, far],
        out_specs=[vmem] * 7,
        scratch_shapes=[
            *[pltpu.VMEM((8, REGION + 2 * PAD, 128), F32)] * 4,
            pltpu.VMEM((STEPS * ROWS, 8, 128), F32),
            pltpu.VMEM((GROUPS, 128, 128), F32),
            pltpu.VMEM((GROUPS, PAIRS, SNAPS, 256), BF16),
            pltpu.VMEM((PAIRS, DEVS, 256), BF16),
            pltpu.VMEM((4, 8, 128), F32),
            pltpu.VMEM((32, 16, 128), BF16),
            pltpu.VMEM((HID, ROWS, 128), BF16),
            pltpu.VMEM((PAIRS, HID, 256), BF16),
            pltpu.VMEM((PAIRS, HID, 256), F32),
            pltpu.VMEM((PAIRS, HID, 256), BF16),
            pltpu.VMEM((DEVS, 16, 128), F32),
            pltpu.VMEM((64, 16, 128), F32),
            pltpu.VMEM((CHIPS, 16, 128), BF16), pltpu.VMEM((CHIPS, 16, 128), BF16),
            pltpu.VMEM((DEVS, 16, 128), BF16),
            pltpu.VMEM((DEVS, 16, 128), F32), pltpu.VMEM((HID, HID), BF16),
            pltpu.VMEM((HID, HID), BF16), pltpu.VMEM((HID, DEVS), BF16),
            pltpu.VMEM((FEAT, HID), BF16), pltpu.VMEM((HID, HID), BF16), pltpu.VMEM((HID, HID), BF16),
            pltpu.VMEM((1, ROWS, 1024), F32), pltpu.VMEM((1, ROWS, 1024), F32), pltpu.VMEM((1, HID), jnp.int32), pltpu.VMEM((4, FEAT), BF16),
            dma((4,)), dma((4,)), dma, dma, dma, dma, dma, dma((4,)),
            dma, dma, dma, dma, dma, dma, dma, dma,
            dma((3,)), dma((8,)), dma, dma((4,)),
        ],
        compiler_params=pltpu.CompilerParams(
            collective_id=0, has_side_effects=True, vmem_limit_bytes=MAIN_VMEM
        ),
        name="solve_and_reduce",
    )(
        pin(initial), pin(conductivity), step_count, pin(emit_steps), pin(assign.reshape(1, HID)), pin(sample_inputs),
        pin(w_first), pin(w_second), pin(w_third), pin(w_out),
    )
    outs = pl.pallas_call(
        final_kernel,
        out_shape=(shape((FEAT, HID), F32), shape((HID, HID), F32), shape((HID, HID), F32), shape((HID, ROWS, 128), BF16)),
        in_specs=[hbm] + [vmem] * 6 + [far] * 2,
        out_specs=[hbm] * 4,
        scratch_shapes=[
            pltpu.VMEM((HID, HID), BF16), pltpu.VMEM((HID, HID), BF16),
            pltpu.VMEM((FEAT, HID), F32), pltpu.VMEM((HID, HID), F32), pltpu.VMEM((HID, HID), F32),
            dma((2,)), dma((4,)),
        ],
        name="outputs",
        compiler_params=pltpu.CompilerParams(vmem_limit_bytes=12 * 1024 * 1024),
    )(gout, *kept, pin(w_second), pin(w_third))
    return tuple(outs)


def solution(mesh):
    placed = (
        P("group", "strip", None), P("group", "strip", None), P("group"), P("group", None), P(),
        P(("group", "strip"), None), P(), P(), P(), P(None, "strip", "group"),
    )
    return jax.shard_map(
        per_device, mesh=mesh, in_specs=placed, out_specs=(P(), P(), P(), P(None, "strip", "group")), check_vma=False
    )
```

```python
import jax
import jax.numpy as jnp
from jax import lax
from jax.experimental import pallas as pl
from jax.experimental.pallas import tpu as pltpu
from jax.sharding import PartitionSpec as P

FLAT = pl.DeviceIdType.LOGICAL
F32, BF16 = jnp.float32, jnp.bfloat16
STEPS, SNAPS, ROWS, HID, FEAT = 32, 16, 32, 512, 128
GROUPS, STRIPS = 8, 16
DEVS, CHIPS = GROUPS * STRIPS, GROUPS * STRIPS // 2
REGION = 3 * ROWS
PAIRS = ROWS // 2
CHUNK = 4
PAD = 8
MAIN_VMEM = 42 * 1024 * 1024


def dot(a, b):
    return jnp.dot(a, b, preferred_element_type=F32)


def dot_nt(a, b):
    return lax.dot_general(a, b, (((1,), (1,)), ((), ())), preferred_element_type=F32)


def swap_matrix():
    row = lax.broadcasted_iota(jnp.int32, (256, 256), 0)
    col = lax.broadcasted_iota(jnp.int32, (256, 256), 1)
    return jnp.where((row % 16) * 16 + row // 16 == col, 1.0, 0.0).astype(BF16)


def main_kernel(
    initial_hbm, conductivity_hbm, step_count, emit_steps, assign_hbm, sample_hbm,
    w_first, w_second, w_third, w_out,
    gout, act_a, act_b, hat, hbt, xt, delta_out,
    state_a, state_b, kap, quarter, hist, tmp, send, snaps, part, gath,
    raw, w2, pred, resid, acc, pair_in, pieces, mine_bf, delta, act_c, hct, hidc, onehot,
    wf, ws, wt, initial, conductivity, assign, sample_inputs,
    halo_send, halo_recv, part_send, part_recv, gath_send, gath_recv, snap_send, snap_recv,
    pair_send, pair_recv, piece_send, piece_recv, delta_send, delta_recv, twin_send, twin_recv,
    w_sem, raw_sem, own_sem, in_sem,
):
    g, s = lax.axis_index("group"), lax.axis_index("strip")
    me = g * STRIPS + s
    core = s % 2
    chip = g * (STRIPS // 2) + s // 2
    twin = me + 1 - 2 * core
    quad = s % 4

    def wrap(i, n):
        return jnp.where(i >= n, i - n, i)

    def each_chip(fn):
        @pl.loop(0, 7)
        def _(i):
            for j in range(9):
                p = wrap(chip + 1 + i * 9 + j, CHIPS)
                fn(p, p * 2 + core)

    def remote(src, dst, send_sem, recv_sem, device):
        return pltpu.make_async_remote_copy(
            src_ref=src, dst_ref=dst, send_sem=send_sem, recv_sem=recv_sem, device_id=device, device_id_type=FLAT
        )

    inputs = [
        pltpu.make_async_copy(a, b, in_sem.at[i])
        for i, (a, b) in enumerate((
            (initial_hbm, initial), (conductivity_hbm, conductivity), (sample_hbm, sample_inputs), (assign_hbm, assign)
        ))
    ]
    for copy in inputs:
        copy.start()
    barrier = pltpu.get_barrier_semaphore()

    z, x_lo, x_hi, y = (s // 2) % 4, s // 8, g % 2, g // 2
    doubling = [
        me + 2 * (3 - 2 * z),
        me + 8 * (1 - 2 * x_lo),
        me + 16 * (1 - 2 * x_hi) + 8 * (1 - 2 * x_lo),
        me + 32 * (1 - 2 * (y % 2)),
        me + 32 * (3 - 2 * y),
    ]

    def greet(device):
        pl.semaphore_signal(barrier, inc=1, device_id=device, device_id_type=FLAT)

    greet(twin)
    greet(me + 3 - 2 * quad)
    greet(me + 2 - 4 * (quad // 2))
    for device in doubling:
        greet(device)
    next_quad = ((quad == 0) & (s > 0)) | ((quad == 3) & (s < STRIPS - 1))

    @pl.when(next_quad)
    def _():
        greet(jnp.where(quad == 0, me - 1, me + 1))

    raw_copies = [
        pltpu.make_async_copy(w_out.at[pl.ds(64 * i, 64)], raw.at[pl.ds(64 * i, 64)], raw_sem.at[i]) for i in range(8)
    ]
    for copy in raw_copies:
        copy.start()
    weight_copies = [
        pltpu.make_async_copy(a, b, w_sem.at[i]) for i, (a, b) in enumerate(((w_first, wf), (w_second, ws), (w_third, wt)))
    ]
    for copy in weight_copies:
        copy.start()

    for copy in inputs:
        copy.wait()
    own_rows, rows_above, rows_below = pl.ds(PAD + ROWS, ROWS), pl.ds(PAD, ROWS), pl.ds(PAD + 2 * ROWS, ROWS)
    for j in range(8):
        state_a[j, own_rows, :] = initial[0, :, j * 128 : (j + 1) * 128]
        kap[j, own_rows, :] = 0.125 * conductivity[0, :, j * 128 : (j + 1) * 128]
        for ref in (state_a, state_b):
            ref[j, 0:PAD, :] = jnp.zeros((PAD, 128), F32)
            ref[j, PAD + REGION :, :] = jnp.zeros((PAD, 128), F32)
    part[quad, 0:4, :] = sample_inputs[...].astype(F32)
    ids = lax.broadcasted_iota(jnp.int32, (DEVS, HID), 0)
    onehot[...] = jnp.transpose(jnp.where(ids == assign[...], 1.0, 0.0)).astype(BF16)
    swap = swap_matrix()

    pl.semaphore_wait(barrier, 8 + jnp.where(next_quad, 1, 0))

    above, below = jnp.where(s > 0, me - 1, me), jnp.where(s < STRIPS - 1, me + 1, me)
    up_copies = [
        remote(ref.at[:, own_rows], ref.at[:, rows_below], halo_send.at[i], halo_recv.at[i], above)
        for i, ref in enumerate((state_a, kap))
    ]
    down_copies = [
        remote(ref.at[:, own_rows], ref.at[:, rows_above], halo_send.at[2 + i], halo_recv.at[2 + i], below)
        for i, ref in enumerate((state_a, kap))
    ]

    @pl.when(s > 0)
    def _():
        for copy in up_copies:
            copy.start()

    @pl.when(s < STRIPS - 1)
    def _():
        for copy in down_copies:
            copy.start()

    for i in range(1, 4):
        remote(part.at[quad], part.at[quad], part_send, part_recv, me - quad + wrap(quad + i, 4)).start()

    def relayout_weights(i, carry):
        for half in range(2):
            k0 = pl.multiple_of((i * 2 + half) * 16, 16)
            x = jnp.concatenate([raw[pl.ds(k0, 16), b * 16 : b * 16 + 16, :].reshape(256, 128) for b in range(2)], axis=1)
            y = dot(swap, x).astype(BF16)
            for b in range(2):
                for r in range(16):
                    row = b * 16 + r
                    w2[row // 2, pl.ds(k0, 16), (row % 2) * 128 : (row % 2) * 128 + 128] = y[
                        r * 16 : r * 16 + 16, b * 128 : b * 128 + 128
                    ]
        return carry

    for i, copy in enumerate(raw_copies):
        copy.wait()
    lax.fori_loop(0, 8, relayout_weights, 0)
    remote(part.at[pl.ds(0, 3)], part.at[pl.ds(0, 3)], part_send, part_recv, twin).wait()
    low = lax.broadcasted_iota(jnp.int32, (8, 128), 0) < 4
    tile = jnp.concatenate(
        [jnp.where(low, part[2 * i], pltpu.roll(part[2 * i + 1], 4, axis=0)) for i in range(2)], axis=0
    )
    mine = g * 4 + s // 4
    gath[mine] = tile.astype(BF16)


    def tiles(stage):
        held = pl.ds(mine // 2**stage * 2**stage, 2**stage)
        return remote(gath.at[held], gath.at[held], gath_send.at[stage], gath_recv.at[stage], doubling[stage])

    tiles(0).start()
    lax.fori_loop(8, 16, relayout_weights, 0)
    tiles(0).wait()
    tiles(1).start()

    def land(has, copies_in, copies_out, rows):
        @pl.when(has)
        def _():
            for copy in copies_in:
                copy.wait_recv()
            for copy in copies_out:
                copy.wait_send()

        @pl.when(jnp.logical_not(has))
        def _():
            zero = jnp.zeros((8, ROWS, 128), F32)
            state_a[:, rows] = zero
            kap[:, rows] = zero

    land(s > 0, down_copies, up_copies, rows_above)
    land(s < STRIPS - 1, up_copies, down_copies, rows_below)

    @pl.loop(0, 8)
    def _(j):
        quarter[j] = 0.25 * kap[j]

    lane = lax.broadcasted_iota(jnp.int32, (8, 128), 1)
    first_lane, last_lane = lane == 0, lane == 127
    zero_tile = jnp.zeros((8, 128), F32)

    def step(src, dst, first, last, t):
        for tile in range(first, last):
            r = PAD + tile * 8
            here = [src[j, r : r + 8, :] for j in range(8)]
            to_east = [zero_tile] + [pltpu.roll(x, 1, axis=1) for x in here]
            to_west = [pltpu.roll(x, 127, axis=1) for x in here] + [zero_tile]
            for j in range(8):
                w = jnp.where(first_lane, to_east[j], to_east[j + 1])
                e = jnp.where(last_lane, to_west[j + 1], to_west[j])
                beside = (src[j, r - 1 : r + 7, :] + src[j, r + 1 : r + 9, :]) + (e + w)
                rate = kap[j, r : r + 8, :] + quarter[j, r : r + 8, :] * jnp.tanh(here[j])
                new = here[j] + rate * (beside - 4.0 * here[j])
                dst[j, r : r + 8, :] = new
                if ROWS // 8 <= tile < 2 * ROWS // 8:
                    hist[t * 32 + (j * 4 + tile - ROWS // 8)] = new

    for phase in range(4):

        @pl.loop(4 * phase, 4 * phase + 4)
        def _(i):
            step(state_a, state_b, phase, REGION // 8 - phase, 2 * i)
            step(state_b, state_a, phase, REGION // 8 - phase, 2 * i + 1)

        tiles(phase + 1).wait()
        if phase < 3:
            tiles(phase + 2).start()

    count = step_count[0]
    bases = [jnp.maximum(jnp.minimum(emit_steps[0, k], count) - 1, 0) * 32 for k in range(SNAPS)]

    def pack(c):
        @pl.loop(0, 4)
        def _(i):
            for half in range(2):
                to = i * 2 + half
                for k in range(SNAPS):
                    tmp[to, pl.ds(k, 8, stride=16), :] = hist[bases[k] + (to * 4 + c)]
                for j in range(8):
                    send[to, c * CHUNK + j // 2, :, (j % 2) * 128 : (j % 2) * 128 + 128] = tmp[
                        to, j * 16 : j * 16 + 16, :
                    ].astype(BF16)

    def snap_copy(c, to):
        rows = pl.ds(c * CHUNK, CHUNK)
        return remote(
            send.at[to, rows],
            snaps.at[rows, pl.ds(pl.multiple_of(g * SNAPS, SNAPS), SNAPS), :],
            snap_send,
            snap_recv.at[c],
            to * STRIPS + s,
        )

    for c in range(PAIRS // CHUNK):
        pack(c)
        for i in range(1, GROUPS):
            snap_copy(c, wrap(g + i, GROUPS)).start()

    own = pltpu.make_async_copy(
        send.at[g], snaps.at[:, pl.ds(pl.multiple_of(g * SNAPS, SNAPS), SNAPS), :], own_sem
    )
    own.start()

    for copy in weight_copies:
        copy.wait()

    @pl.loop(0, 4)
    def _(m):
        rows = pl.ds(pl.multiple_of(m * 128, 128), 128)
        x = gath[pl.ds(m * 8, 8)].reshape(128, FEAT)
        xt[:, rows] = jnp.transpose(x.astype(F32)).astype(BF16)
        a = jnp.tanh(dot(x, wf[...]))
        act_a[rows, :] = a
        hat[:, rows] = jnp.transpose(a).astype(BF16)
        b = jnp.tanh(dot(a.astype(BF16), ws[...]))
        act_b[rows, :] = b
        hbt[:, rows] = jnp.transpose(b).astype(BF16)
        c = jnp.tanh(dot(b.astype(BF16), wt[...]))
        hct[:, rows] = jnp.transpose(c).astype(BF16)
        hidc[rows, :] = c.astype(BF16)
        for kb in range(4):
            act_c[pl.ds(kb * 32 + m * 8, 8)] = c[:, kb * 128 : kb * 128 + 128].reshape(8, 16, 128)

    @pl.loop(0, PAIRS)
    def _(rp):
        pred[rp] = dot(hidc[...], w2[rp])

    own.wait()
    inverse_root = F32(1.0) / jnp.sqrt(F32(HID))

    def residual_chunk(c):
        remote(snaps.at[pl.ds(0, CHUNK), pl.ds(0, 112), :], snaps.at[pl.ds(0, CHUNK), pl.ds(0, 112), :],
               snap_send, snap_recv.at[c], twin).wait_recv()

        @pl.loop(0, CHUNK // 2)
        def _(i):
            for half in range(2):
                rp = c * CHUNK + 2 * i + half
                resid[rp] = ((pred[rp] - dot(onehot[...], snaps[rp])) * inverse_root).astype(BF16)

    def back_half(c, half, fresh):
        left = jnp.concatenate([resid[c * CHUNK + i] for i in range(CHUNK)], axis=1)
        k0 = pl.multiple_of(half * 256, 256)
        right = jnp.concatenate([w2[c * CHUNK + i, pl.ds(k0, 256), :] for i in range(CHUNK)], axis=1)
        value = dot_nt(left, right)
        for kb in range(2):
            at = pl.ds(half * 64 + kb * 32, 32)
            v = value[:, kb * 128 : kb * 128 + 128].reshape(32, 16, 128)
            acc[at] = v if fresh else acc[at] + v

    residual_chunk(0)
    back_half(0, 1 - core, True)

    @pl.loop(1, PAIRS // CHUNK)
    def _(c):
        residual_chunk(c)
        back_half(c, 1 - core, False)

    theirs = pl.ds((1 - core) * 64, 64)
    to_twin = remote(acc.at[theirs], pair_in, pair_send, pair_recv, twin)
    to_twin.start()
    back_half(0, core, True)

    @pl.loop(1, PAIRS // CHUNK)
    def _(c):
        back_half(c, core, False)

    to_twin.wait_recv()

    @pl.loop(0, 8)
    def _(i):
        at = pl.ds(i * 8, 8)
        mine_bf[at] = (acc[pl.ds(core * 64 + i * 8, 8)] + pair_in[at]).astype(BF16)

    each_chip(
        lambda p, device: remote(mine_bf.at[p], pieces.at[chip], piece_send, piece_recv, device).start()
    )

    pieces[chip] = mine_bf[chip]

    @pl.loop(0, PAIRS)
    def _(rp):
        w2[rp] = dot(hct[...], resid[rp]).astype(BF16)

    remote(pieces.at[pl.ds(0, 63)], pieces.at[pl.ds(0, 63)], piece_send, piece_recv, twin).wait_recv()
    total = pieces[0].astype(F32)
    for i in range(1, CHIPS):
        total = total + pieces[i].astype(F32)
    a = act_c[core * 64 + chip]
    delta[core * 64 + chip] = (total * (1.0 - a * a)).astype(BF16)

    at = core * 64 + chip
    each_chip(lambda p, device: remote(delta.at[at], delta.at[at], delta_send, delta_recv, device).start())

    def relayout_grad(i, carry):
        for half in range(2):
            k0 = pl.multiple_of((i * 2 + half) * 16, 16)
            x = jnp.concatenate(
                [
                    jnp.concatenate(
                        [w2[b * 8 + r // 2, pl.ds(k0, 16), (r % 2) * 128 : (r % 2) * 128 + 128] for r in range(16)], axis=0
                    )
                    for b in range(2)
                ],
                axis=1,
            )
            y = dot(swap, x).astype(BF16)
            for b in range(2):
                gout[pl.ds(k0, 16), b * 16 : b * 16 + 16, :] = y[:, b * 128 : b * 128 + 128].reshape(16, 16, 128)
        return carry

    lax.fori_loop(0, 16, relayout_grad, 0)

    remote(delta.at[pl.ds(0, 63)], delta.at[pl.ds(0, 63)], delta_send, delta_recv, twin).wait_recv()
    ours = pl.ds(core * 64, 64)
    to_twin2 = remote(delta.at[ours], delta.at[ours], twin_send, twin_recv, twin)
    to_twin2.start()
    to_twin2.wait_recv()
    delta_out[...] = delta[...]

    remote(send.at[pl.ds(0, 7)], send.at[pl.ds(0, 7)], snap_send, snap_recv.at[0], twin).wait_send()
    to_twin.wait_send()
    remote(pieces.at[pl.ds(0, 63)], pieces.at[pl.ds(0, 63)], piece_send, piece_recv, twin).wait_send()
    remote(delta.at[pl.ds(0, 63)], delta.at[pl.ds(0, 63)], delta_send, delta_recv, twin).wait_send()
    to_twin2.wait_send()


def final_kernel(
    gout_in, act_a, act_b, hat, hbt, xt, delta, ws_in, wt_in, g1_out, g2_out, g3_out, gout_out, ws, wt, g1, g2, g3, in_sem, out_sem
):
    loads = [pltpu.make_async_copy(a, b, in_sem.at[i]) for i, (a, b) in enumerate(((wt_in, wt), (ws_in, ws)))]
    for copy in loads:
        copy.start()
    to_gout = pltpu.make_async_copy(gout_in, gout_out, out_sem.at[3])
    to_gout.start()
    dc = jnp.concatenate([delta[i * 32 : i * 32 + 32].reshape(HID, 128) for i in range(4)], axis=1)
    g3[...] = dot(hbt[...], dc)
    to_g3 = pltpu.make_async_copy(g3, g3_out, out_sem.at[0])
    to_g3.start()
    loads[0].wait()
    db = (dot_nt(dc, wt[...]) * (1.0 - act_b[...] * act_b[...])).astype(BF16)
    g2[...] = dot(hat[...], db)
    to_g2 = pltpu.make_async_copy(g2, g2_out, out_sem.at[1])
    to_g2.start()
    loads[1].wait()
    da = (dot_nt(db, ws[...]) * (1.0 - act_a[...] * act_a[...])).astype(BF16)
    g1[...] = dot(xt[...], da)
    to_g1 = pltpu.make_async_copy(g1, g1_out, out_sem.at[2])
    to_g1.start()
    for copy in (to_gout, to_g3, to_g2, to_g1):
        copy.wait()


def per_device(initial, conductivity, step_count, emit_steps, assign, sample_inputs, w_first, w_second, w_third, w_out):
    vmem, smem = pl.BlockSpec(memory_space=pltpu.VMEM), pl.BlockSpec(memory_space=pltpu.SMEM)
    hbm = pl.BlockSpec(memory_space=pl.ANY)
    far = pl.BlockSpec(memory_space=pltpu.HBM)
    shape = jax.ShapeDtypeStruct
    dma = pltpu.SemaphoreType.DMA
    pin = lambda x: pltpu.with_memory_space_constraint(x, pltpu.HBM)
    mats = (
        shape((HID, HID), F32), shape((HID, HID), F32), shape((HID, HID), BF16), shape((HID, HID), BF16),
        shape((FEAT, HID), BF16), shape((DEVS, 16, 128), BF16),
    )
    gout, *kept = pl.pallas_call(
        main_kernel,
        out_shape=(shape((HID, ROWS, 128), BF16),) + mats,
        in_specs=[far, far, smem, smem, far, far, far, far, far, far],
        out_specs=[vmem] * 7,
        scratch_shapes=[
            *[pltpu.VMEM((8, REGION + 2 * PAD, 128), F32)] * 4,
            pltpu.VMEM((STEPS * ROWS, 8, 128), F32),
            pltpu.VMEM((GROUPS, 128, 128), F32),
            pltpu.VMEM((GROUPS, PAIRS, SNAPS, 256), BF16),
            pltpu.VMEM((PAIRS, DEVS, 256), BF16),
            pltpu.VMEM((4, 8, 128), F32),
            pltpu.VMEM((32, 16, 128), BF16),
            pltpu.VMEM((HID, ROWS, 128), BF16),
            pltpu.VMEM((PAIRS, HID, 256), BF16),
            pltpu.VMEM((PAIRS, HID, 256), F32),
            pltpu.VMEM((PAIRS, HID, 256), BF16),
            pltpu.VMEM((DEVS, 16, 128), F32),
            pltpu.VMEM((64, 16, 128), F32),
            pltpu.VMEM((CHIPS, 16, 128), BF16), pltpu.VMEM((CHIPS, 16, 128), BF16),
            pltpu.VMEM((DEVS, 16, 128), BF16),
            pltpu.VMEM((DEVS, 16, 128), F32), pltpu.VMEM((HID, HID), BF16),
            pltpu.VMEM((HID, HID), BF16), pltpu.VMEM((HID, DEVS), BF16),
            pltpu.VMEM((FEAT, HID), BF16), pltpu.VMEM((HID, HID), BF16), pltpu.VMEM((HID, HID), BF16),
            pltpu.VMEM((1, ROWS, 1024), F32), pltpu.VMEM((1, ROWS, 1024), F32), pltpu.VMEM((1, HID), jnp.int32), pltpu.VMEM((4, FEAT), BF16),
            dma((4,)), dma((4,)), dma, dma, dma((5,)), dma((5,)), dma, dma((4,)),
            dma, dma, dma, dma, dma, dma, dma, dma,
            dma((3,)), dma((8,)), dma, dma((4,)),
        ],
        compiler_params=pltpu.CompilerParams(
            collective_id=0, has_side_effects=True, vmem_limit_bytes=MAIN_VMEM
        ),
        name="solve_and_reduce",
    )(
        pin(initial), pin(conductivity), step_count, pin(emit_steps), pin(assign.reshape(1, HID)), pin(sample_inputs),
        pin(w_first), pin(w_second), pin(w_third), pin(w_out),
    )
    outs = pl.pallas_call(
        final_kernel,
        out_shape=(shape((FEAT, HID), F32), shape((HID, HID), F32), shape((HID, HID), F32), shape((HID, ROWS, 128), BF16)),
        in_specs=[hbm] + [vmem] * 6 + [far] * 2,
        out_specs=[hbm] * 4,
        scratch_shapes=[
            pltpu.VMEM((HID, HID), BF16), pltpu.VMEM((HID, HID), BF16),
            pltpu.VMEM((FEAT, HID), F32), pltpu.VMEM((HID, HID), F32), pltpu.VMEM((HID, HID), F32),
            dma((2,)), dma((4,)),
        ],
        name="outputs",
        compiler_params=pltpu.CompilerParams(vmem_limit_bytes=12 * 1024 * 1024),
    )(gout, *kept, pin(w_second), pin(w_third))
    return tuple(outs)


def solution(mesh):
    placed = (
        P("group", "strip", None), P("group", "strip", None), P("group"), P("group", None), P(),
        P(("group", "strip"), None), P(), P(), P(), P(None, "strip", "group"),
    )
    return jax.shard_map(
        per_device, mesh=mesh, in_specs=placed, out_specs=(P(), P(), P(), P(None, "strip", "group")), check_vma=False
    )
```

```python
import jax
import jax.numpy as jnp
from jax import lax
from jax.experimental import pallas as pl
from jax.experimental.pallas import tpu as pltpu
from jax.sharding import PartitionSpec as P

FLAT = pl.DeviceIdType.LOGICAL
F32, BF16 = jnp.float32, jnp.bfloat16
STEPS, SNAPS, ROWS, HID, FEAT = 32, 16, 32, 512, 128
GROUPS, STRIPS = 8, 16
DEVS, CHIPS = GROUPS * STRIPS, GROUPS * STRIPS // 2
REGION = 3 * ROWS
PAIRS = ROWS // 2
CHUNK = 4
PAD = 8
MAIN_VMEM = 42 * 1024 * 1024


def dot(a, b):
    return jnp.dot(a, b, preferred_element_type=F32)


def dot_nt(a, b):
    return lax.dot_general(a, b, (((1,), (1,)), ((), ())), preferred_element_type=F32)


def swap_matrix():
    row = lax.broadcasted_iota(jnp.int32, (256, 256), 0)
    col = lax.broadcasted_iota(jnp.int32, (256, 256), 1)
    return jnp.where((row % 16) * 16 + row // 16 == col, 1.0, 0.0).astype(BF16)


def main_kernel(
    initial_hbm, conductivity_hbm, step_count, emit_steps, assign_hbm, sample_hbm,
    w_first, w_second, w_third, w_out,
    gout, act_a, act_b, hat, hbt, xt, delta_out,
    state_a, state_b, kap, quarter, hist, tmp, send, snaps, part, gath,
    raw, w2, pred, resid, acc, pair_in, pieces, mine_bf, delta, act_c, hct, hidc, onehot,
    wf, ws, wt, initial, conductivity, assign, sample_inputs,
    halo_send, halo_recv, part_send, part_recv, gath_send, gath_recv, snap_send, snap_recv,
    pair_send, pair_recv, piece_send, piece_recv, delta_send, delta_recv, twin_send, twin_recv,
    w_sem, raw_sem, own_sem, in_sem, known,
):
    g, s = lax.axis_index("group"), lax.axis_index("strip")
    me = g * STRIPS + s
    core = s % 2
    chip = g * (STRIPS // 2) + s // 2
    twin = me + 1 - 2 * core
    quad = s % 4

    def wrap(i, n):
        return jnp.where(i >= n, i - n, i)

    def each_chip(fn):
        @pl.loop(0, 7)
        def _(i):
            for j in range(9):
                p = wrap(chip + 1 + i * 9 + j, CHIPS)
                fn(p, p * 2 + core)

    def remote(src, dst, send_sem, recv_sem, device):
        return pltpu.make_async_remote_copy(
            src_ref=src, dst_ref=dst, send_sem=send_sem, recv_sem=recv_sem, device_id=device, device_id_type=FLAT
        )

    inputs = [
        pltpu.make_async_copy(a, b, in_sem.at[i])
        for i, (a, b) in enumerate((
            (initial_hbm, initial), (conductivity_hbm, conductivity), (sample_hbm, sample_inputs), (assign_hbm, assign)
        ))
    ]
    for copy in inputs:
        copy.start()
    barrier = pltpu.get_barrier_semaphore()

    z, x_lo, x_hi, y = (s // 2) % 4, s // 8, g % 2, g // 2
    doubling = [
        me + 2 * (3 - 2 * z),
        me + 8 * (1 - 2 * x_lo),
        me + 16 * (1 - 2 * x_hi) + 8 * (1 - 2 * x_lo),
        me + 32 * (1 - 2 * (y % 2)),
        me + 32 * (3 - 2 * y),
    ]

    def greet(device):
        pl.semaphore_signal(barrier, inc=1, device_id=device, device_id_type=FLAT)

    greet(twin)
    greet(me + 3 - 2 * quad)
    greet(me + 2 - 4 * (quad // 2))
    for device in doubling:
        greet(device)
    next_quad = ((quad == 0) & (s > 0)) | ((quad == 3) & (s < STRIPS - 1))

    @pl.when(next_quad)
    def _():
        greet(jnp.where(quad == 0, me - 1, me + 1))

    raw_copies = [
        pltpu.make_async_copy(w_out.at[pl.ds(64 * i, 64)], raw.at[pl.ds(64 * i, 64)], raw_sem.at[i]) for i in range(8)
    ]
    for copy in raw_copies:
        copy.start()
    weight_copies = [
        pltpu.make_async_copy(a, b, w_sem.at[i]) for i, (a, b) in enumerate(((w_first, wf), (w_second, ws), (w_third, wt)))
    ]
    for copy in weight_copies:
        copy.start()

    for copy in inputs:
        copy.wait()
    own_rows, rows_above, rows_below = pl.ds(PAD + ROWS, ROWS), pl.ds(PAD, ROWS), pl.ds(PAD + 2 * ROWS, ROWS)
    for j in range(8):
        state_a[j, own_rows, :] = initial[0, :, j * 128 : (j + 1) * 128]
        kap[j, own_rows, :] = 0.125 * conductivity[0, :, j * 128 : (j + 1) * 128]
        for ref in (state_a, state_b):
            ref[j, 0:PAD, :] = jnp.zeros((PAD, 128), F32)
            ref[j, PAD + REGION :, :] = jnp.zeros((PAD, 128), F32)
    part[quad, 0:4, :] = sample_inputs[...].astype(F32)
    ids = lax.broadcasted_iota(jnp.int32, (DEVS, HID), 0)
    onehot[...] = jnp.transpose(jnp.where(ids == assign[...], 1.0, 0.0)).astype(BF16)
    swap = swap_matrix()

    pl.semaphore_wait(barrier, 8 + jnp.where(next_quad, 1, 0))

    above, below = jnp.where(s > 0, me - 1, me), jnp.where(s < STRIPS - 1, me + 1, me)
    up_copies = [
        remote(ref.at[:, own_rows], ref.at[:, rows_below], halo_send.at[i], halo_recv.at[i], above)
        for i, ref in enumerate((state_a, kap))
    ]
    down_copies = [
        remote(ref.at[:, own_rows], ref.at[:, rows_above], halo_send.at[2 + i], halo_recv.at[2 + i], below)
        for i, ref in enumerate((state_a, kap))
    ]

    @pl.when(s > 0)
    def _():
        for copy in up_copies:
            copy.start()

    @pl.when(s < STRIPS - 1)
    def _():
        for copy in down_copies:
            copy.start()

    for i in range(1, 4):
        remote(part.at[quad], part.at[quad], part_send, part_recv, me - quad + wrap(quad + i, 4)).start()

    def relayout_weights(i, carry):
        for half in range(2):
            k0 = pl.multiple_of((i * 2 + half) * 16, 16)
            x = jnp.concatenate([raw[pl.ds(k0, 16), b * 16 : b * 16 + 16, :].reshape(256, 128) for b in range(2)], axis=1)
            y = dot(swap, x).astype(BF16)
            for b in range(2):
                for r in range(16):
                    row = b * 16 + r
                    w2[row // 2, pl.ds(k0, 16), (row % 2) * 128 : (row % 2) * 128 + 128] = y[
                        r * 16 : r * 16 + 16, b * 128 : b * 128 + 128
                    ]
        return carry

    for i, copy in enumerate(raw_copies):
        copy.wait()
    def tell(stage):
        pl.semaphore_signal(known.at[stage], inc=1, device_id=doubling[stage], device_id_type=FLAT)

    def hear(stage):
        pl.semaphore_wait(known.at[stage], 1)

    lax.fori_loop(0, 7, relayout_weights, 0)
    remote(part.at[pl.ds(0, 3)], part.at[pl.ds(0, 3)], part_send, part_recv, twin).wait()
    low = lax.broadcasted_iota(jnp.int32, (8, 128), 0) < 4
    tile = jnp.concatenate(
        [jnp.where(low, part[2 * i], pltpu.roll(part[2 * i + 1], 4, axis=0)) for i in range(2)], axis=0
    )
    mine = g * 4 + s // 4
    gath[mine] = tile.astype(BF16)
    for stage in range(3):
        tell(stage)
        lax.fori_loop(7 + 3 * stage, 10 + 3 * stage, relayout_weights, 0)
        hear(stage)
    tell(3)

    def land(has, copies_in, copies_out, rows):
        @pl.when(has)
        def _():
            for copy in copies_in:
                copy.wait_recv()
            for copy in copies_out:
                copy.wait_send()

        @pl.when(jnp.logical_not(has))
        def _():
            zero = jnp.zeros((8, ROWS, 128), F32)
            state_a[:, rows] = zero
            kap[:, rows] = zero

    land(s > 0, down_copies, up_copies, rows_above)
    land(s < STRIPS - 1, up_copies, down_copies, rows_below)

    hear(3)
    tell(4)

    @pl.loop(0, 8)
    def _(j):
        quarter[j] = 0.25 * kap[j]

    lane = lax.broadcasted_iota(jnp.int32, (8, 128), 1)
    first_lane, last_lane = lane == 0, lane == 127
    zero_tile = jnp.zeros((8, 128), F32)

    def step(src, dst, first, last, t):
        for tile in range(first, last):
            r = PAD + tile * 8
            here = [src[j, r : r + 8, :] for j in range(8)]
            to_east = [zero_tile] + [pltpu.roll(x, 1, axis=1) for x in here]
            to_west = [pltpu.roll(x, 127, axis=1) for x in here] + [zero_tile]
            for j in range(8):
                w = jnp.where(first_lane, to_east[j], to_east[j + 1])
                e = jnp.where(last_lane, to_west[j + 1], to_west[j])
                beside = (src[j, r - 1 : r + 7, :] + src[j, r + 1 : r + 9, :]) + (e + w)
                rate = kap[j, r : r + 8, :] + quarter[j, r : r + 8, :] * jnp.tanh(here[j])
                new = here[j] + rate * (beside - 4.0 * here[j])
                dst[j, r : r + 8, :] = new
                if ROWS // 8 <= tile < 2 * ROWS // 8:
                    hist[t * 32 + (j * 4 + tile - ROWS // 8)] = new

    for phase in range(4):

        @pl.loop(4 * phase, 4 * phase + 4)
        def _(i):
            step(state_a, state_b, phase, REGION // 8 - phase, 2 * i)
            step(state_b, state_a, phase, REGION // 8 - phase, 2 * i + 1)

        if phase == 0:
            hear(4)
            for i in range(1, 32):
                remote(gath.at[mine], gath.at[mine], gath_send, gath_recv, wrap(mine + i, 32) * 4 + quad).start()

    count = step_count[0]
    bases = [jnp.maximum(jnp.minimum(emit_steps[0, k], count) - 1, 0) * 32 for k in range(SNAPS)]

    def pack(c):
        @pl.loop(0, 4)
        def _(i):
            for half in range(2):
                to = i * 2 + half
                for k in range(SNAPS):
                    tmp[to, pl.ds(k, 8, stride=16), :] = hist[bases[k] + (to * 4 + c)]
                for j in range(8):
                    send[to, c * CHUNK + j // 2, :, (j % 2) * 128 : (j % 2) * 128 + 128] = tmp[
                        to, j * 16 : j * 16 + 16, :
                    ].astype(BF16)

    def snap_copy(c, to):
        rows = pl.ds(c * CHUNK, CHUNK)
        return remote(
            send.at[to, rows],
            snaps.at[rows, pl.ds(pl.multiple_of(g * SNAPS, SNAPS), SNAPS), :],
            snap_send,
            snap_recv.at[c],
            to * STRIPS + s,
        )

    for c in range(PAIRS // CHUNK):
        pack(c)
        for i in range(1, GROUPS):
            snap_copy(c, wrap(g + i, GROUPS)).start()

    own = pltpu.make_async_copy(
        send.at[g], snaps.at[:, pl.ds(pl.multiple_of(g * SNAPS, SNAPS), SNAPS), :], own_sem
    )
    own.start()

    for copy in weight_copies:
        copy.wait()
    remote(gath.at[pl.ds(0, 31)], gath.at[pl.ds(0, 31)], gath_send, gath_recv, twin).wait()

    @pl.loop(0, 4)
    def _(m):
        rows = pl.ds(pl.multiple_of(m * 128, 128), 128)
        x = gath[pl.ds(m * 8, 8)].reshape(128, FEAT)
        xt[:, rows] = jnp.transpose(x.astype(F32)).astype(BF16)
        a = jnp.tanh(dot(x, wf[...]))
        act_a[rows, :] = a
        hat[:, rows] = jnp.transpose(a).astype(BF16)
        b = jnp.tanh(dot(a.astype(BF16), ws[...]))
        act_b[rows, :] = b
        hbt[:, rows] = jnp.transpose(b).astype(BF16)
        c = jnp.tanh(dot(b.astype(BF16), wt[...]))
        hct[:, rows] = jnp.transpose(c).astype(BF16)
        hidc[rows, :] = c.astype(BF16)
        for kb in range(4):
            act_c[pl.ds(kb * 32 + m * 8, 8)] = c[:, kb * 128 : kb * 128 + 128].reshape(8, 16, 128)

    @pl.loop(0, PAIRS)
    def _(rp):
        pred[rp] = dot(hidc[...], w2[rp])

    own.wait()
    inverse_root = F32(1.0) / jnp.sqrt(F32(HID))

    def residual_chunk(c):
        remote(snaps.at[pl.ds(0, CHUNK), pl.ds(0, 112), :], snaps.at[pl.ds(0, CHUNK), pl.ds(0, 112), :],
               snap_send, snap_recv.at[c], twin).wait_recv()

        @pl.loop(0, CHUNK // 2)
        def _(i):
            for half in range(2):
                rp = c * CHUNK + 2 * i + half
                resid[rp] = ((pred[rp] - dot(onehot[...], snaps[rp])) * inverse_root).astype(BF16)

    def back_half(c, half, fresh):
        left = jnp.concatenate([resid[c * CHUNK + i] for i in range(CHUNK)], axis=1)
        k0 = pl.multiple_of(half * 256, 256)
        right = jnp.concatenate([w2[c * CHUNK + i, pl.ds(k0, 256), :] for i in range(CHUNK)], axis=1)
        value = dot_nt(left, right)
        for kb in range(2):
            at = pl.ds(half * 64 + kb * 32, 32)
            v = value[:, kb * 128 : kb * 128 + 128].reshape(32, 16, 128)
            acc[at] = v if fresh else acc[at] + v

    residual_chunk(0)
    back_half(0, 1 - core, True)

    @pl.loop(1, PAIRS // CHUNK)
    def _(c):
        residual_chunk(c)
        back_half(c, 1 - core, False)

    theirs = pl.ds((1 - core) * 64, 64)
    to_twin = remote(acc.at[theirs], pair_in, pair_send, pair_recv, twin)
    to_twin.start()
    back_half(0, core, True)

    @pl.loop(1, PAIRS // CHUNK)
    def _(c):
        back_half(c, core, False)

    to_twin.wait_recv()

    @pl.loop(0, 8)
    def _(i):
        at = pl.ds(i * 8, 8)
        mine_bf[at] = (acc[pl.ds(core * 64 + i * 8, 8)] + pair_in[at]).astype(BF16)

    each_chip(
        lambda p, device: remote(mine_bf.at[p], pieces.at[chip], piece_send, piece_recv, device).start()
    )

    pieces[chip] = mine_bf[chip]

    @pl.loop(0, PAIRS)
    def _(rp):
        w2[rp] = dot(hct[...], resid[rp]).astype(BF16)

    remote(pieces.at[pl.ds(0, 63)], pieces.at[pl.ds(0, 63)], piece_send, piece_recv, twin).wait_recv()
    total = pieces[0].astype(F32)
    for i in range(1, CHIPS):
        total = total + pieces[i].astype(F32)
    a = act_c[core * 64 + chip]
    delta[core * 64 + chip] = (total * (1.0 - a * a)).astype(BF16)

    at = core * 64 + chip
    each_chip(lambda p, device: remote(delta.at[at], delta.at[at], delta_send, delta_recv, device).start())

    def relayout_grad(i, carry):
        for half in range(2):
            k0 = pl.multiple_of((i * 2 + half) * 16, 16)
            x = jnp.concatenate(
                [
                    jnp.concatenate(
                        [w2[b * 8 + r // 2, pl.ds(k0, 16), (r % 2) * 128 : (r % 2) * 128 + 128] for r in range(16)], axis=0
                    )
                    for b in range(2)
                ],
                axis=1,
            )
            y = dot(swap, x).astype(BF16)
            for b in range(2):
                gout[pl.ds(k0, 16), b * 16 : b * 16 + 16, :] = y[:, b * 128 : b * 128 + 128].reshape(16, 16, 128)
        return carry

    lax.fori_loop(0, 16, relayout_grad, 0)

    remote(delta.at[pl.ds(0, 63)], delta.at[pl.ds(0, 63)], delta_send, delta_recv, twin).wait_recv()
    ours = pl.ds(core * 64, 64)
    to_twin2 = remote(delta.at[ours], delta.at[ours], twin_send, twin_recv, twin)
    to_twin2.start()
    to_twin2.wait_recv()
    delta_out[...] = delta[...]

    remote(send.at[pl.ds(0, 7)], send.at[pl.ds(0, 7)], snap_send, snap_recv.at[0], twin).wait_send()
    to_twin.wait_send()
    remote(pieces.at[pl.ds(0, 63)], pieces.at[pl.ds(0, 63)], piece_send, piece_recv, twin).wait_send()
    remote(delta.at[pl.ds(0, 63)], delta.at[pl.ds(0, 63)], delta_send, delta_recv, twin).wait_send()
    to_twin2.wait_send()


def final_kernel(
    gout_in, act_a, act_b, hat, hbt, xt, delta, ws_in, wt_in, g1_out, g2_out, g3_out, gout_out, ws, wt, g1, g2, g3, in_sem, out_sem
):
    loads = [pltpu.make_async_copy(a, b, in_sem.at[i]) for i, (a, b) in enumerate(((wt_in, wt), (ws_in, ws)))]
    for copy in loads:
        copy.start()
    to_gout = pltpu.make_async_copy(gout_in, gout_out, out_sem.at[3])
    to_gout.start()
    dc = jnp.concatenate([delta[i * 32 : i * 32 + 32].reshape(HID, 128) for i in range(4)], axis=1)
    g3[...] = dot(hbt[...], dc)
    to_g3 = pltpu.make_async_copy(g3, g3_out, out_sem.at[0])
    to_g3.start()
    loads[0].wait()
    db = (dot_nt(dc, wt[...]) * (1.0 - act_b[...] * act_b[...])).astype(BF16)
    g2[...] = dot(hat[...], db)
    to_g2 = pltpu.make_async_copy(g2, g2_out, out_sem.at[1])
    to_g2.start()
    loads[1].wait()
    da = (dot_nt(db, ws[...]) * (1.0 - act_a[...] * act_a[...])).astype(BF16)
    g1[...] = dot(xt[...], da)
    to_g1 = pltpu.make_async_copy(g1, g1_out, out_sem.at[2])
    to_g1.start()
    for copy in (to_gout, to_g3, to_g2, to_g1):
        copy.wait()


def per_device(initial, conductivity, step_count, emit_steps, assign, sample_inputs, w_first, w_second, w_third, w_out):
    vmem, smem = pl.BlockSpec(memory_space=pltpu.VMEM), pl.BlockSpec(memory_space=pltpu.SMEM)
    hbm = pl.BlockSpec(memory_space=pl.ANY)
    far = pl.BlockSpec(memory_space=pltpu.HBM)
    shape = jax.ShapeDtypeStruct
    dma = pltpu.SemaphoreType.DMA
    pin = lambda x: pltpu.with_memory_space_constraint(x, pltpu.HBM)
    mats = (
        shape((HID, HID), F32), shape((HID, HID), F32), shape((HID, HID), BF16), shape((HID, HID), BF16),
        shape((FEAT, HID), BF16), shape((DEVS, 16, 128), BF16),
    )
    gout, *kept = pl.pallas_call(
        main_kernel,
        out_shape=(shape((HID, ROWS, 128), BF16),) + mats,
        in_specs=[far, far, smem, smem, far, far, far, far, far, far],
        out_specs=[vmem] * 7,
        scratch_shapes=[
            *[pltpu.VMEM((8, REGION + 2 * PAD, 128), F32)] * 4,
            pltpu.VMEM((STEPS * ROWS, 8, 128), F32),
            pltpu.VMEM((GROUPS, 128, 128), F32),
            pltpu.VMEM((GROUPS, PAIRS, SNAPS, 256), BF16),
            pltpu.VMEM((PAIRS, DEVS, 256), BF16),
            pltpu.VMEM((4, 8, 128), F32),
            pltpu.VMEM((32, 16, 128), BF16),
            pltpu.VMEM((HID, ROWS, 128), BF16),
            pltpu.VMEM((PAIRS, HID, 256), BF16),
            pltpu.VMEM((PAIRS, HID, 256), F32),
            pltpu.VMEM((PAIRS, HID, 256), BF16),
            pltpu.VMEM((DEVS, 16, 128), F32),
            pltpu.VMEM((64, 16, 128), F32),
            pltpu.VMEM((CHIPS, 16, 128), BF16), pltpu.VMEM((CHIPS, 16, 128), BF16),
            pltpu.VMEM((DEVS, 16, 128), BF16),
            pltpu.VMEM((DEVS, 16, 128), F32), pltpu.VMEM((HID, HID), BF16),
            pltpu.VMEM((HID, HID), BF16), pltpu.VMEM((HID, DEVS), BF16),
            pltpu.VMEM((FEAT, HID), BF16), pltpu.VMEM((HID, HID), BF16), pltpu.VMEM((HID, HID), BF16),
            pltpu.VMEM((1, ROWS, 1024), F32), pltpu.VMEM((1, ROWS, 1024), F32), pltpu.VMEM((1, HID), jnp.int32), pltpu.VMEM((4, FEAT), BF16),
            dma((4,)), dma((4,)), dma, dma, dma, dma, dma, dma((4,)),
            dma, dma, dma, dma, dma, dma, dma, dma,
            dma((3,)), dma((8,)), dma, dma((4,)), pltpu.SemaphoreType.REGULAR((5,)),
        ],
        compiler_params=pltpu.CompilerParams(
            collective_id=0, has_side_effects=True, vmem_limit_bytes=MAIN_VMEM
        ),
        name="solve_and_reduce",
    )(
        pin(initial), pin(conductivity), step_count, pin(emit_steps), pin(assign.reshape(1, HID)), pin(sample_inputs),
        pin(w_first), pin(w_second), pin(w_third), pin(w_out),
    )
    outs = pl.pallas_call(
        final_kernel,
        out_shape=(shape((FEAT, HID), F32), shape((HID, HID), F32), shape((HID, HID), F32), shape((HID, ROWS, 128), BF16)),
        in_specs=[hbm] + [vmem] * 6 + [far] * 2,
        out_specs=[hbm] * 4,
        scratch_shapes=[
            pltpu.VMEM((HID, HID), BF16), pltpu.VMEM((HID, HID), BF16),
            pltpu.VMEM((FEAT, HID), F32), pltpu.VMEM((HID, HID), F32), pltpu.VMEM((HID, HID), F32),
            dma((2,)), dma((4,)),
        ],
        name="outputs",
        compiler_params=pltpu.CompilerParams(vmem_limit_bytes=12 * 1024 * 1024),
    )(gout, *kept, pin(w_second), pin(w_third))
    return tuple(outs)


def solution(mesh):
    placed = (
        P("group", "strip", None), P("group", "strip", None), P("group"), P("group", None), P(),
        P(("group", "strip"), None), P(), P(), P(), P(None, "strip", "group"),
    )
    return jax.shard_map(
        per_device, mesh=mesh, in_specs=placed, out_specs=(P(), P(), P(), P(None, "strip", "group")), check_vma=False
    )
```

```python
import jax
import jax.numpy as jnp
from jax import lax
from jax.experimental import pallas as pl
from jax.experimental.pallas import tpu as pltpu
from jax.sharding import PartitionSpec as P

FLAT = pl.DeviceIdType.LOGICAL
F32, BF16 = jnp.float32, jnp.bfloat16
STEPS, SNAPS, ROWS, HID, FEAT = 32, 16, 32, 512, 128
GROUPS, STRIPS = 8, 16
DEVS, CHIPS = GROUPS * STRIPS, GROUPS * STRIPS // 2
REGION = 3 * ROWS
PAIRS = ROWS // 2
CHUNK = 4
PAD = 8
MAIN_VMEM = 42 * 1024 * 1024


def dot(a, b):
    return jnp.dot(a, b, preferred_element_type=F32)


def dot_nt(a, b):
    return lax.dot_general(a, b, (((1,), (1,)), ((), ())), preferred_element_type=F32)


def swap_matrix():
    row = lax.broadcasted_iota(jnp.int32, (256, 256), 0)
    col = lax.broadcasted_iota(jnp.int32, (256, 256), 1)
    return jnp.where((row % 16) * 16 + row // 16 == col, 1.0, 0.0).astype(BF16)


def main_kernel(
    initial_hbm, conductivity_hbm, step_count, emit_steps, assign_hbm, sample_hbm,
    w_first, w_second, w_third, w_out,
    gout, act_a, act_b, hat, hbt, xt, delta_out,
    state_a, state_b, kap, quarter, hist, tmp, send, snaps, part, gath,
    raw, w2, pred, resid, acc, pair_in, pair_out, pieces, mine_bf, delta, act_c, hct, hidc, onehot,
    wf, ws, wt, initial, conductivity, assign, sample_inputs,
    halo_send, halo_recv, part_send, part_recv, gath_send, gath_recv, snap_send, snap_recv,
    pair_send, pair_recv, piece_send, piece_recv, delta_send, delta_recv, twin_send, twin_recv,
    w_sem, raw_sem, own_sem, in_sem, known,
):
    g, s = lax.axis_index("group"), lax.axis_index("strip")
    me = g * STRIPS + s
    core = s % 2
    chip = g * (STRIPS // 2) + s // 2
    twin = me + 1 - 2 * core
    quad = s % 4

    def wrap(i, n):
        return jnp.where(i >= n, i - n, i)

    def each_chip(fn):
        @pl.loop(0, 7)
        def _(i):
            for j in range(9):
                p = wrap(chip + 1 + i * 9 + j, CHIPS)
                fn(p, p * 2 + core)

    def remote(src, dst, send_sem, recv_sem, device):
        return pltpu.make_async_remote_copy(
            src_ref=src, dst_ref=dst, send_sem=send_sem, recv_sem=recv_sem, device_id=device, device_id_type=FLAT
        )

    inputs = [
        pltpu.make_async_copy(a, b, in_sem.at[i])
        for i, (a, b) in enumerate((
            (initial_hbm, initial), (conductivity_hbm, conductivity), (sample_hbm, sample_inputs), (assign_hbm, assign)
        ))
    ]
    for copy in inputs:
        copy.start()
    barrier = pltpu.get_barrier_semaphore()

    for i in range(1, STRIPS):
        pl.semaphore_signal(barrier, inc=1, device_id=g * STRIPS + wrap(s + i, STRIPS), device_id_type=FLAT)
    for i in range(1, GROUPS):
        pl.semaphore_signal(barrier, inc=1, device_id=wrap(g + i, GROUPS) * STRIPS + s, device_id_type=FLAT)

    raw_copies = [
        pltpu.make_async_copy(w_out.at[pl.ds(64 * i, 64)], raw.at[pl.ds(64 * i, 64)], raw_sem.at[i]) for i in range(8)
    ]
    for copy in raw_copies:
        copy.start()
    weight_copies = [
        pltpu.make_async_copy(a, b, w_sem.at[i]) for i, (a, b) in enumerate(((w_first, wf), (w_second, ws), (w_third, wt)))
    ]
    for copy in weight_copies:
        copy.start()

    for copy in inputs:
        copy.wait()
    own_rows, rows_above, rows_below = pl.ds(PAD + ROWS, ROWS), pl.ds(PAD, ROWS), pl.ds(PAD + 2 * ROWS, ROWS)
    for j in range(8):
        state_a[j, own_rows, :] = initial[0, :, j * 128 : (j + 1) * 128]
        kap[j, own_rows, :] = 0.125 * conductivity[0, :, j * 128 : (j + 1) * 128]
        for ref in (state_a, state_b):
            ref[j, 0:PAD, :] = jnp.zeros((PAD, 128), F32)
            ref[j, PAD + REGION :, :] = jnp.zeros((PAD, 128), F32)
    part[quad, 0:4, :] = sample_inputs[...].astype(F32)
    ids = lax.broadcasted_iota(jnp.int32, (DEVS, HID), 0)
    onehot[...] = jnp.transpose(jnp.where(ids == assign[...], 1.0, 0.0)).astype(BF16)
    swap = swap_matrix()

    pl.semaphore_wait(barrier, STRIPS + GROUPS - 2)
    for i in range(1, STRIPS):
        pl.semaphore_signal(known, inc=1, device_id=g * STRIPS + wrap(s + i, STRIPS), device_id_type=FLAT)

    for i in range(1, 4):
        remote(part.at[quad], part.at[quad], part_send, part_recv, me - quad + wrap(quad + i, 4)).start()

    above, below = jnp.where(s > 0, me - 1, me), jnp.where(s < STRIPS - 1, me + 1, me)
    up_copies = [
        remote(ref.at[:, own_rows], ref.at[:, rows_below], halo_send.at[i], halo_recv.at[i], above)
        for i, ref in enumerate((state_a, kap))
    ]
    down_copies = [
        remote(ref.at[:, own_rows], ref.at[:, rows_above], halo_send.at[2 + i], halo_recv.at[2 + i], below)
        for i, ref in enumerate((state_a, kap))
    ]

    @pl.when(s > 0)
    def _():
        for copy in up_copies:
            copy.start()

    @pl.when(s < STRIPS - 1)
    def _():
        for copy in down_copies:
            copy.start()

    def relayout_weights(i, carry):
        for half in range(2):
            k0 = pl.multiple_of((i * 2 + half) * 16, 16)
            x = jnp.concatenate([raw[pl.ds(k0, 16), b * 16 : b * 16 + 16, :].reshape(256, 128) for b in range(2)], axis=1)
            y = dot(swap, x).astype(BF16)
            for b in range(2):
                for r in range(16):
                    row = b * 16 + r
                    w2[row // 2, pl.ds(k0, 16), (row % 2) * 128 : (row % 2) * 128 + 128] = y[
                        r * 16 : r * 16 + 16, b * 128 : b * 128 + 128
                    ]
        return carry

    for i, copy in enumerate(raw_copies):
        copy.wait()
    lax.fori_loop(0, 16, relayout_weights, 0)

    remote(part.at[pl.ds(0, 3)], part.at[pl.ds(0, 3)], part_send, part_recv, twin).wait()
    low = lax.broadcasted_iota(jnp.int32, (8, 128), 0) < 4
    tile = jnp.concatenate(
        [jnp.where(low, part[2 * i], pltpu.roll(part[2 * i + 1], 4, axis=0)) for i in range(2)], axis=0
    )
    mine = g * 4 + s // 4
    gath[mine] = tile.astype(BF16)
    pl.semaphore_wait(known, STRIPS - 1)

    for i in range(1, 32):
        remote(gath.at[mine], gath.at[mine], gath_send, gath_recv, wrap(mine + i, 32) * 4 + quad).start()

    def land(has, copies_in, copies_out, rows):
        @pl.when(has)
        def _():
            for copy in copies_in:
                copy.wait_recv()
            for copy in copies_out:
                copy.wait_send()

        @pl.when(jnp.logical_not(has))
        def _():
            zero = jnp.zeros((8, ROWS, 128), F32)
            state_a[:, rows] = zero
            kap[:, rows] = zero

    land(s > 0, down_copies, up_copies, rows_above)
    land(s < STRIPS - 1, up_copies, down_copies, rows_below)

    @pl.loop(0, 8)
    def _(j):
        quarter[j] = 0.25 * kap[j]

    lane = lax.broadcasted_iota(jnp.int32, (8, 128), 1)
    first_lane, last_lane = lane == 0, lane == 127
    zero_tile = jnp.zeros((8, 128), F32)

    def step(src, dst, first, last, t):
        for tile in range(first, last):
            r = PAD + tile * 8
            here = [src[j, r : r + 8, :] for j in range(8)]
            to_east = [zero_tile] + [pltpu.roll(x, 1, axis=1) for x in here]
            to_west = [pltpu.roll(x, 127, axis=1) for x in here] + [zero_tile]
            for j in range(8):
                w = jnp.where(first_lane, to_east[j], to_east[j + 1])
                e = jnp.where(last_lane, to_west[j + 1], to_west[j])
                beside = (src[j, r - 1 : r + 7, :] + src[j, r + 1 : r + 9, :]) + (e + w)
                rate = kap[j, r : r + 8, :] + quarter[j, r : r + 8, :] * jnp.tanh(here[j])
                new = here[j] + rate * (beside - 4.0 * here[j])
                dst[j, r : r + 8, :] = new
                if ROWS // 8 <= tile < 2 * ROWS // 8:
                    hist[t * 32 + (j * 4 + tile - ROWS // 8)] = new

    for phase in range(4):

        @pl.loop(4 * phase, 4 * phase + 4)
        def _(i):
            step(state_a, state_b, phase, REGION // 8 - phase, 2 * i)
            step(state_b, state_a, phase, REGION // 8 - phase, 2 * i + 1)

    count = step_count[0]
    bases = [jnp.maximum(jnp.minimum(emit_steps[0, k], count) - 1, 0) * 32 for k in range(SNAPS)]

    def pack(c):
        @pl.loop(0, 4)
        def _(i):
            for half in range(2):
                to = i * 2 + half
                for k in range(SNAPS):
                    tmp[to, pl.ds(k, 8, stride=16), :] = hist[bases[k] + (to * 4 + c)]
                for j in range(8):
                    send[to, c * CHUNK + j // 2, :, (j % 2) * 128 : (j % 2) * 128 + 128] = tmp[
                        to, j * 16 : j * 16 + 16, :
                    ].astype(BF16)

    def snap_copy(c, to):
        rows = pl.ds(c * CHUNK, CHUNK)
        return remote(
            send.at[to, rows],
            snaps.at[rows, pl.ds(pl.multiple_of(g * SNAPS, SNAPS), SNAPS), :],
            snap_send,
            snap_recv.at[c],
            to * STRIPS + s,
        )

    for c in range(PAIRS // CHUNK):
        pack(c)
        for i in range(1, GROUPS):
            snap_copy(c, wrap(g + i, GROUPS)).start()

    own = pltpu.make_async_copy(
        send.at[g], snaps.at[:, pl.ds(pl.multiple_of(g * SNAPS, SNAPS), SNAPS), :], own_sem
    )
    own.start()

    for copy in weight_copies:
        copy.wait()
    remote(gath.at[pl.ds(0, 31)], gath.at[pl.ds(0, 31)], gath_send, gath_recv, twin).wait()

    @pl.loop(0, 4)
    def _(m):
        rows = pl.ds(pl.multiple_of(m * 128, 128), 128)
        x = gath[pl.ds(m * 8, 8)].reshape(128, FEAT)
        xt[:, rows] = jnp.transpose(x.astype(F32)).astype(BF16)
        a = jnp.tanh(dot(x, wf[...]))
        act_a[rows, :] = a
        hat[:, rows] = jnp.transpose(a).astype(BF16)
        b = jnp.tanh(dot(a.astype(BF16), ws[...]))
        act_b[rows, :] = b
        hbt[:, rows] = jnp.transpose(b).astype(BF16)
        c = jnp.tanh(dot(b.astype(BF16), wt[...]))
        hct[:, rows] = jnp.transpose(c).astype(BF16)
        hidc[rows, :] = c.astype(BF16)
        for kb in range(4):
            act_c[pl.ds(kb * 32 + m * 8, 8)] = c[:, kb * 128 : kb * 128 + 128].reshape(8, 16, 128)

    @pl.loop(0, PAIRS)
    def _(rp):
        pred[rp] = dot(hidc[...], w2[rp])

    own.wait()
    inverse_root = F32(1.0) / jnp.sqrt(F32(HID))

    def residual_chunk(c):
        remote(snaps.at[pl.ds(0, CHUNK), pl.ds(0, 112), :], snaps.at[pl.ds(0, CHUNK), pl.ds(0, 112), :],
               snap_send, snap_recv.at[c], twin).wait_recv()

        @pl.loop(0, CHUNK // 2)
        def _(i):
            for half in range(2):
                rp = c * CHUNK + 2 * i + half
                resid[rp] = ((pred[rp] - dot(onehot[...], snaps[rp])) * inverse_root).astype(BF16)

    def back_half(c, half, fresh):
        left = jnp.concatenate([resid[c * CHUNK + i] for i in range(CHUNK)], axis=1)
        k0 = pl.multiple_of(half * 256, 256)
        right = jnp.concatenate([w2[c * CHUNK + i, pl.ds(k0, 256), :] for i in range(CHUNK)], axis=1)
        value = dot_nt(left, right)
        for kb in range(2):
            at = pl.ds(half * 64 + kb * 32, 32)
            v = value[:, kb * 128 : kb * 128 + 128].reshape(32, 16, 128)
            acc[at] = v if fresh else acc[at] + v

    residual_chunk(0)
    back_half(0, 1 - core, True)

    @pl.loop(1, PAIRS // CHUNK)
    def _(c):
        residual_chunk(c)
        back_half(c, 1 - core, False)

    @pl.loop(0, 8)
    def _(i):
        pair_out[pl.ds(i * 8, 8)] = acc[pl.ds((1 - core) * 64 + i * 8, 8)].astype(BF16)

    to_twin = remote(pair_out, pair_in, pair_send, pair_recv, twin)
    to_twin.start()
    back_half(0, core, True)

    @pl.loop(1, PAIRS // CHUNK)
    def _(c):
        back_half(c, core, False)

    to_twin.wait_recv()

    @pl.loop(0, 8)
    def _(i):
        at = pl.ds(i * 8, 8)
        mine_bf[at] = (acc[pl.ds(core * 64 + i * 8, 8)] + pair_in[at].astype(F32)).astype(BF16)

    each_chip(
        lambda p, device: remote(mine_bf.at[p], pieces.at[chip], piece_send, piece_recv, device).start()
    )

    pieces[chip] = mine_bf[chip]

    @pl.loop(0, PAIRS)
    def _(rp):
        w2[rp] = dot(hct[...], resid[rp]).astype(BF16)

    remote(pieces.at[pl.ds(0, 63)], pieces.at[pl.ds(0, 63)], piece_send, piece_recv, twin).wait_recv()
    total = pieces[0].astype(F32)
    for i in range(1, CHIPS):
        total = total + pieces[i].astype(F32)
    a = act_c[core * 64 + chip]
    delta[core * 64 + chip] = (total * (1.0 - a * a)).astype(BF16)

    at = core * 64 + chip
    each_chip(lambda p, device: remote(delta.at[at], delta.at[at], delta_send, delta_recv, device).start())

    def relayout_grad(i, carry):
        for half in range(2):
            k0 = pl.multiple_of((i * 2 + half) * 16, 16)
            x = jnp.concatenate(
                [
                    jnp.concatenate(
                        [w2[b * 8 + r // 2, pl.ds(k0, 16), (r % 2) * 128 : (r % 2) * 128 + 128] for r in range(16)], axis=0
                    )
                    for b in range(2)
                ],
                axis=1,
            )
            y = dot(swap, x).astype(BF16)
            for b in range(2):
                gout[pl.ds(k0, 16), b * 16 : b * 16 + 16, :] = y[:, b * 128 : b * 128 + 128].reshape(16, 16, 128)
        return carry

    lax.fori_loop(0, 16, relayout_grad, 0)

    remote(delta.at[pl.ds(0, 63)], delta.at[pl.ds(0, 63)], delta_send, delta_recv, twin).wait_recv()
    ours = pl.ds(core * 64, 64)
    to_twin2 = remote(delta.at[ours], delta.at[ours], twin_send, twin_recv, twin)
    to_twin2.start()
    to_twin2.wait_recv()
    delta_out[...] = delta[...]

    remote(send.at[pl.ds(0, 7)], send.at[pl.ds(0, 7)], snap_send, snap_recv.at[0], twin).wait_send()
    to_twin.wait_send()
    remote(pieces.at[pl.ds(0, 63)], pieces.at[pl.ds(0, 63)], piece_send, piece_recv, twin).wait_send()
    remote(delta.at[pl.ds(0, 63)], delta.at[pl.ds(0, 63)], delta_send, delta_recv, twin).wait_send()
    to_twin2.wait_send()


def final_kernel(
    gout_in, act_a, act_b, hat, hbt, xt, delta, ws_in, wt_in, g1_out, g2_out, g3_out, gout_out, ws, wt, g1, g2, g3, in_sem, out_sem
):
    loads = [pltpu.make_async_copy(a, b, in_sem.at[i]) for i, (a, b) in enumerate(((wt_in, wt), (ws_in, ws)))]
    for copy in loads:
        copy.start()
    to_gout = pltpu.make_async_copy(gout_in, gout_out, out_sem.at[3])
    to_gout.start()
    dc = jnp.concatenate([delta[i * 32 : i * 32 + 32].reshape(HID, 128) for i in range(4)], axis=1)
    g3[...] = dot(hbt[...], dc)
    to_g3 = pltpu.make_async_copy(g3, g3_out, out_sem.at[0])
    to_g3.start()
    loads[0].wait()
    db = (dot_nt(dc, wt[...]) * (1.0 - act_b[...] * act_b[...])).astype(BF16)
    g2[...] = dot(hat[...], db)
    to_g2 = pltpu.make_async_copy(g2, g2_out, out_sem.at[1])
    to_g2.start()
    loads[1].wait()
    da = (dot_nt(db, ws[...]) * (1.0 - act_a[...] * act_a[...])).astype(BF16)
    g1[...] = dot(xt[...], da)
    to_g1 = pltpu.make_async_copy(g1, g1_out, out_sem.at[2])
    to_g1.start()
    for copy in (to_gout, to_g3, to_g2, to_g1):
        copy.wait()


def per_device(initial, conductivity, step_count, emit_steps, assign, sample_inputs, w_first, w_second, w_third, w_out):
    vmem, smem = pl.BlockSpec(memory_space=pltpu.VMEM), pl.BlockSpec(memory_space=pltpu.SMEM)
    hbm = pl.BlockSpec(memory_space=pl.ANY)
    far = pl.BlockSpec(memory_space=pltpu.HBM)
    shape = jax.ShapeDtypeStruct
    dma = pltpu.SemaphoreType.DMA
    pin = lambda x: pltpu.with_memory_space_constraint(x, pltpu.HBM)
    mats = (
        shape((HID, HID), F32), shape((HID, HID), F32), shape((HID, HID), BF16), shape((HID, HID), BF16),
        shape((FEAT, HID), BF16), shape((DEVS, 16, 128), BF16),
    )
    gout, *kept = pl.pallas_call(
        main_kernel,
        out_shape=(shape((HID, ROWS, 128), BF16),) + mats,
        in_specs=[far, far, smem, smem, far, far, far, far, far, far],
        out_specs=[vmem] * 7,
        scratch_shapes=[
            *[pltpu.VMEM((8, REGION + 2 * PAD, 128), F32)] * 4,
            pltpu.VMEM((STEPS * ROWS, 8, 128), F32),
            pltpu.VMEM((GROUPS, 128, 128), F32),
            pltpu.VMEM((GROUPS, PAIRS, SNAPS, 256), BF16),
            pltpu.VMEM((PAIRS, DEVS, 256), BF16),
            pltpu.VMEM((4, 8, 128), F32),
            pltpu.VMEM((32, 16, 128), BF16),
            pltpu.VMEM((HID, ROWS, 128), BF16),
            pltpu.VMEM((PAIRS, HID, 256), BF16),
            pltpu.VMEM((PAIRS, HID, 256), F32),
            pltpu.VMEM((PAIRS, HID, 256), BF16),
            pltpu.VMEM((DEVS, 16, 128), F32),
            pltpu.VMEM((64, 16, 128), BF16), pltpu.VMEM((64, 16, 128), BF16),
            pltpu.VMEM((CHIPS, 16, 128), BF16), pltpu.VMEM((CHIPS, 16, 128), BF16),
            pltpu.VMEM((DEVS, 16, 128), BF16),
            pltpu.VMEM((DEVS, 16, 128), F32), pltpu.VMEM((HID, HID), BF16),
            pltpu.VMEM((HID, HID), BF16), pltpu.VMEM((HID, DEVS), BF16),
            pltpu.VMEM((FEAT, HID), BF16), pltpu.VMEM((HID, HID), BF16), pltpu.VMEM((HID, HID), BF16),
            pltpu.VMEM((1, ROWS, 1024), F32), pltpu.VMEM((1, ROWS, 1024), F32), pltpu.VMEM((1, HID), jnp.int32), pltpu.VMEM((4, FEAT), BF16),
            dma((4,)), dma((4,)), dma, dma, dma, dma, dma, dma((4,)),
            dma, dma, dma, dma, dma, dma, dma, dma,
            dma((3,)), dma((8,)), dma, dma((4,)), pltpu.SemaphoreType.REGULAR,
        ],
        compiler_params=pltpu.CompilerParams(
            collective_id=0, has_side_effects=True, vmem_limit_bytes=MAIN_VMEM
        ),
        name="solve_and_reduce",
    )(
        pin(initial), pin(conductivity), step_count, pin(emit_steps), pin(assign.reshape(1, HID)), pin(sample_inputs),
        pin(w_first), pin(w_second), pin(w_third), pin(w_out),
    )
    outs = pl.pallas_call(
        final_kernel,
        out_shape=(shape((FEAT, HID), F32), shape((HID, HID), F32), shape((HID, HID), F32), shape((HID, ROWS, 128), BF16)),
        in_specs=[hbm] + [vmem] * 6 + [far] * 2,
        out_specs=[hbm] * 4,
        scratch_shapes=[
            pltpu.VMEM((HID, HID), BF16), pltpu.VMEM((HID, HID), BF16),
            pltpu.VMEM((FEAT, HID), F32), pltpu.VMEM((HID, HID), F32), pltpu.VMEM((HID, HID), F32),
            dma((2,)), dma((4,)),
        ],
        name="outputs",
        compiler_params=pltpu.CompilerParams(vmem_limit_bytes=12 * 1024 * 1024),
    )(gout, *kept, pin(w_second), pin(w_third))
    return tuple(outs)


def solution(mesh):
    placed = (
        P("group", "strip", None), P("group", "strip", None), P("group"), P("group", None), P(),
        P(("group", "strip"), None), P(), P(), P(), P(None, "strip", "group"),
    )
    return jax.shard_map(
        per_device, mesh=mesh, in_specs=placed, out_specs=(P(), P(), P(), P(None, "strip", "group")), check_vma=False
    )
```

```python
import jax
import jax.numpy as jnp
from jax import lax
from jax.experimental import pallas as pl
from jax.experimental.pallas import tpu as pltpu
from jax.sharding import PartitionSpec as P

FLAT = pl.DeviceIdType.LOGICAL
F32, BF16 = jnp.float32, jnp.bfloat16
STEPS, SNAPS, ROWS, HID, FEAT = 32, 16, 32, 512, 128
GROUPS, STRIPS = 8, 16
DEVS, CHIPS = GROUPS * STRIPS, GROUPS * STRIPS // 2
REGION = 3 * ROWS
PAIRS = ROWS // 2
CHUNK = 4
OFFSETS = sorted(
    [(i // 16, i // 4 % 4, i % 4) for i in range(1, 64)], key=lambda o: -sum(min(d, 4 - d) for d in o)
)
PAD = 8
MAIN_VMEM = 42 * 1024 * 1024


def dot(a, b):
    return jnp.dot(a, b, preferred_element_type=F32)


def dot_nt(a, b):
    return lax.dot_general(a, b, (((1,), (1,)), ((), ())), preferred_element_type=F32)


def swap_matrix():
    row = lax.broadcasted_iota(jnp.int32, (256, 256), 0)
    col = lax.broadcasted_iota(jnp.int32, (256, 256), 1)
    return jnp.where((row % 16) * 16 + row // 16 == col, 1.0, 0.0).astype(BF16)


def main_kernel(
    initial_hbm, conductivity_hbm, step_count, emit_steps, assign_hbm, sample_hbm,
    w_first, w_second, w_third, w_out,
    gout, act_a, act_b, hat, hbt, xt, delta_out,
    state_a, state_b, kap, quarter, hist, tmp, send, snaps, part, gath,
    raw, w2, pred, resid, acc, pair_in, pair_out, pieces, mine_bf, delta, act_c, hct, hidc, onehot,
    wf, ws, wt, initial, conductivity, assign, sample_inputs,
    halo_send, halo_recv, part_send, part_recv, gath_send, gath_recv, snap_send, snap_recv,
    pair_send, pair_recv, piece_send, piece_recv, delta_send, delta_recv, twin_send, twin_recv,
    w_sem, raw_sem, own_sem, in_sem, known,
):
    g, s = lax.axis_index("group"), lax.axis_index("strip")
    me = g * STRIPS + s
    core = s % 2
    chip = g * (STRIPS // 2) + s // 2
    twin = me + 1 - 2 * core
    quad = s % 4

    def wrap(i, n):
        return jnp.where(i >= n, i - n, i)

    ring = lambda v, stride: [wrap(v + d, 4) * stride for d in range(4)]
    ys, xs, zs = ring(chip // 16, 16), ring(chip // 4 % 4, 4), ring(chip % 4, 1)

    def each_chip(fn):
        for dy, dx, dz in OFFSETS:
            p = ys[dy] + xs[dx] + zs[dz]
            fn(p, p * 2 + core)

    def remote(src, dst, send_sem, recv_sem, device):
        return pltpu.make_async_remote_copy(
            src_ref=src, dst_ref=dst, send_sem=send_sem, recv_sem=recv_sem, device_id=device, device_id_type=FLAT
        )

    inputs = [
        pltpu.make_async_copy(a, b, in_sem.at[i])
        for i, (a, b) in enumerate((
            (initial_hbm, initial), (conductivity_hbm, conductivity), (sample_hbm, sample_inputs), (assign_hbm, assign)
        ))
    ]
    for copy in inputs:
        copy.start()
    barrier = pltpu.get_barrier_semaphore()

    for i in range(1, STRIPS):
        pl.semaphore_signal(barrier, inc=1, device_id=g * STRIPS + wrap(s + i, STRIPS), device_id_type=FLAT)
    for i in range(1, GROUPS):
        pl.semaphore_signal(barrier, inc=1, device_id=wrap(g + i, GROUPS) * STRIPS + s, device_id_type=FLAT)

    raw_copies = [
        pltpu.make_async_copy(w_out.at[pl.ds(64 * i, 64)], raw.at[pl.ds(64 * i, 64)], raw_sem.at[i]) for i in range(8)
    ]
    for copy in raw_copies:
        copy.start()
    weight_copies = [
        pltpu.make_async_copy(a, b, w_sem.at[i]) for i, (a, b) in enumerate(((w_first, wf), (w_second, ws), (w_third, wt)))
    ]
    for copy in weight_copies:
        copy.start()

    for copy in inputs:
        copy.wait()
    own_rows, rows_above, rows_below = pl.ds(PAD + ROWS, ROWS), pl.ds(PAD, ROWS), pl.ds(PAD + 2 * ROWS, ROWS)
    for j in range(8):
        state_a[j, own_rows, :] = initial[0, :, j * 128 : (j + 1) * 128]
        kap[j, own_rows, :] = 0.125 * conductivity[0, :, j * 128 : (j + 1) * 128]
        for ref in (state_a, state_b):
            ref[j, 0:PAD, :] = jnp.zeros((PAD, 128), F32)
            ref[j, PAD + REGION :, :] = jnp.zeros((PAD, 128), F32)
    part[quad, 0:4, :] = sample_inputs[...].astype(F32)
    ids = lax.broadcasted_iota(jnp.int32, (DEVS, HID), 0)
    onehot[...] = jnp.transpose(jnp.where(ids == assign[...], 1.0, 0.0)).astype(BF16)
    swap = swap_matrix()

    pl.semaphore_wait(barrier, STRIPS + GROUPS - 2)
    for i in range(1, STRIPS):
        pl.semaphore_signal(known, inc=1, device_id=g * STRIPS + wrap(s + i, STRIPS), device_id_type=FLAT)

    for i in range(1, 4):
        remote(part.at[quad], part.at[quad], part_send, part_recv, me - quad + wrap(quad + i, 4)).start()

    above, below = jnp.where(s > 0, me - 1, me), jnp.where(s < STRIPS - 1, me + 1, me)
    up_copies = [
        remote(ref.at[:, own_rows], ref.at[:, rows_below], halo_send.at[i], halo_recv.at[i], above)
        for i, ref in enumerate((state_a, kap))
    ]
    down_copies = [
        remote(ref.at[:, own_rows], ref.at[:, rows_above], halo_send.at[2 + i], halo_recv.at[2 + i], below)
        for i, ref in enumerate((state_a, kap))
    ]

    @pl.when(s > 0)
    def _():
        for copy in up_copies:
            copy.start()

    @pl.when(s < STRIPS - 1)
    def _():
        for copy in down_copies:
            copy.start()

    def relayout_weights(i, carry):
        for half in range(2):
            k0 = pl.multiple_of((i * 2 + half) * 16, 16)
            x = jnp.concatenate([raw[pl.ds(k0, 16), b * 16 : b * 16 + 16, :].reshape(256, 128) for b in range(2)], axis=1)
            y = dot(swap, x).astype(BF16)
            for b in range(2):
                for r in range(16):
                    row = b * 16 + r
                    w2[row // 2, pl.ds(k0, 16), (row % 2) * 128 : (row % 2) * 128 + 128] = y[
                        r * 16 : r * 16 + 16, b * 128 : b * 128 + 128
                    ]
        return carry

    for i, copy in enumerate(raw_copies):
        copy.wait()
    lax.fori_loop(0, 16, relayout_weights, 0)

    remote(part.at[pl.ds(0, 3)], part.at[pl.ds(0, 3)], part_send, part_recv, twin).wait()
    low = lax.broadcasted_iota(jnp.int32, (8, 128), 0) < 4
    tile = jnp.concatenate(
        [jnp.where(low, part[2 * i], pltpu.roll(part[2 * i + 1], 4, axis=0)) for i in range(2)], axis=0
    )
    mine = g * 4 + s // 4
    gath[mine] = tile.astype(BF16)
    pl.semaphore_wait(known, STRIPS - 1)

    for i in range(1, 32):
        remote(gath.at[mine], gath.at[mine], gath_send, gath_recv, wrap(mine + i, 32) * 4 + quad).start()

    def land(has, copies_in, copies_out, rows):
        @pl.when(has)
        def _():
            for copy in copies_in:
                copy.wait_recv()
            for copy in copies_out:
                copy.wait_send()

        @pl.when(jnp.logical_not(has))
        def _():
            zero = jnp.zeros((8, ROWS, 128), F32)
            state_a[:, rows] = zero
            kap[:, rows] = zero

    land(s > 0, down_copies, up_copies, rows_above)
    land(s < STRIPS - 1, up_copies, down_copies, rows_below)

    @pl.loop(0, 8)
    def _(j):
        quarter[j] = 0.25 * kap[j]

    lane = lax.broadcasted_iota(jnp.int32, (8, 128), 1)
    first_lane, last_lane = lane == 0, lane == 127
    zero_tile = jnp.zeros((8, 128), F32)

    def step(src, dst, first, last, t):
        for tile in range(first, last):
            r = PAD + tile * 8
            here = [src[j, r : r + 8, :] for j in range(8)]
            to_east = [zero_tile] + [pltpu.roll(x, 1, axis=1) for x in here]
            to_west = [pltpu.roll(x, 127, axis=1) for x in here] + [zero_tile]
            for j in range(8):
                w = jnp.where(first_lane, to_east[j], to_east[j + 1])
                e = jnp.where(last_lane, to_west[j + 1], to_west[j])
                beside = (src[j, r - 1 : r + 7, :] + src[j, r + 1 : r + 9, :]) + (e + w)
                rate = kap[j, r : r + 8, :] + quarter[j, r : r + 8, :] * jnp.tanh(here[j])
                new = here[j] + rate * (beside - 4.0 * here[j])
                dst[j, r : r + 8, :] = new
                if ROWS // 8 <= tile < 2 * ROWS // 8:
                    hist[t * 32 + (j * 4 + tile - ROWS // 8)] = new

    for phase in range(4):

        @pl.loop(4 * phase, 4 * phase + 4)
        def _(i):
            step(state_a, state_b, phase, REGION // 8 - phase, 2 * i)
            step(state_b, state_a, phase, REGION // 8 - phase, 2 * i + 1)

    count = step_count[0]
    bases = [jnp.maximum(jnp.minimum(emit_steps[0, k], count) - 1, 0) * 32 for k in range(SNAPS)]

    def pack(c):
        @pl.loop(0, 4)
        def _(i):
            for half in range(2):
                to = i * 2 + half
                for k in range(SNAPS):
                    tmp[to, pl.ds(k, 8, stride=16), :] = hist[bases[k] + (to * 4 + c)]
                for j in range(8):
                    send[to, c * CHUNK + j // 2, :, (j % 2) * 128 : (j % 2) * 128 + 128] = tmp[
                        to, j * 16 : j * 16 + 16, :
                    ].astype(BF16)

    def snap_copy(c, to):
        rows = pl.ds(c * CHUNK, CHUNK)
        return remote(
            send.at[to, rows],
            snaps.at[rows, pl.ds(pl.multiple_of(g * SNAPS, SNAPS), SNAPS), :],
            snap_send,
            snap_recv.at[c],
            to * STRIPS + s,
        )

    for c in range(PAIRS // CHUNK):
        pack(c)
        for i in range(1, GROUPS):
            snap_copy(c, wrap(g + i, GROUPS)).start()

    own = pltpu.make_async_copy(
        send.at[g], snaps.at[:, pl.ds(pl.multiple_of(g * SNAPS, SNAPS), SNAPS), :], own_sem
    )
    own.start()

    for copy in weight_copies:
        copy.wait()
    remote(gath.at[pl.ds(0, 31)], gath.at[pl.ds(0, 31)], gath_send, gath_recv, twin).wait()

    @pl.loop(0, 4)
    def _(m):
        rows = pl.ds(pl.multiple_of(m * 128, 128), 128)
        x = gath[pl.ds(m * 8, 8)].reshape(128, FEAT)
        xt[:, rows] = jnp.transpose(x.astype(F32)).astype(BF16)
        a = jnp.tanh(dot(x, wf[...]))
        act_a[rows, :] = a
        hat[:, rows] = jnp.transpose(a).astype(BF16)
        b = jnp.tanh(dot(a.astype(BF16), ws[...]))
        act_b[rows, :] = b
        hbt[:, rows] = jnp.transpose(b).astype(BF16)
        c = jnp.tanh(dot(b.astype(BF16), wt[...]))
        hct[:, rows] = jnp.transpose(c).astype(BF16)
        hidc[rows, :] = c.astype(BF16)
        for kb in range(4):
            act_c[pl.ds(kb * 32 + m * 8, 8)] = c[:, kb * 128 : kb * 128 + 128].reshape(8, 16, 128)

    @pl.loop(0, PAIRS)
    def _(rp):
        pred[rp] = dot(hidc[...], w2[rp])

    own.wait()
    inverse_root = F32(1.0) / jnp.sqrt(F32(HID))

    def residual_chunk(c):
        remote(snaps.at[pl.ds(0, CHUNK), pl.ds(0, 112), :], snaps.at[pl.ds(0, CHUNK), pl.ds(0, 112), :],
               snap_send, snap_recv.at[c], twin).wait_recv()

        @pl.loop(0, CHUNK // 2)
        def _(i):
            for half in range(2):
                rp = c * CHUNK + 2 * i + half
                resid[rp] = ((pred[rp] - dot(onehot[...], snaps[rp])) * inverse_root).astype(BF16)

    def back_half(c, half, fresh):
        left = jnp.concatenate([resid[c * CHUNK + i] for i in range(CHUNK)], axis=1)
        k0 = pl.multiple_of(half * 256, 256)
        right = jnp.concatenate([w2[c * CHUNK + i, pl.ds(k0, 256), :] for i in range(CHUNK)], axis=1)
        value = dot_nt(left, right)
        for kb in range(2):
            at = pl.ds(half * 64 + kb * 32, 32)
            v = value[:, kb * 128 : kb * 128 + 128].reshape(32, 16, 128)
            acc[at] = v if fresh else acc[at] + v

    residual_chunk(0)
    back_half(0, 1 - core, True)

    @pl.loop(1, PAIRS // CHUNK)
    def _(c):
        residual_chunk(c)
        back_half(c, 1 - core, False)

    @pl.loop(0, 8)
    def _(i):
        pair_out[pl.ds(i * 8, 8)] = acc[pl.ds((1 - core) * 64 + i * 8, 8)].astype(BF16)

    to_twin = remote(pair_out, pair_in, pair_send, pair_recv, twin)
    to_twin.start()
    back_half(0, core, True)

    @pl.loop(1, PAIRS // CHUNK)
    def _(c):
        back_half(c, core, False)

    to_twin.wait_recv()

    @pl.loop(0, 8)
    def _(i):
        at = pl.ds(i * 8, 8)
        mine_bf[at] = (acc[pl.ds(core * 64 + i * 8, 8)] + pair_in[at].astype(F32)).astype(BF16)

    each_chip(
        lambda p, device: remote(mine_bf.at[p], pieces.at[chip], piece_send, piece_recv, device).start()
    )

    pieces[chip] = mine_bf[chip]

    @pl.loop(0, PAIRS)
    def _(rp):
        w2[rp] = dot(hct[...], resid[rp]).astype(BF16)

    remote(pieces.at[pl.ds(0, 63)], pieces.at[pl.ds(0, 63)], piece_send, piece_recv, twin).wait_recv()
    total = pieces[0].astype(F32)
    for i in range(1, CHIPS):
        total = total + pieces[i].astype(F32)
    a = act_c[core * 64 + chip]
    delta[core * 64 + chip] = (total * (1.0 - a * a)).astype(BF16)

    at = core * 64 + chip
    each_chip(lambda p, device: remote(delta.at[at], delta.at[at], delta_send, delta_recv, device).start())

    def relayout_grad(i, carry):
        for half in range(2):
            k0 = pl.multiple_of((i * 2 + half) * 16, 16)
            x = jnp.concatenate(
                [
                    jnp.concatenate(
                        [w2[b * 8 + r // 2, pl.ds(k0, 16), (r % 2) * 128 : (r % 2) * 128 + 128] for r in range(16)], axis=0
                    )
                    for b in range(2)
                ],
                axis=1,
            )
            y = dot(swap, x).astype(BF16)
            for b in range(2):
                gout[pl.ds(k0, 16), b * 16 : b * 16 + 16, :] = y[:, b * 128 : b * 128 + 128].reshape(16, 16, 128)
        return carry

    lax.fori_loop(0, 16, relayout_grad, 0)

    remote(delta.at[pl.ds(0, 63)], delta.at[pl.ds(0, 63)], delta_send, delta_recv, twin).wait_recv()
    ours = pl.ds(core * 64, 64)
    to_twin2 = remote(delta.at[ours], delta.at[ours], twin_send, twin_recv, twin)
    to_twin2.start()
    to_twin2.wait_recv()
    delta_out[...] = delta[...]

    remote(send.at[pl.ds(0, 7)], send.at[pl.ds(0, 7)], snap_send, snap_recv.at[0], twin).wait_send()
    to_twin.wait_send()
    remote(pieces.at[pl.ds(0, 63)], pieces.at[pl.ds(0, 63)], piece_send, piece_recv, twin).wait_send()
    remote(delta.at[pl.ds(0, 63)], delta.at[pl.ds(0, 63)], delta_send, delta_recv, twin).wait_send()
    to_twin2.wait_send()


def final_kernel(
    gout_in, act_a, act_b, hat, hbt, xt, delta, ws_in, wt_in, g1_out, g2_out, g3_out, gout_out, ws, wt, g1, g2, g3, in_sem, out_sem
):
    loads = [pltpu.make_async_copy(a, b, in_sem.at[i]) for i, (a, b) in enumerate(((wt_in, wt), (ws_in, ws)))]
    for copy in loads:
        copy.start()
    to_gout = pltpu.make_async_copy(gout_in, gout_out, out_sem.at[3])
    to_gout.start()
    dc = jnp.concatenate([delta[i * 32 : i * 32 + 32].reshape(HID, 128) for i in range(4)], axis=1)
    g3[...] = dot(hbt[...], dc)
    to_g3 = pltpu.make_async_copy(g3, g3_out, out_sem.at[0])
    to_g3.start()
    loads[0].wait()
    db = (dot_nt(dc, wt[...]) * (1.0 - act_b[...] * act_b[...])).astype(BF16)
    g2[...] = dot(hat[...], db)
    to_g2 = pltpu.make_async_copy(g2, g2_out, out_sem.at[1])
    to_g2.start()
    loads[1].wait()
    da = (dot_nt(db, ws[...]) * (1.0 - act_a[...] * act_a[...])).astype(BF16)
    g1[...] = dot(xt[...], da)
    to_g1 = pltpu.make_async_copy(g1, g1_out, out_sem.at[2])
    to_g1.start()
    for copy in (to_gout, to_g3, to_g2, to_g1):
        copy.wait()


def per_device(initial, conductivity, step_count, emit_steps, assign, sample_inputs, w_first, w_second, w_third, w_out):
    vmem, smem = pl.BlockSpec(memory_space=pltpu.VMEM), pl.BlockSpec(memory_space=pltpu.SMEM)
    hbm = pl.BlockSpec(memory_space=pl.ANY)
    far = pl.BlockSpec(memory_space=pltpu.HBM)
    shape = jax.ShapeDtypeStruct
    dma = pltpu.SemaphoreType.DMA
    pin = lambda x: pltpu.with_memory_space_constraint(x, pltpu.HBM)
    mats = (
        shape((HID, HID), F32), shape((HID, HID), F32), shape((HID, HID), BF16), shape((HID, HID), BF16),
        shape((FEAT, HID), BF16), shape((DEVS, 16, 128), BF16),
    )
    gout, *kept = pl.pallas_call(
        main_kernel,
        out_shape=(shape((HID, ROWS, 128), BF16),) + mats,
        in_specs=[far, far, smem, smem, far, far, far, far, far, far],
        out_specs=[vmem] * 7,
        scratch_shapes=[
            *[pltpu.VMEM((8, REGION + 2 * PAD, 128), F32)] * 4,
            pltpu.VMEM((STEPS * ROWS, 8, 128), F32),
            pltpu.VMEM((GROUPS, 128, 128), F32),
            pltpu.VMEM((GROUPS, PAIRS, SNAPS, 256), BF16),
            pltpu.VMEM((PAIRS, DEVS, 256), BF16),
            pltpu.VMEM((4, 8, 128), F32),
            pltpu.VMEM((32, 16, 128), BF16),
            pltpu.VMEM((HID, ROWS, 128), BF16),
            pltpu.VMEM((PAIRS, HID, 256), BF16),
            pltpu.VMEM((PAIRS, HID, 256), F32),
            pltpu.VMEM((PAIRS, HID, 256), BF16),
            pltpu.VMEM((DEVS, 16, 128), F32),
            pltpu.VMEM((64, 16, 128), BF16), pltpu.VMEM((64, 16, 128), BF16),
            pltpu.VMEM((CHIPS, 16, 128), BF16), pltpu.VMEM((CHIPS, 16, 128), BF16),
            pltpu.VMEM((DEVS, 16, 128), BF16),
            pltpu.VMEM((DEVS, 16, 128), F32), pltpu.VMEM((HID, HID), BF16),
            pltpu.VMEM((HID, HID), BF16), pltpu.VMEM((HID, DEVS), BF16),
            pltpu.VMEM((FEAT, HID), BF16), pltpu.VMEM((HID, HID), BF16), pltpu.VMEM((HID, HID), BF16),
            pltpu.VMEM((1, ROWS, 1024), F32), pltpu.VMEM((1, ROWS, 1024), F32), pltpu.VMEM((1, HID), jnp.int32), pltpu.VMEM((4, FEAT), BF16),
            dma((4,)), dma((4,)), dma, dma, dma, dma, dma, dma((4,)),
            dma, dma, dma, dma, dma, dma, dma, dma,
            dma((3,)), dma((8,)), dma, dma((4,)), pltpu.SemaphoreType.REGULAR,
        ],
        compiler_params=pltpu.CompilerParams(
            collective_id=0, has_side_effects=True, vmem_limit_bytes=MAIN_VMEM
        ),
        name="solve_and_reduce",
    )(
        pin(initial), pin(conductivity), step_count, pin(emit_steps), pin(assign.reshape(1, HID)), pin(sample_inputs),
        pin(w_first), pin(w_second), pin(w_third), pin(w_out),
    )
    outs = pl.pallas_call(
        final_kernel,
        out_shape=(shape((FEAT, HID), F32), shape((HID, HID), F32), shape((HID, HID), F32), shape((HID, ROWS, 128), BF16)),
        in_specs=[hbm] + [vmem] * 6 + [far] * 2,
        out_specs=[hbm] * 4,
        scratch_shapes=[
            pltpu.VMEM((HID, HID), BF16), pltpu.VMEM((HID, HID), BF16),
            pltpu.VMEM((FEAT, HID), F32), pltpu.VMEM((HID, HID), F32), pltpu.VMEM((HID, HID), F32),
            dma((2,)), dma((4,)),
        ],
        name="outputs",
        compiler_params=pltpu.CompilerParams(vmem_limit_bytes=12 * 1024 * 1024),
    )(gout, *kept, pin(w_second), pin(w_third))
    return tuple(outs)


def solution(mesh):
    placed = (
        P("group", "strip", None), P("group", "strip", None), P("group"), P("group", None), P(),
        P(("group", "strip"), None), P(), P(), P(), P(None, "strip", "group"),
    )
    return jax.shard_map(
        per_device, mesh=mesh, in_specs=placed, out_specs=(P(), P(), P(), P(None, "strip", "group")), check_vma=False
    )
```

```python
import jax
import jax.numpy as jnp
from jax import lax
from jax.experimental import pallas as pl
from jax.experimental.pallas import tpu as pltpu
from jax.sharding import PartitionSpec as P

FLAT = pl.DeviceIdType.LOGICAL
F32, BF16 = jnp.float32, jnp.bfloat16
STEPS, SNAPS, ROWS, HID, FEAT = 32, 16, 32, 512, 128
GROUPS, STRIPS = 8, 16
DEVS, CHIPS = GROUPS * STRIPS, GROUPS * STRIPS // 2
REGION = 3 * ROWS
PAIRS = ROWS // 2
CHUNK = 4
OFFSETS = sorted(
    [(i // 16, i // 4 % 4, i % 4) for i in range(1, 64)], key=lambda o: -sum(min(d, 4 - d) for d in o)
)
GROUP_OFFSETS = sorted([(i // 2, i % 2) for i in range(1, 8)], key=lambda o: -min(o[0], 4 - o[0]) - 2 * o[1])
TILE_OFFSETS = sorted(
    [(i // 8, i // 2 % 4, i % 2) for i in range(1, 32)],
    key=lambda o: -min(o[0], 4 - o[0]) - min(o[1], 4 - o[1]) - 2 * o[2],
)
PAD = 8
MAIN_VMEM = 42 * 1024 * 1024


def dot(a, b):
    return jnp.dot(a, b, preferred_element_type=F32)


def dot_nt(a, b):
    return lax.dot_general(a, b, (((1,), (1,)), ((), ())), preferred_element_type=F32)


def swap_matrix():
    row = lax.broadcasted_iota(jnp.int32, (256, 256), 0)
    col = lax.broadcasted_iota(jnp.int32, (256, 256), 1)
    return jnp.where((row % 16) * 16 + row // 16 == col, 1.0, 0.0).astype(BF16)


def main_kernel(
    initial_hbm, conductivity_hbm, step_count, emit_steps, assign_hbm, sample_hbm,
    w_first, w_second, w_third, w_out,
    gout, act_a, act_b, hat, hbt, xt, delta_out,
    state_a, state_b, kap, quarter, hist, tmp, send, snaps, part, gath,
    raw, w2, pred, resid, acc, pair_in, pair_out, pieces, mine_bf, delta, act_c, hct, hidc, onehot,
    wf, ws, wt, initial, conductivity, assign, sample_inputs,
    halo_send, halo_recv, part_send, part_recv, gath_send, gath_recv, snap_send, snap_recv,
    pair_send, pair_recv, piece_send, piece_recv, delta_send, delta_recv, twin_send, twin_recv,
    w_sem, raw_sem, own_sem, in_sem, known,
):
    g, s = lax.axis_index("group"), lax.axis_index("strip")
    me = g * STRIPS + s
    core = s % 2
    chip = g * (STRIPS // 2) + s // 2
    twin = me + 1 - 2 * core
    quad = s % 4

    def wrap(i, n):
        return jnp.where(i >= n, i - n, i)

    ring = lambda v, stride: [wrap(v + d, 4) * stride for d in range(4)]
    ys, xs, zs = ring(chip // 16, 16), ring(chip // 4 % 4, 4), ring(chip % 4, 1)

    def each_chip(fn):
        for dy, dx, dz in OFFSETS:
            p = ys[dy] + xs[dx] + zs[dz]
            fn(p, p * 2 + core)

    def remote(src, dst, send_sem, recv_sem, device):
        return pltpu.make_async_remote_copy(
            src_ref=src, dst_ref=dst, send_sem=send_sem, recv_sem=recv_sem, device_id=device, device_id_type=FLAT
        )

    inputs = [
        pltpu.make_async_copy(a, b, in_sem.at[i])
        for i, (a, b) in enumerate((
            (initial_hbm, initial), (conductivity_hbm, conductivity), (sample_hbm, sample_inputs), (assign_hbm, assign)
        ))
    ]
    for copy in inputs:
        copy.start()
    barrier = pltpu.get_barrier_semaphore()

    for i in range(1, STRIPS):
        pl.semaphore_signal(barrier, inc=1, device_id=g * STRIPS + wrap(s + i, STRIPS), device_id_type=FLAT)
    for i in range(1, GROUPS):
        pl.semaphore_signal(barrier, inc=1, device_id=wrap(g + i, GROUPS) * STRIPS + s, device_id_type=FLAT)

    raw_copies = [
        pltpu.make_async_copy(w_out.at[pl.ds(64 * i, 64)], raw.at[pl.ds(64 * i, 64)], raw_sem.at[i]) for i in range(8)
    ]
    for copy in raw_copies:
        copy.start()
    weight_copies = [
        pltpu.make_async_copy(a, b, w_sem.at[i]) for i, (a, b) in enumerate(((w_first, wf), (w_second, ws), (w_third, wt)))
    ]
    for copy in weight_copies:
        copy.start()

    for copy in inputs:
        copy.wait()
    own_rows, rows_above, rows_below = pl.ds(PAD + ROWS, ROWS), pl.ds(PAD, ROWS), pl.ds(PAD + 2 * ROWS, ROWS)
    for j in range(8):
        state_a[j, own_rows, :] = initial[0, :, j * 128 : (j + 1) * 128]
        kap[j, own_rows, :] = 0.125 * conductivity[0, :, j * 128 : (j + 1) * 128]
        for ref in (state_a, state_b):
            ref[j, 0:PAD, :] = jnp.zeros((PAD, 128), F32)
            ref[j, PAD + REGION :, :] = jnp.zeros((PAD, 128), F32)
    part[quad, 0:4, :] = sample_inputs[...].astype(F32)
    ids = lax.broadcasted_iota(jnp.int32, (DEVS, HID), 0)
    onehot[...] = jnp.transpose(jnp.where(ids == assign[...], 1.0, 0.0)).astype(BF16)
    swap = swap_matrix()

    pl.semaphore_wait(barrier, STRIPS + GROUPS - 2)
    for i in range(1, STRIPS):
        pl.semaphore_signal(known, inc=1, device_id=g * STRIPS + wrap(s + i, STRIPS), device_id_type=FLAT)

    for i in range(1, 4):
        remote(part.at[quad], part.at[quad], part_send, part_recv, me - quad + wrap(quad + i, 4)).start()

    above, below = jnp.where(s > 0, me - 1, me), jnp.where(s < STRIPS - 1, me + 1, me)
    up_copies = [
        remote(ref.at[:, own_rows], ref.at[:, rows_below], halo_send.at[i], halo_recv.at[i], above)
        for i, ref in enumerate((state_a, kap))
    ]
    down_copies = [
        remote(ref.at[:, own_rows], ref.at[:, rows_above], halo_send.at[2 + i], halo_recv.at[2 + i], below)
        for i, ref in enumerate((state_a, kap))
    ]

    @pl.when(s > 0)
    def _():
        for copy in up_copies:
            copy.start()

    @pl.when(s < STRIPS - 1)
    def _():
        for copy in down_copies:
            copy.start()

    def relayout_weights(i, carry):
        for half in range(2):
            k0 = pl.multiple_of((i * 2 + half) * 16, 16)
            x = jnp.concatenate([raw[pl.ds(k0, 16), b * 16 : b * 16 + 16, :].reshape(256, 128) for b in range(2)], axis=1)
            y = dot(swap, x).astype(BF16)
            for b in range(2):
                for r in range(16):
                    row = b * 16 + r
                    w2[row // 2, pl.ds(k0, 16), (row % 2) * 128 : (row % 2) * 128 + 128] = y[
                        r * 16 : r * 16 + 16, b * 128 : b * 128 + 128
                    ]
        return carry

    for i, copy in enumerate(raw_copies):
        copy.wait()
    lax.fori_loop(0, 16, relayout_weights, 0)

    remote(part.at[pl.ds(0, 3)], part.at[pl.ds(0, 3)], part_send, part_recv, twin).wait()
    low = lax.broadcasted_iota(jnp.int32, (8, 128), 0) < 4
    tile = jnp.concatenate(
        [jnp.where(low, part[2 * i], pltpu.roll(part[2 * i + 1], 4, axis=0)) for i in range(2)], axis=0
    )
    mine = g * 4 + s // 4
    gath[mine] = tile.astype(BF16)
    pl.semaphore_wait(known, STRIPS - 1)

    for dy, dx, dz in TILE_OFFSETS:
        other = ys[dy] // 2 + xs[dx] // 2 + wrap(mine % 2 + dz, 2)
        remote(gath.at[mine], gath.at[mine], gath_send, gath_recv, other * 4 + quad).start()

    def land(has, copies_in, copies_out, rows):
        @pl.when(has)
        def _():
            for copy in copies_in:
                copy.wait_recv()
            for copy in copies_out:
                copy.wait_send()

        @pl.when(jnp.logical_not(has))
        def _():
            zero = jnp.zeros((8, ROWS, 128), F32)
            state_a[:, rows] = zero
            kap[:, rows] = zero

    land(s > 0, down_copies, up_copies, rows_above)
    land(s < STRIPS - 1, up_copies, down_copies, rows_below)

    @pl.loop(0, 8)
    def _(j):
        quarter[j] = 0.25 * kap[j]

    lane = lax.broadcasted_iota(jnp.int32, (8, 128), 1)
    first_lane, last_lane = lane == 0, lane == 127
    zero_tile = jnp.zeros((8, 128), F32)

    def step(src, dst, first, last, t):
        for tile in range(first, last):
            r = PAD + tile * 8
            here = [src[j, r : r + 8, :] for j in range(8)]
            to_east = [zero_tile] + [pltpu.roll(x, 1, axis=1) for x in here]
            to_west = [pltpu.roll(x, 127, axis=1) for x in here] + [zero_tile]
            for j in range(8):
                w = jnp.where(first_lane, to_east[j], to_east[j + 1])
                e = jnp.where(last_lane, to_west[j + 1], to_west[j])
                beside = (src[j, r - 1 : r + 7, :] + src[j, r + 1 : r + 9, :]) + (e + w)
                rate = kap[j, r : r + 8, :] + quarter[j, r : r + 8, :] * jnp.tanh(here[j])
                new = here[j] + rate * (beside - 4.0 * here[j])
                dst[j, r : r + 8, :] = new
                if ROWS // 8 <= tile < 2 * ROWS // 8:
                    hist[t * 32 + (j * 4 + tile - ROWS // 8)] = new

    for phase in range(4):

        @pl.loop(4 * phase, 4 * phase + 4)
        def _(i):
            step(state_a, state_b, phase, REGION // 8 - phase, 2 * i)
            step(state_b, state_a, phase, REGION // 8 - phase, 2 * i + 1)

    count = step_count[0]
    bases = [jnp.maximum(jnp.minimum(emit_steps[0, k], count) - 1, 0) * 32 for k in range(SNAPS)]

    def pack(c):
        @pl.loop(0, 4)
        def _(i):
            for half in range(2):
                to = i * 2 + half
                for k in range(SNAPS):
                    tmp[to, pl.ds(k, 8, stride=16), :] = hist[bases[k] + (to * 4 + c)]
                for j in range(8):
                    send[to, c * CHUNK + j // 2, :, (j % 2) * 128 : (j % 2) * 128 + 128] = tmp[
                        to, j * 16 : j * 16 + 16, :
                    ].astype(BF16)

    def snap_copy(c, to):
        rows = pl.ds(c * CHUNK, CHUNK)
        return remote(
            send.at[to, rows],
            snaps.at[rows, pl.ds(pl.multiple_of(g * SNAPS, SNAPS), SNAPS), :],
            snap_send,
            snap_recv.at[c],
            to * STRIPS + s,
        )

    for c in range(PAIRS // CHUNK):
        pack(c)
        for dy, dx in GROUP_OFFSETS:
            snap_copy(c, wrap(g // 2 + dy, 4) * 2 + wrap(g % 2 + dx, 2)).start()

    own = pltpu.make_async_copy(
        send.at[g], snaps.at[:, pl.ds(pl.multiple_of(g * SNAPS, SNAPS), SNAPS), :], own_sem
    )
    own.start()

    for copy in weight_copies:
        copy.wait()
    remote(gath.at[pl.ds(0, 31)], gath.at[pl.ds(0, 31)], gath_send, gath_recv, twin).wait()

    @pl.loop(0, 4)
    def _(m):
        rows = pl.ds(pl.multiple_of(m * 128, 128), 128)
        x = gath[pl.ds(m * 8, 8)].reshape(128, FEAT)
        xt[:, rows] = jnp.transpose(x.astype(F32)).astype(BF16)
        a = jnp.tanh(dot(x, wf[...]))
        act_a[rows, :] = a
        hat[:, rows] = jnp.transpose(a).astype(BF16)
        b = jnp.tanh(dot(a.astype(BF16), ws[...]))
        act_b[rows, :] = b
        hbt[:, rows] = jnp.transpose(b).astype(BF16)
        c = jnp.tanh(dot(b.astype(BF16), wt[...]))
        hct[:, rows] = jnp.transpose(c).astype(BF16)
        hidc[rows, :] = c.astype(BF16)
        for kb in range(4):
            act_c[pl.ds(kb * 32 + m * 8, 8)] = c[:, kb * 128 : kb * 128 + 128].reshape(8, 16, 128)

    @pl.loop(0, PAIRS)
    def _(rp):
        pred[rp] = dot(hidc[...], w2[rp])

    own.wait()
    inverse_root = F32(1.0) / jnp.sqrt(F32(HID))

    def residual_chunk(c):
        remote(snaps.at[pl.ds(0, CHUNK), pl.ds(0, 112), :], snaps.at[pl.ds(0, CHUNK), pl.ds(0, 112), :],
               snap_send, snap_recv.at[c], twin).wait_recv()

        @pl.loop(0, CHUNK // 2)
        def _(i):
            for half in range(2):
                rp = c * CHUNK + 2 * i + half
                resid[rp] = ((pred[rp] - dot(onehot[...], snaps[rp])) * inverse_root).astype(BF16)

    def back_half(c, half, fresh):
        left = jnp.concatenate([resid[c * CHUNK + i] for i in range(CHUNK)], axis=1)
        k0 = pl.multiple_of(half * 256, 256)
        right = jnp.concatenate([w2[c * CHUNK + i, pl.ds(k0, 256), :] for i in range(CHUNK)], axis=1)
        value = dot_nt(left, right)
        for kb in range(2):
            at = pl.ds(half * 64 + kb * 32, 32)
            v = value[:, kb * 128 : kb * 128 + 128].reshape(32, 16, 128)
            acc[at] = v if fresh else acc[at] + v

    residual_chunk(0)
    back_half(0, 1 - core, True)

    @pl.loop(1, PAIRS // CHUNK)
    def _(c):
        residual_chunk(c)
        back_half(c, 1 - core, False)

    @pl.loop(0, 8)
    def _(i):
        pair_out[pl.ds(i * 8, 8)] = acc[pl.ds((1 - core) * 64 + i * 8, 8)].astype(BF16)

    to_twin = remote(pair_out, pair_in, pair_send, pair_recv, twin)
    to_twin.start()
    back_half(0, core, True)

    @pl.loop(1, PAIRS // CHUNK)
    def _(c):
        back_half(c, core, False)

    to_twin.wait_recv()

    @pl.loop(0, 8)
    def _(i):
        at = pl.ds(i * 8, 8)
        mine_bf[at] = (acc[pl.ds(core * 64 + i * 8, 8)] + pair_in[at].astype(F32)).astype(BF16)

    each_chip(
        lambda p, device: remote(mine_bf.at[p], pieces.at[chip], piece_send, piece_recv, device).start()
    )

    pieces[chip] = mine_bf[chip]

    @pl.loop(0, PAIRS)
    def _(rp):
        w2[rp] = dot(hct[...], resid[rp]).astype(BF16)

    remote(pieces.at[pl.ds(0, 63)], pieces.at[pl.ds(0, 63)], piece_send, piece_recv, twin).wait_recv()
    total = pieces[0].astype(F32)
    for i in range(1, CHIPS):
        total = total + pieces[i].astype(F32)
    a = act_c[core * 64 + chip]
    delta[core * 64 + chip] = (total * (1.0 - a * a)).astype(BF16)

    at = core * 64 + chip
    each_chip(lambda p, device: remote(delta.at[at], delta.at[at], delta_send, delta_recv, device).start())

    def relayout_grad(i, carry):
        for half in range(2):
            k0 = pl.multiple_of((i * 2 + half) * 16, 16)
            x = jnp.concatenate(
                [
                    jnp.concatenate(
                        [w2[b * 8 + r // 2, pl.ds(k0, 16), (r % 2) * 128 : (r % 2) * 128 + 128] for r in range(16)], axis=0
                    )
                    for b in range(2)
                ],
                axis=1,
            )
            y = dot(swap, x).astype(BF16)
            for b in range(2):
                gout[pl.ds(k0, 16), b * 16 : b * 16 + 16, :] = y[:, b * 128 : b * 128 + 128].reshape(16, 16, 128)
        return carry

    lax.fori_loop(0, 16, relayout_grad, 0)

    remote(delta.at[pl.ds(0, 63)], delta.at[pl.ds(0, 63)], delta_send, delta_recv, twin).wait_recv()
    ours = pl.ds(core * 64, 64)
    to_twin2 = remote(delta.at[ours], delta.at[ours], twin_send, twin_recv, twin)
    to_twin2.start()
    to_twin2.wait_recv()
    delta_out[...] = delta[...]

    remote(send.at[pl.ds(0, 7)], send.at[pl.ds(0, 7)], snap_send, snap_recv.at[0], twin).wait_send()
    to_twin.wait_send()
    remote(pieces.at[pl.ds(0, 63)], pieces.at[pl.ds(0, 63)], piece_send, piece_recv, twin).wait_send()
    remote(delta.at[pl.ds(0, 63)], delta.at[pl.ds(0, 63)], delta_send, delta_recv, twin).wait_send()
    to_twin2.wait_send()


def final_kernel(
    gout_in, act_a, act_b, hat, hbt, xt, delta, ws_in, wt_in, g1_out, g2_out, g3_out, gout_out, ws, wt, g1, g2, g3, in_sem, out_sem
):
    loads = [pltpu.make_async_copy(a, b, in_sem.at[i]) for i, (a, b) in enumerate(((wt_in, wt), (ws_in, ws)))]
    for copy in loads:
        copy.start()
    to_gout = pltpu.make_async_copy(gout_in, gout_out, out_sem.at[3])
    to_gout.start()
    dc = jnp.concatenate([delta[i * 32 : i * 32 + 32].reshape(HID, 128) for i in range(4)], axis=1)
    g3[...] = dot(hbt[...], dc)
    to_g3 = pltpu.make_async_copy(g3, g3_out, out_sem.at[0])
    to_g3.start()
    loads[0].wait()
    db = (dot_nt(dc, wt[...]) * (1.0 - act_b[...] * act_b[...])).astype(BF16)
    g2[...] = dot(hat[...], db)
    to_g2 = pltpu.make_async_copy(g2, g2_out, out_sem.at[1])
    to_g2.start()
    loads[1].wait()
    da = (dot_nt(db, ws[...]) * (1.0 - act_a[...] * act_a[...])).astype(BF16)
    g1[...] = dot(xt[...], da)
    to_g1 = pltpu.make_async_copy(g1, g1_out, out_sem.at[2])
    to_g1.start()
    for copy in (to_gout, to_g3, to_g2, to_g1):
        copy.wait()


def per_device(initial, conductivity, step_count, emit_steps, assign, sample_inputs, w_first, w_second, w_third, w_out):
    vmem, smem = pl.BlockSpec(memory_space=pltpu.VMEM), pl.BlockSpec(memory_space=pltpu.SMEM)
    hbm = pl.BlockSpec(memory_space=pl.ANY)
    far = pl.BlockSpec(memory_space=pltpu.HBM)
    shape = jax.ShapeDtypeStruct
    dma = pltpu.SemaphoreType.DMA
    pin = lambda x: pltpu.with_memory_space_constraint(x, pltpu.HBM)
    mats = (
        shape((HID, HID), F32), shape((HID, HID), F32), shape((HID, HID), BF16), shape((HID, HID), BF16),
        shape((FEAT, HID), BF16), shape((DEVS, 16, 128), BF16),
    )
    gout, *kept = pl.pallas_call(
        main_kernel,
        out_shape=(shape((HID, ROWS, 128), BF16),) + mats,
        in_specs=[far, far, smem, smem, far, far, far, far, far, far],
        out_specs=[vmem] * 7,
        scratch_shapes=[
            *[pltpu.VMEM((8, REGION + 2 * PAD, 128), F32)] * 4,
            pltpu.VMEM((STEPS * ROWS, 8, 128), F32),
            pltpu.VMEM((GROUPS, 128, 128), F32),
            pltpu.VMEM((GROUPS, PAIRS, SNAPS, 256), BF16),
            pltpu.VMEM((PAIRS, DEVS, 256), BF16),
            pltpu.VMEM((4, 8, 128), F32),
            pltpu.VMEM((32, 16, 128), BF16),
            pltpu.VMEM((HID, ROWS, 128), BF16),
            pltpu.VMEM((PAIRS, HID, 256), BF16),
            pltpu.VMEM((PAIRS, HID, 256), F32),
            pltpu.VMEM((PAIRS, HID, 256), BF16),
            pltpu.VMEM((DEVS, 16, 128), F32),
            pltpu.VMEM((64, 16, 128), BF16), pltpu.VMEM((64, 16, 128), BF16),
            pltpu.VMEM((CHIPS, 16, 128), BF16), pltpu.VMEM((CHIPS, 16, 128), BF16),
            pltpu.VMEM((DEVS, 16, 128), BF16),
            pltpu.VMEM((DEVS, 16, 128), F32), pltpu.VMEM((HID, HID), BF16),
            pltpu.VMEM((HID, HID), BF16), pltpu.VMEM((HID, DEVS), BF16),
            pltpu.VMEM((FEAT, HID), BF16), pltpu.VMEM((HID, HID), BF16), pltpu.VMEM((HID, HID), BF16),
            pltpu.VMEM((1, ROWS, 1024), F32), pltpu.VMEM((1, ROWS, 1024), F32), pltpu.VMEM((1, HID), jnp.int32), pltpu.VMEM((4, FEAT), BF16),
            dma((4,)), dma((4,)), dma, dma, dma, dma, dma, dma((4,)),
            dma, dma, dma, dma, dma, dma, dma, dma,
            dma((3,)), dma((8,)), dma, dma((4,)), pltpu.SemaphoreType.REGULAR,
        ],
        compiler_params=pltpu.CompilerParams(
            collective_id=0, has_side_effects=True, vmem_limit_bytes=MAIN_VMEM
        ),
        name="solve_and_reduce",
    )(
        pin(initial), pin(conductivity), step_count, pin(emit_steps), pin(assign.reshape(1, HID)), pin(sample_inputs),
        pin(w_first), pin(w_second), pin(w_third), pin(w_out),
    )
    outs = pl.pallas_call(
        final_kernel,
        out_shape=(shape((FEAT, HID), F32), shape((HID, HID), F32), shape((HID, HID), F32), shape((HID, ROWS, 128), BF16)),
        in_specs=[hbm] + [vmem] * 6 + [far] * 2,
        out_specs=[hbm] * 4,
        scratch_shapes=[
            pltpu.VMEM((HID, HID), BF16), pltpu.VMEM((HID, HID), BF16),
            pltpu.VMEM((FEAT, HID), F32), pltpu.VMEM((HID, HID), F32), pltpu.VMEM((HID, HID), F32),
            dma((2,)), dma((4,)),
        ],
        name="outputs",
        compiler_params=pltpu.CompilerParams(vmem_limit_bytes=12 * 1024 * 1024),
    )(gout, *kept, pin(w_second), pin(w_third))
    return tuple(outs)


def solution(mesh):
    placed = (
        P("group", "strip", None), P("group", "strip", None), P("group"), P("group", None), P(),
        P(("group", "strip"), None), P(), P(), P(), P(None, "strip", "group"),
    )
    return jax.shard_map(
        per_device, mesh=mesh, in_specs=placed, out_specs=(P(), P(), P(), P(None, "strip", "group")), check_vma=False
    )
```

```python
import jax
import jax.numpy as jnp
from jax import lax
from jax.experimental import pallas as pl
from jax.experimental.pallas import tpu as pltpu
from jax.sharding import PartitionSpec as P

FLAT = pl.DeviceIdType.LOGICAL
F32, BF16 = jnp.float32, jnp.bfloat16
STEPS, SNAPS, ROWS, HID, FEAT = 32, 16, 32, 512, 128
GROUPS, STRIPS = 8, 16
DEVS, CHIPS = GROUPS * STRIPS, GROUPS * STRIPS // 2
REGION = 3 * ROWS
PAIRS = ROWS // 2
CHUNK = 4
OFFSETS = sorted(
    [(i // 16, i // 4 % 4, i % 4) for i in range(1, 64)], key=lambda o: -sum(min(d, 4 - d) for d in o)
)
GROUP_OFFSETS = sorted([(i // 2, i % 2) for i in range(1, 8)], key=lambda o: -min(o[0], 4 - o[0]) - 2 * o[1])
TILE_OFFSETS = sorted(
    [(i // 8, i // 2 % 4, i % 2) for i in range(1, 32)],
    key=lambda o: -min(o[0], 4 - o[0]) - min(o[1], 4 - o[1]) - 2 * o[2],
)
PAD = 8
MAIN_VMEM = 42 * 1024 * 1024


def dot(a, b):
    return jnp.dot(a, b, preferred_element_type=F32)


def dot_nt(a, b):
    return lax.dot_general(a, b, (((1,), (1,)), ((), ())), preferred_element_type=F32)


def swap_matrix():
    row = lax.broadcasted_iota(jnp.int32, (256, 256), 0)
    col = lax.broadcasted_iota(jnp.int32, (256, 256), 1)
    return jnp.where((row % 16) * 16 + row // 16 == col, 1.0, 0.0).astype(BF16)


def main_kernel(
    initial_hbm, conductivity_hbm, step_count, emit_steps, assign_hbm, sample_hbm,
    w_first, w_second, w_third, w_out,
    gout, act_a, act_b, hat, hbt, xt, delta_out,
    state_a, state_b, kap, quarter, hist, tmp, send, snaps, part, gath,
    raw, w2, pred, resid, acc, pair_in, pair_out, pieces, mine_bf, delta, act_c, hct, hidc, onehot,
    wf, ws, wt, initial, conductivity, assign, sample_inputs,
    halo_send, halo_recv, part_send, part_recv, gath_send, gath_recv, snap_send, snap_recv,
    pair_send, pair_recv, piece_send, piece_recv, delta_send, delta_recv, twin_send, twin_recv,
    w_sem, raw_sem, own_sem, in_sem, known,
):
    g, s = lax.axis_index("group"), lax.axis_index("strip")
    me = g * STRIPS + s
    core = s % 2
    chip = g * (STRIPS // 2) + s // 2
    twin = me + 1 - 2 * core
    quad = s % 4

    def wrap(i, n):
        return jnp.where(i >= n, i - n, i)

    ring = lambda v, stride: [wrap(v + d, 4) * stride for d in range(4)]
    ys, xs, zs = ring(chip // 16, 16), ring(chip // 4 % 4, 4), ring(chip % 4, 1)

    def each_chip(fn):
        for dy, dx, dz in OFFSETS:
            p = ys[dy] + xs[dx] + zs[dz]
            fn(p, p * 2 + core)

    def remote(src, dst, send_sem, recv_sem, device):
        return pltpu.make_async_remote_copy(
            src_ref=src, dst_ref=dst, send_sem=send_sem, recv_sem=recv_sem, device_id=device, device_id_type=FLAT
        )

    inputs = [
        pltpu.make_async_copy(a, b, in_sem.at[i])
        for i, (a, b) in enumerate((
            (initial_hbm, initial), (conductivity_hbm, conductivity), (sample_hbm, sample_inputs), (assign_hbm, assign)
        ))
    ]
    for copy in inputs:
        copy.start()
    barrier = pltpu.get_barrier_semaphore()

    for i in range(1, STRIPS):
        pl.semaphore_signal(barrier, inc=1, device_id=g * STRIPS + wrap(s + i, STRIPS), device_id_type=FLAT)
    for i in range(1, GROUPS):
        pl.semaphore_signal(barrier, inc=1, device_id=wrap(g + i, GROUPS) * STRIPS + s, device_id_type=FLAT)

    raw_copies = [
        pltpu.make_async_copy(w_out.at[pl.ds(64 * i, 64)], raw.at[pl.ds(64 * i, 64)], raw_sem.at[i]) for i in range(8)
    ]
    for copy in raw_copies:
        copy.start()
    weight_copies = [
        pltpu.make_async_copy(a, b, w_sem.at[i]) for i, (a, b) in enumerate(((w_first, wf), (w_second, ws), (w_third, wt)))
    ]
    for copy in weight_copies:
        copy.start()

    for copy in inputs:
        copy.wait()
    own_rows, rows_above, rows_below = pl.ds(PAD + ROWS, ROWS), pl.ds(PAD, ROWS), pl.ds(PAD + 2 * ROWS, ROWS)
    for j in range(8):
        state_a[j, own_rows, :] = initial[0, :, j * 128 : (j + 1) * 128]
        kap[j, own_rows, :] = 0.125 * conductivity[0, :, j * 128 : (j + 1) * 128]
        for ref in (state_a, state_b):
            ref[j, 0:PAD, :] = jnp.zeros((PAD, 128), F32)
            ref[j, PAD + REGION :, :] = jnp.zeros((PAD, 128), F32)
    part[quad, 0:4, :] = sample_inputs[...].astype(F32)
    ids = lax.broadcasted_iota(jnp.int32, (DEVS, HID), 0)
    onehot[...] = jnp.transpose(jnp.where(ids == assign[...], 1.0, 0.0)).astype(BF16)
    swap = swap_matrix()

    pl.semaphore_wait(barrier, STRIPS + GROUPS - 2)
    for i in range(1, STRIPS):
        pl.semaphore_signal(known, inc=1, device_id=g * STRIPS + wrap(s + i, STRIPS), device_id_type=FLAT)

    for i in range(1, 4):
        remote(part.at[quad], part.at[quad], part_send, part_recv, me - quad + wrap(quad + i, 4)).start()

    above, below = jnp.where(s > 0, me - 1, me), jnp.where(s < STRIPS - 1, me + 1, me)
    up_copies = [
        remote(ref.at[:, own_rows], ref.at[:, rows_below], halo_send.at[i], halo_recv.at[i], above)
        for i, ref in enumerate((state_a, kap))
    ]
    down_copies = [
        remote(ref.at[:, own_rows], ref.at[:, rows_above], halo_send.at[2 + i], halo_recv.at[2 + i], below)
        for i, ref in enumerate((state_a, kap))
    ]

    @pl.when(s > 0)
    def _():
        for copy in up_copies:
            copy.start()

    @pl.when(s < STRIPS - 1)
    def _():
        for copy in down_copies:
            copy.start()

    def relayout_weights(i, carry):
        for half in range(2):
            k0 = pl.multiple_of((i * 2 + half) * 16, 16)
            x = jnp.concatenate([raw[pl.ds(k0, 16), b * 16 : b * 16 + 16, :].reshape(256, 128) for b in range(2)], axis=1)
            y = dot(swap, x).astype(BF16)
            for b in range(2):
                for r in range(16):
                    row = b * 16 + r
                    w2[row // 2, pl.ds(k0, 16), (row % 2) * 128 : (row % 2) * 128 + 128] = y[
                        r * 16 : r * 16 + 16, b * 128 : b * 128 + 128
                    ]
        return carry

    for i, copy in enumerate(raw_copies):
        copy.wait()
    lax.fori_loop(0, 16, relayout_weights, 0)

    remote(part.at[pl.ds(0, 3)], part.at[pl.ds(0, 3)], part_send, part_recv, twin).wait()
    low = lax.broadcasted_iota(jnp.int32, (8, 128), 0) < 4
    tile = jnp.concatenate(
        [jnp.where(low, part[2 * i], pltpu.roll(part[2 * i + 1], 4, axis=0)) for i in range(2)], axis=0
    )
    mine = g * 4 + s // 4
    gath[mine] = tile.astype(BF16)
    pl.semaphore_wait(known, STRIPS - 1)

    for dy, dx, dz in TILE_OFFSETS:
        other = ys[dy] // 2 + xs[dx] // 2 + wrap(mine % 2 + dz, 2)
        remote(gath.at[mine], gath.at[mine], gath_send, gath_recv, other * 4 + quad).start()

    def land(has, copies_in, copies_out, rows):
        @pl.when(has)
        def _():
            for copy in copies_in:
                copy.wait_recv()
            for copy in copies_out:
                copy.wait_send()

        @pl.when(jnp.logical_not(has))
        def _():
            zero = jnp.zeros((8, ROWS, 128), F32)
            state_a[:, rows] = zero
            kap[:, rows] = zero

    land(s > 0, down_copies, up_copies, rows_above)
    land(s < STRIPS - 1, up_copies, down_copies, rows_below)

    @pl.loop(0, 8)
    def _(j):
        quarter[j] = 0.25 * kap[j]

    lane = lax.broadcasted_iota(jnp.int32, (8, 128), 1)
    first_lane, last_lane = lane == 0, lane == 127
    zero_tile = jnp.zeros((8, 128), F32)

    def step(src, dst, first, last, t):
        for tile in range(first, last):
            r = PAD + tile * 8
            here = [src[j, r : r + 8, :] for j in range(8)]
            to_east = [zero_tile] + [pltpu.roll(x, 1, axis=1) for x in here]
            to_west = [pltpu.roll(x, 127, axis=1) for x in here] + [zero_tile]
            for j in range(8):
                w = jnp.where(first_lane, to_east[j], to_east[j + 1])
                e = jnp.where(last_lane, to_west[j + 1], to_west[j])
                beside = (src[j, r - 1 : r + 7, :] + src[j, r + 1 : r + 9, :]) + (e + w)
                rate = kap[j, r : r + 8, :] + quarter[j, r : r + 8, :] * jnp.tanh(here[j])
                new = here[j] + rate * (beside - 4.0 * here[j])
                dst[j, r : r + 8, :] = new
                if ROWS // 8 <= tile < 2 * ROWS // 8:
                    hist[t * 32 + (j * 4 + tile - ROWS // 8)] = new

    for phase in range(4):

        @pl.loop(4 * phase, 4 * phase + 4)
        def _(i):
            step(state_a, state_b, phase, REGION // 8 - phase, 2 * i)
            step(state_b, state_a, phase, REGION // 8 - phase, 2 * i + 1)

    count = step_count[0]
    bases = [jnp.maximum(jnp.minimum(emit_steps[0, k], count) - 1, 0) * 32 for k in range(SNAPS)]

    def pack(c):
        @pl.loop(0, 4)
        def _(i):
            for half in range(2):
                to = i * 2 + half
                for k in range(SNAPS):
                    tmp[to, pl.ds(k, 8, stride=16), :] = hist[bases[k] + (to * 4 + c)]
                for j in range(8):
                    send[to, c * CHUNK + j // 2, :, (j % 2) * 128 : (j % 2) * 128 + 128] = tmp[
                        to, j * 16 : j * 16 + 16, :
                    ].astype(BF16)

    def snap_copy(c, to):
        rows = pl.ds(c * CHUNK, CHUNK)
        return remote(
            send.at[to, rows],
            snaps.at[rows, pl.ds(pl.multiple_of(g * SNAPS, SNAPS), SNAPS), :],
            snap_send,
            snap_recv.at[c],
            to * STRIPS + s,
        )

    for c in range(PAIRS // CHUNK):
        pack(c)
        for dy, dx in GROUP_OFFSETS:
            snap_copy(c, wrap(g // 2 + dy, 4) * 2 + wrap(g % 2 + dx, 2)).start()

    own = pltpu.make_async_copy(
        send.at[g], snaps.at[:, pl.ds(pl.multiple_of(g * SNAPS, SNAPS), SNAPS), :], own_sem
    )
    own.start()

    for copy in weight_copies:
        copy.wait()
    remote(gath.at[pl.ds(0, 31)], gath.at[pl.ds(0, 31)], gath_send, gath_recv, twin).wait()

    @pl.loop(0, 4)
    def _(m):
        rows = pl.ds(pl.multiple_of(m * 128, 128), 128)
        x = gath[pl.ds(m * 8, 8)].reshape(128, FEAT)
        xt[:, rows] = jnp.transpose(x.astype(F32)).astype(BF16)
        a = jnp.tanh(dot(x, wf[...]))
        act_a[rows, :] = a
        hat[:, rows] = jnp.transpose(a).astype(BF16)
        b = jnp.tanh(dot(a.astype(BF16), ws[...]))
        act_b[rows, :] = b
        hbt[:, rows] = jnp.transpose(b).astype(BF16)
        c = jnp.tanh(dot(b.astype(BF16), wt[...]))
        hct[:, rows] = jnp.transpose(c).astype(BF16)
        hidc[rows, :] = c.astype(BF16)
        for kb in range(4):
            act_c[pl.ds(kb * 32 + m * 8, 8)] = c[:, kb * 128 : kb * 128 + 128].reshape(8, 16, 128)

    @pl.loop(0, PAIRS // 2)
    def _(i):
        for half in range(2):
            pred[2 * i + half] = dot(hidc[...], w2[2 * i + half])

    own.wait()
    inverse_root = F32(1.0) / jnp.sqrt(F32(HID))

    def residual_chunk(c):
        remote(snaps.at[pl.ds(0, CHUNK), pl.ds(0, 112), :], snaps.at[pl.ds(0, CHUNK), pl.ds(0, 112), :],
               snap_send, snap_recv.at[c], twin).wait_recv()

        @pl.loop(0, CHUNK // 2)
        def _(i):
            for half in range(2):
                rp = c * CHUNK + 2 * i + half
                resid[rp] = ((pred[rp] - dot(onehot[...], snaps[rp])) * inverse_root).astype(BF16)

    def back_half(c, half, fresh):
        left = jnp.concatenate([resid[c * CHUNK + i] for i in range(CHUNK)], axis=1)
        k0 = pl.multiple_of(half * 256, 256)
        right = jnp.concatenate([w2[c * CHUNK + i, pl.ds(k0, 256), :] for i in range(CHUNK)], axis=1)
        value = dot_nt(left, right)
        for kb in range(2):
            at = pl.ds(half * 64 + kb * 32, 32)
            v = value[:, kb * 128 : kb * 128 + 128].reshape(32, 16, 128)
            acc[at] = v if fresh else acc[at] + v

    residual_chunk(0)
    back_half(0, 1 - core, True)

    @pl.loop(1, PAIRS // CHUNK)
    def _(c):
        residual_chunk(c)
        back_half(c, 1 - core, False)

    @pl.loop(0, 8)
    def _(i):
        pair_out[pl.ds(i * 8, 8)] = acc[pl.ds((1 - core) * 64 + i * 8, 8)].astype(BF16)

    to_twin = remote(pair_out, pair_in, pair_send, pair_recv, twin)
    to_twin.start()
    back_half(0, core, True)

    @pl.loop(1, PAIRS // CHUNK)
    def _(c):
        back_half(c, core, False)

    to_twin.wait_recv()

    @pl.loop(0, 8)
    def _(i):
        at = pl.ds(i * 8, 8)
        mine_bf[at] = (acc[pl.ds(core * 64 + i * 8, 8)] + pair_in[at].astype(F32)).astype(BF16)

    each_chip(
        lambda p, device: remote(mine_bf.at[p], pieces.at[chip], piece_send, piece_recv, device).start()
    )

    pieces[chip] = mine_bf[chip]

    @pl.loop(0, PAIRS)
    def _(rp):
        w2[rp] = dot(hct[...], resid[rp]).astype(BF16)

    remote(pieces.at[pl.ds(0, 63)], pieces.at[pl.ds(0, 63)], piece_send, piece_recv, twin).wait_recv()
    total = pieces[0].astype(F32)
    for i in range(1, CHIPS):
        total = total + pieces[i].astype(F32)
    a = act_c[core * 64 + chip]
    delta[core * 64 + chip] = (total * (1.0 - a * a)).astype(BF16)

    at = core * 64 + chip
    each_chip(lambda p, device: remote(delta.at[at], delta.at[at], delta_send, delta_recv, device).start())

    def relayout_grad(i, carry):
        for half in range(2):
            k0 = pl.multiple_of((i * 2 + half) * 16, 16)
            x = jnp.concatenate(
                [
                    jnp.concatenate(
                        [w2[b * 8 + r // 2, pl.ds(k0, 16), (r % 2) * 128 : (r % 2) * 128 + 128] for r in range(16)], axis=0
                    )
                    for b in range(2)
                ],
                axis=1,
            )
            y = dot(swap, x).astype(BF16)
            for b in range(2):
                gout[pl.ds(k0, 16), b * 16 : b * 16 + 16, :] = y[:, b * 128 : b * 128 + 128].reshape(16, 16, 128)
        return carry

    lax.fori_loop(0, 16, relayout_grad, 0)

    remote(delta.at[pl.ds(0, 63)], delta.at[pl.ds(0, 63)], delta_send, delta_recv, twin).wait_recv()
    ours = pl.ds(core * 64, 64)
    to_twin2 = remote(delta.at[ours], delta.at[ours], twin_send, twin_recv, twin)
    to_twin2.start()
    to_twin2.wait_recv()
    delta_out[...] = delta[...]

    remote(send.at[pl.ds(0, 7)], send.at[pl.ds(0, 7)], snap_send, snap_recv.at[0], twin).wait_send()
    to_twin.wait_send()
    remote(pieces.at[pl.ds(0, 63)], pieces.at[pl.ds(0, 63)], piece_send, piece_recv, twin).wait_send()
    remote(delta.at[pl.ds(0, 63)], delta.at[pl.ds(0, 63)], delta_send, delta_recv, twin).wait_send()
    to_twin2.wait_send()


def final_kernel(
    gout_in, act_a, act_b, hat, hbt, xt, delta, ws_in, wt_in, g1_out, g2_out, g3_out, gout_out, ws, wt, g1, g2, g3, in_sem, out_sem
):
    loads = [pltpu.make_async_copy(a, b, in_sem.at[i]) for i, (a, b) in enumerate(((wt_in, wt), (ws_in, ws)))]
    for copy in loads:
        copy.start()
    to_gout = pltpu.make_async_copy(gout_in, gout_out, out_sem.at[3])
    to_gout.start()
    dc = jnp.concatenate([delta[i * 32 : i * 32 + 32].reshape(HID, 128) for i in range(4)], axis=1)
    g3[...] = dot(hbt[...], dc)
    to_g3 = pltpu.make_async_copy(g3, g3_out, out_sem.at[0])
    to_g3.start()
    loads[0].wait()
    db = (dot_nt(dc, wt[...]) * (1.0 - act_b[...] * act_b[...])).astype(BF16)
    g2[...] = dot(hat[...], db)
    to_g2 = pltpu.make_async_copy(g2, g2_out, out_sem.at[1])
    to_g2.start()
    loads[1].wait()
    da = (dot_nt(db, ws[...]) * (1.0 - act_a[...] * act_a[...])).astype(BF16)
    g1[...] = dot(xt[...], da)
    to_g1 = pltpu.make_async_copy(g1, g1_out, out_sem.at[2])
    to_g1.start()
    for copy in (to_gout, to_g3, to_g2, to_g1):
        copy.wait()


def per_device(initial, conductivity, step_count, emit_steps, assign, sample_inputs, w_first, w_second, w_third, w_out):
    vmem, smem = pl.BlockSpec(memory_space=pltpu.VMEM), pl.BlockSpec(memory_space=pltpu.SMEM)
    hbm = pl.BlockSpec(memory_space=pl.ANY)
    far = pl.BlockSpec(memory_space=pltpu.HBM)
    shape = jax.ShapeDtypeStruct
    dma = pltpu.SemaphoreType.DMA
    pin = lambda x: pltpu.with_memory_space_constraint(x, pltpu.HBM)
    mats = (
        shape((HID, HID), F32), shape((HID, HID), F32), shape((HID, HID), BF16), shape((HID, HID), BF16),
        shape((FEAT, HID), BF16), shape((DEVS, 16, 128), BF16),
    )
    gout, *kept = pl.pallas_call(
        main_kernel,
        out_shape=(shape((HID, ROWS, 128), BF16),) + mats,
        in_specs=[far, far, smem, smem, far, far, far, far, far, far],
        out_specs=[vmem] * 7,
        scratch_shapes=[
            *[pltpu.VMEM((8, REGION + 2 * PAD, 128), F32)] * 4,
            pltpu.VMEM((STEPS * ROWS, 8, 128), F32),
            pltpu.VMEM((GROUPS, 128, 128), F32),
            pltpu.VMEM((GROUPS, PAIRS, SNAPS, 256), BF16),
            pltpu.VMEM((PAIRS, DEVS, 256), BF16),
            pltpu.VMEM((4, 8, 128), F32),
            pltpu.VMEM((32, 16, 128), BF16),
            pltpu.VMEM((HID, ROWS, 128), BF16),
            pltpu.VMEM((PAIRS, HID, 256), BF16),
            pltpu.VMEM((PAIRS, HID, 256), F32),
            pltpu.VMEM((PAIRS, HID, 256), BF16),
            pltpu.VMEM((DEVS, 16, 128), F32),
            pltpu.VMEM((64, 16, 128), BF16), pltpu.VMEM((64, 16, 128), BF16),
            pltpu.VMEM((CHIPS, 16, 128), BF16), pltpu.VMEM((CHIPS, 16, 128), BF16),
            pltpu.VMEM((DEVS, 16, 128), BF16),
            pltpu.VMEM((DEVS, 16, 128), F32), pltpu.VMEM((HID, HID), BF16),
            pltpu.VMEM((HID, HID), BF16), pltpu.VMEM((HID, DEVS), BF16),
            pltpu.VMEM((FEAT, HID), BF16), pltpu.VMEM((HID, HID), BF16), pltpu.VMEM((HID, HID), BF16),
            pltpu.VMEM((1, ROWS, 1024), F32), pltpu.VMEM((1, ROWS, 1024), F32), pltpu.VMEM((1, HID), jnp.int32), pltpu.VMEM((4, FEAT), BF16),
            dma((4,)), dma((4,)), dma, dma, dma, dma, dma, dma((4,)),
            dma, dma, dma, dma, dma, dma, dma, dma,
            dma((3,)), dma((8,)), dma, dma((4,)), pltpu.SemaphoreType.REGULAR,
        ],
        compiler_params=pltpu.CompilerParams(
            collective_id=0, has_side_effects=True, vmem_limit_bytes=MAIN_VMEM
        ),
        name="solve_and_reduce",
    )(
        pin(initial), pin(conductivity), step_count, pin(emit_steps), pin(assign.reshape(1, HID)), pin(sample_inputs),
        pin(w_first), pin(w_second), pin(w_third), pin(w_out),
    )
    outs = pl.pallas_call(
        final_kernel,
        out_shape=(shape((FEAT, HID), F32), shape((HID, HID), F32), shape((HID, HID), F32), shape((HID, ROWS, 128), BF16)),
        in_specs=[hbm] + [vmem] * 6 + [far] * 2,
        out_specs=[hbm] * 4,
        scratch_shapes=[
            pltpu.VMEM((HID, HID), BF16), pltpu.VMEM((HID, HID), BF16),
            pltpu.VMEM((FEAT, HID), F32), pltpu.VMEM((HID, HID), F32), pltpu.VMEM((HID, HID), F32),
            dma((2,)), dma((4,)),
        ],
        name="outputs",
        compiler_params=pltpu.CompilerParams(vmem_limit_bytes=12 * 1024 * 1024),
    )(gout, *kept, pin(w_second), pin(w_third))
    return tuple(outs)


def solution(mesh):
    placed = (
        P("group", "strip", None), P("group", "strip", None), P("group"), P("group", None), P(),
        P(("group", "strip"), None), P(), P(), P(), P(None, "strip", "group"),
    )
    return jax.shard_map(
        per_device, mesh=mesh, in_specs=placed, out_specs=(P(), P(), P(), P(None, "strip", "group")), check_vma=False
    )
```
